256 devices in a mesh: ctx: 32 (over y, x, core), head: 8 (over z).
Axes of the slice: x: 4, y: 4, z: 8, core: 2. Of those that a mesh axis runs over, the one named last changes fastest.
Arguments:
- queries: bfloat16 [4096, 1024], P('ctx', 'head'), may hold values from -6 to 6
- key_vectors: bfloat16 [4096, 1024], P('ctx', 'head'), may hold values from -6 to 6
- value_rows: bfloat16 [4096, 2048], P('ctx', 'head'), may hold values from -6 to 6
- write_rate: float32 [16, 4096], P('head', 'ctx'), may hold values from 0.001953125 to 1
- log_decay: float32 [16, 4096], P('head', 'ctx'), may hold values from -0.9 to 0
- doc_offsets: int32 [5], replicated, may hold values from 0 to 4096, as said below
- out_weight: bfloat16 [2048, 2048], P('head'), may hold values from -0.125 to 0.125
- grad_out: bfloat16 [4096, 2048], P(('ctx', 'head')), may hold values from -24 to 24
Outputs:
- layer_out: float32 [4096, 2048], P(('ctx', 'head'))
- grad_q: float32 [4096, 1024], P('ctx', 'head')
- grad_k: float32 [4096, 1024], P('ctx', 'head')
- grad_v: float32 [4096, 2048], P('ctx', 'head')
- grad_rate: float32 [16, 4096], P('head', 'ctx')
- grad_decay: float32 [16, 4096], P('head', 'ctx')
- weight_grad: float32 [2048, 2048], P('ctx', 'head')
The draws below stay inside these ranges and needn't reach their ends.
Inputs may be any that keep to these rules, and one draw needn't show every extreme that they name: `doc_offsets`: Increasing; the first entry is 0 and the last is 4096.
All inputs are finite; a program needn't handle non-finite values.
Results may differ from the reference program's by a relative error of at most 0.0029.
Values may be sent and summed in bfloat16 or wider, within the bound.
A program may use at most 64 MiB of HBM per device.

```python
import jax
import jax.numpy as jnp
from jax import lax

D = 2048
VHEADS = 16
KHEADS = 8
DK = 128
DV = 128
STRETCH = 64
DOCS = 4
TOKEN_TOTAL = 4096


def draw_write_rate(key, part):
    head_key, token_random_key = jax.random.split(key)
    lowest = DK / (4.0 * TOKEN_TOTAL)
    head_scale = jnp.exp(jax.random.uniform(head_key, (VHEADS, 1), jnp.float32, jnp.log(lowest), 0.0))
    factor = jax.random.uniform(token_random_key, (VHEADS, TOKEN_TOTAL), jnp.float32, 0.5, 1.0)
    return (head_scale * factor).astype(jnp.float32)


def draw_log_decay(key, part):
    rate_random_key, token_random_key, spurt_random_key, levels_random_key = jax.random.split(key, 4)
    slowest = 0.1 / TOKEN_TOTAL
    per_head_rate = jnp.exp(jax.random.uniform(rate_random_key, (VHEADS, 1), jnp.float32, jnp.log(slowest), jnp.log(0.06)))
    random_wobble = jax.random.uniform(token_random_key, (VHEADS, TOKEN_TOTAL), jnp.float32, 0.5, 1.5)
    spurt_groups = jax.random.uniform(spurt_random_key, (1, TOKEN_TOTAL), jnp.float32) < 6.0 / TOKEN_TOTAL
    layer_levels = jnp.log(jax.random.uniform(levels_random_key, (VHEADS, TOKEN_TOTAL), jnp.float32, 0.5, 0.8))
    return (-per_head_rate * random_wobble + jnp.where(spurt_groups, layer_levels, 0.0)).astype(jnp.float32)


def draw_doc_offsets(key, part):
    shuffled = jax.random.permutation(key, TOKEN_TOTAL - 1)[:DOCS - 1] + 1
    inner = jnp.sort(shuffled.astype(jnp.int32))
    return jnp.concatenate([jnp.zeros((1,), jnp.int32), inner, jnp.full((1,), TOKEN_TOTAL, jnp.int32)]).astype(jnp.int32)


def with_spikes(drawn, rng, source, target, parts, factor):
    owner, partner = [(jnp.arange(drawn.shape[axis_at]) // (drawn.shape[axis_at] // parts)).reshape([-1 if axis == axis_at else 1 for axis in range(drawn.ndim)]) for axis_at in (source, target)]
    chosen = jax.random.permutation(rng, parts)[partner]
    strong = (owner == chosen) | (owner == (partner + parts // 2) % parts)
    return jnp.where(strong, factor * drawn, drawn)


def levels(key, shape, cuts, least, largest):
    def one(position, shards_of):
        draws = jax.random.uniform(jax.random.fold_in(jax.random.fold_in(key, 6), position), (shards_of,), jnp.float32, least / len(cuts), largest / len(cuts))
        return jnp.repeat(jnp.exp(draws), shape[position] // shards_of).reshape((-1,) + (1,) * (len(shape) - position - 1))

    gain = one(*cuts[0])
    for cut in cuts[1:]:
        gain = gain * one(*cut)
    return gain


def noise(key, shape, deviation, most, cuts=(), kind=jnp.bfloat16):
    level = levels(key, shape, cuts, -0.22, 0.18) if cuts else 1.0
    values = jax.random.normal(key, shape, jnp.float32) * deviation * level
    return jnp.minimum(jnp.maximum(values, -most), most).astype(kind)


def gaussian_with(stream_key, shape, scale, bound, cuts, heavy, kind=jnp.bfloat16):
    entries = scale * jax.random.normal(stream_key, shape, jnp.float32)
    if cuts:
        entries = entries * levels(stream_key, shape, cuts, -0.22, 0.18)
    return jnp.clip(with_spikes(entries, jax.random.fold_in(stream_key, 3), *heavy), -bound, bound).astype(kind)


def setup_inputs(seed: int = 0) -> dict:
    streams_of = jax.random.split(jax.random.key(seed), 9)
    queries = noise(streams_of[0], (TOKEN_TOTAL, KHEADS * DK), 1.0, 6.0, ((0, 32), (1, 8)))
    key_vectors = noise(streams_of[1], (TOKEN_TOTAL, KHEADS * DK), 1.0, 6.0, ((0, 32), (1, 8)))
    value_rows = noise(streams_of[2], (TOKEN_TOTAL, VHEADS * DV), 1.0, 6.0, ((0, 32), (1, 8)))
    write_rate = draw_write_rate(jax.random.fold_in(streams_of[8], 71), 0)
    log_decay = draw_log_decay(jax.random.fold_in(streams_of[8], 71), 0)
    doc_offsets = draw_doc_offsets(jax.random.fold_in(streams_of[8], 71), 0)
    out_weight = noise(streams_of[6], (VHEADS * DV, D), (VHEADS * DV) ** -0.5, 0.125, ((0, 8),))
    grad_out = gaussian_with(streams_of[7], (TOKEN_TOTAL, D), 1.0, 24.0, ((0, 256),), (0, 1, 256, 6.0))
    return dict(queries=queries, key_vectors=key_vectors, value_rows=value_rows, write_rate=write_rate, log_decay=log_decay, doc_offsets=doc_offsets, out_weight=out_weight, grad_out=grad_out)


full_precision = lax.Precision.HIGHEST

def tri_inverse(strict_lower):
    order_size = strict_lower.shape[-1]
    identity = jnp.eye(order_size, dtype=strict_lower.dtype)
    powers = -strict_lower
    result = identity + powers
    reach_span = 2
    while reach_span < order_size:
        powers = jnp.einsum('hij,hjk->hik', powers, powers, precision=full_precision)
        result = jnp.einsum('hij,hjk->hik', result, identity + powers, precision=full_precision)
        reach_span = reach_span * 2
    return result

def block_step(state, inputs):
    query_blk, key_blk, value_blk, rate_blk, decay_blk, reset_blk = inputs
    dtype_f = decay_blk.dtype
    cumul = jnp.cumsum(decay_blk, axis=-1)
    segment = jnp.cumsum(reset_blk)
    block_len = reset_blk.shape[0]
    row_ids = lax.broadcasted_iota(jnp.int32, (block_len, block_len), 0)
    col_ids = lax.broadcasted_iota(jnp.int32, (block_len, block_len), 1)
    same_seg = segment[:, None] == segment[None, :]
    together = same_seg & (row_ids >= col_ids)
    strict = same_seg & (row_ids > col_ids)
    gaps = cumul[:, :, None] - cumul[:, None, :]
    ratio = jnp.exp(jnp.where(together, gaps, 0.0)) * together.astype(dtype_f)
    from_start = jnp.exp(cumul) * (segment == 0).astype(dtype_f)
    to_end = jnp.exp(cumul[:, -1:] - cumul) * (segment == segment[-1]).astype(dtype_f)
    whole_decay = jnp.exp(cumul[:, -1]) * (segment[-1] == 0).astype(dtype_f)
    key_dots = jnp.einsum('hik,hjk->hij', key_blk, key_blk, precision=full_precision)
    coupling = rate_blk[:, :, None] * key_dots * ratio * strict.astype(dtype_f)
    inverse = tri_inverse(coupling)
    right_side = jnp.concatenate([rate_blk[:, :, None] * value_blk, (rate_blk * from_start)[:, :, None] * key_blk], axis=-1)
    solved = jnp.einsum('hij,hjw->hiw', inverse, right_side, precision=full_precision)
    value_width = value_blk.shape[-1]
    pseudo = solved[..., :value_width] - jnp.einsum('hck,hvk->hcv', solved[..., value_width:], state, precision=full_precision)
    scores = jnp.einsum('hik,hjk->hij', query_blk, key_blk, precision=full_precision) * ratio
    outputs = from_start[:, :, None] * jnp.einsum('hck,hvk->hcv', query_blk, state, precision=full_precision)
    outputs = outputs + jnp.einsum('hij,hjv->hiv', scores, pseudo, precision=full_precision)
    new_state = whole_decay[:, None, None] * state + jnp.einsum('hcv,hck->hvk', pseudo, to_end[:, :, None] * key_blk, precision=full_precision)
    return (new_state, outputs)

def run_blocks(state, query_heads, key_heads, value_heads, rates, decays, resets, block_size):
    head_count, length = rates.shape
    blocks = length // block_size

    def split_rows(tensor):
        return jnp.moveaxis(tensor.reshape(head_count, blocks, block_size, tensor.shape[-1]), 1, 0)
    stacked = (split_rows(query_heads), split_rows(key_heads), split_rows(value_heads), jnp.moveaxis(rates.reshape(head_count, blocks, block_size), 1, 0), jnp.moveaxis(decays.reshape(head_count, blocks, block_size), 1, 0), resets.reshape(blocks, block_size))
    final_state, outputs = lax.scan(jax.checkpoint(block_step), state, stacked)
    outputs = jnp.moveaxis(outputs, 0, 1).reshape(head_count, length, outputs.shape[-1])
    return (final_state, outputs)

def to_heads(query_f, key_f, value_f):
    length = query_f.shape[0]

    def heads_first(tensor, width):
        return jnp.transpose(tensor.reshape(length, tensor.shape[1] // width, width), (1, 0, 2))

    def unit_rows(tensor):
        return tensor / jnp.sqrt(lax.optimization_barrier(jnp.sum(tensor * tensor, axis=-1, keepdims=True)) + 1e-06)
    value_heads = heads_first(value_f, DV)
    repeat_by = value_heads.shape[0] // (key_f.shape[1] // DK)
    query_heads = jnp.repeat(unit_rows(heads_first(query_f, DK)), repeat_by, axis=0)
    key_heads = jnp.repeat(unit_rows(heads_first(key_f, DK)), repeat_by, axis=0)
    return (query_heads, key_heads, value_heads)

def reference(queries, key_vectors, value_rows, write_rate, log_decay, doc_offsets, out_weight, grad_out):
    positions = jnp.arange(TOKEN_TOTAL, dtype=jnp.int32)
    resets = jnp.any(positions[:, None] == doc_offsets[None, :DOCS].astype(jnp.int32), axis=1).astype(jnp.int32)

    def core(query_f, key_f, value_f, rates, decays):
        query_heads, key_heads, value_heads = to_heads(query_f, key_f, value_f)
        head_count = value_heads.shape[0]
        start_state = jnp.zeros((head_count, DV, DK), dtype=value_f.dtype)
        final_state, outputs = run_blocks(start_state, query_heads, key_heads, value_heads, rates, decays, resets, STRETCH)
        return jnp.transpose(outputs, (1, 0, 2)).reshape(query_f.shape[0], head_count * DV)
    core_out, core_vjp = jax.vjp(core, queries.astype(jnp.float32), key_vectors.astype(jnp.float32), value_rows.astype(jnp.float32), write_rate, log_decay)
    mixed_in = core_out.astype(jnp.bfloat16)
    layer_out = jnp.dot(mixed_in, out_weight, preferred_element_type=jnp.float32)
    d_core = jnp.dot(grad_out, out_weight.T, preferred_element_type=jnp.float32)
    weight_grad = jnp.dot(grad_out.T, mixed_in, preferred_element_type=jnp.float32)
    grad_q, grad_k, grad_v, grad_rate, grad_decay = core_vjp(d_core)
    return (layer_out, grad_q, grad_k, grad_v, grad_rate, grad_decay, weight_grad)
```

```python
import functools

import jax
import jax.numpy as jnp
from jax import lax
from jax.experimental import pallas as pl
from jax.experimental.pallas import tpu as pltpu
from jax.sharding import PartitionSpec as P

f32 = jnp.float32
bf16 = jnp.bfloat16
MESH = pl.DeviceIdType.MESH


def split(x):
    hi = x.astype(bf16)
    return hi, (x - hi.astype(f32)).astype(bf16)


def mm(a, b, ca=1, cb=0):
    if not isinstance(a, tuple):
        a = (a,) if a.dtype == bf16 else split(a)
    if not isinstance(b, tuple):
        b = (b,) if b.dtype == bf16 else split(b)
    left, right = [a[0]], [b[0]]
    if len(a) == 2:
        left.append(a[1])
        right.append(b[0])
    if len(b) == 2:
        left.append(a[0])
        right.append(b[1])
    left = jnp.concatenate(left, axis=ca) if len(left) > 1 else left[0]
    right = jnp.concatenate(right, axis=cb) if len(right) > 1 else right[0]
    return lax.dot_general(left, right, (((ca,), (cb,)), ((), ())), preferred_element_type=f32)


def rows(*parts):
    parts = [p if isinstance(p, tuple) else split(p) for p in parts]
    return tuple(jnp.concatenate([p[i] for p in parts], axis=0) for i in range(2))


def cols(*parts):
    parts = [p if isinstance(p, tuple) else split(p) for p in parts]
    return tuple(jnp.concatenate([p[i] for p in parts], axis=1) for i in range(2))


def rowsum(x):
    return jnp.sum(x, axis=1, keepdims=True)


def kernel(
    n_ctx, n_head,
    docs_ref, q_ref, k_ref, v_ref, rate_ref, decay_ref, w_ref, g_ref,
    out_ref, gq_ref, gk_ref, gv_ref, grate_ref, gdecay_ref, wg_ref,
    gfull, tl_own, tl_pair, a_own, a_pair, tall, tsend, lslice, aslice, lsend, asend,
    ret_out, ret_in, sg_pair, sg_fin, lpart, lrecv, wpart, wrecv, keep,
    g_ss, g_rs, p_ss, p_rs, t_ss, t_rs, l_ss, l_rs, a_ss, a_rs, r_ss, r_rs, o_ss, o_rs, w_ss, w_rs,
):
    n_chip = n_ctx // 2
    c = lax.axis_index("ctx")
    z = lax.axis_index("head")
    chip = lax.div(c, 2)
    core = lax.rem(c, 2)
    partner = c + 1 - 2 * core
    tok = q_ref.shape[0]
    dim = 128
    n_docs = docs_ref.shape[0] - 1
    slice_rows = dim // n_chip

    barrier = pltpu.get_barrier_semaphore()

    def greet_head(i, carry):
        pl.semaphore_signal(barrier, inc=1, device_id=(c, lax.rem(z + i, n_head)), device_id_type=MESH)
        return carry

    def greet_ctx(i, carry):
        pl.semaphore_signal(barrier, inc=1, device_id=(lax.rem(c + i, n_ctx), z), device_id_type=MESH)
        return carry

    lax.fori_loop(1, n_head, greet_head, 0)
    lax.fori_loop(1, n_ctx, greet_ctx, 0)

    def grad_copy(i):
        return pltpu.make_async_remote_copy(
            src_ref=g_ref, dst_ref=gfull.at[z], send_sem=g_ss.at[i], recv_sem=g_rs.at[i],
            device_id=(c, lax.rem(z + i, n_head)), device_id_type=MESH)

    def pair_copy(i, src, dst):
        return pltpu.make_async_remote_copy(
            src_ref=src, dst_ref=dst, send_sem=p_ss.at[i], recv_sem=p_rs.at[i],
            device_id=(partner, z), device_id_type=MESH)

    def peer(i):
        return lax.rem(chip + i, n_chip)

    def t_copy(i):
        return pltpu.make_async_remote_copy(
            src_ref=tsend, dst_ref=tall.at[chip], send_sem=t_ss.at[i], recv_sem=t_rs.at[i],
            device_id=(peer(i) * 2 + core, z), device_id_type=MESH)

    def l_copy(i):
        return pltpu.make_async_remote_copy(
            src_ref=lsend.at[peer(i)], dst_ref=lslice.at[chip], send_sem=l_ss.at[i], recv_sem=l_rs.at[i],
            device_id=(peer(i) * 2 + core, z), device_id_type=MESH)

    def a_copy(i):
        return pltpu.make_async_remote_copy(
            src_ref=asend.at[peer(i)], dst_ref=aslice.at[chip], send_sem=a_ss.at[i], recv_sem=a_rs.at[i],
            device_id=(peer(i) * 2 + core, z), device_id_type=MESH)

    def r_copy(i):
        return pltpu.make_async_remote_copy(
            src_ref=ret_out.at[peer(i)], dst_ref=ret_in.at[chip], send_sem=r_ss.at[i], recv_sem=r_rs.at[i],
            device_id=(peer(i) * 2 + core, z), device_id_type=MESH)

    def o_copy(i):
        to = lax.rem(z + i, n_head)
        return pltpu.make_async_remote_copy(
            src_ref=lpart.at[to], dst_ref=lrecv.at[z], send_sem=o_ss.at[i], recv_sem=o_rs.at[i],
            device_id=(c, to), device_id_type=MESH)

    def w_copy(i):
        to = lax.rem(c + i, n_ctx)
        return pltpu.make_async_remote_copy(
            src_ref=wpart.at[to], dst_ref=wrecv.at[c], send_sem=w_ss.at[i], recv_sem=w_rs.at[i],
            device_id=(to, z), device_id_type=MESH)

    def start_all(copy, n):
        def body(i, carry):
            copy(i).start()
            return carry
        lax.fori_loop(1, n, body, 0)

    def recv_all(copy, n):
        def body(i, carry):
            copy(i).wait_recv()
            return carry
        lax.fori_loop(1, n, body, 0)

    def sent_all(copy, n):
        def body(i, carry):
            copy(i).wait_send()
            return carry
        lax.fori_loop(1, n, body, 0)

    q = q_ref[...].astype(f32)
    k = k_ref[...].astype(f32)
    q_inv = 1.0 / jnp.sqrt(rowsum(q * q) + 1e-6)
    k_inv = 1.0 / jnp.sqrt(rowsum(k * k) + 1e-6)
    qn = q * q_inv
    kn = k * k_inv
    ks, qs = split(kn), split(qn)
    dots = mm(rows(ks, qs), ks, 1, 1)
    kk, qk = dots[:tok], dots[tok:]
    ii = lax.broadcasted_iota(jnp.int32, (tok, tok), 0)
    jj = lax.broadcasted_iota(jnp.int32, (tok, tok), 1)
    first = c * tok
    seg_i = jnp.zeros((tok, tok), f32)
    seg_j = jnp.zeros((tok, tok), f32)
    seg_all = jnp.zeros((1, 1), f32)
    for d in range(n_docs):
        at = docs_ref[d] - first
        seg_i = seg_i + jnp.where((ii >= at) & (at >= 0), 1.0, 0.0)
        seg_j = seg_j + jnp.where((jj >= at) & (at >= 0), 1.0, 0.0)
    seg_all = seg_i[tok - 1:, :]
    same = jnp.where(seg_i == seg_j, 1.0, 0.0)
    low = jnp.where(ii >= jj, same, 0.0)
    strict = jnp.where(ii > jj, same, 0.0)
    eye = jnp.where(ii == jj, 1.0, 0.0)
    at_start = jnp.where(seg_i[:, :1] == 0.0, 1.0, 0.0)
    at_end = jnp.where(seg_i[:, :1] == seg_all[:, :1], 1.0, 0.0)
    no_reset = jnp.where(seg_all[:, :1] == 0.0, 1.0, 0.0)

    upto = jnp.where(ii <= jj, 1.0, 0.0)
    cum_rows = lax.dot_general(decay_ref[...], upto, (((1,), (0,)), ((), ())),
                               precision=lax.Precision.HIGHEST, preferred_element_type=f32)

    def column(row):
        return rowsum(jnp.where(ii == jj, row, 0.0))

    info = []
    for h in range(2):
        cr = cum_rows[h:h + 1]
        cc = column(cr)
        b = column(rate_ref[h:h + 1, :])
        last = cr[:, tok - 1:]
        info.append(dict(
            b=b,
            ratio=jnp.exp(jnp.where(low > 0.0, cc - cr, 0.0)) * low,
            f=jnp.exp(cc) * at_start,
            e=jnp.exp(last - cc) * at_end,
            w=jnp.exp(last) * no_reset,
        ))

    pl.semaphore_wait(barrier, n_head + n_ctx - 2)
    start_all(grad_copy, n_head)
    gfull[z] = g_ref[...]

    def same_block(width):
        shift = width.bit_length() - 1
        return lax.shift_right_logical(ii, shift) == lax.shift_right_logical(jj, shift)

    for h in range(2):
        t = info[h]
        t["kr"] = kk * t["ratio"] * strict
        t["n"] = t["b"] * t["kr"]
    for h in range(2):
        t = info[h]
        x = jnp.where(same_block(16), -t["n"], 0.0)
        xs = split(x)
        x2 = mm(xs, xs)
        x2s = split(x2)
        x4 = mm(x2s, x2s)
        x4s = split(x4)
        x8s = split(mm(x4s, x4s))
        m = eye + x
        m = m + mm(m, x2s)
        m = m + mm(m, x4s)
        m = m + mm(m, x8s)
        t["m"] = m
    for width in (16, 32, 64):
        for h in range(2):
            t = info[h]
            off = jnp.where(same_block(2 * width) & ~same_block(width), t["n"], 0.0)
            ms = split(t["m"])
            t["m"] = t["m"] - mm(ms, mm(off, ms))
    v_all = v_ref[...].astype(f32)
    for h in range(2):
        t = info[h]
        v = v_all[:, h * dim:(h + 1) * dim]
        t["v"] = v
        t["ms"] = split(t["m"])
        uw = mm(t["ms"], cols(t["b"] * v, (t["b"] * t["f"]) * kn))
        uws = split(uw)
        t["u"], t["wks"] = uw[:, :dim], (uws[0][:, dim:], uws[1][:, dim:])
        ek = t["e"] * kn
        t["eks"] = split(ek)
        lt = mm(uws, t["eks"], 0, 0)
        tl_own[h, 0] = t["w"] * eye - lt[dim:]
        tl_own[h, 1] = lt[:dim]
        t["uws"] = uws

    tl_pair[core] = tl_own[core]
    tl_copy = pair_copy(0, tl_own.at[1 - core], tl_pair.at[core])
    tl_copy.start()
    for h in range(2):
        t = info[h]
        p = qk * t["ratio"]
        t["ps"] = split(p)
        ow = mm(t["ps"], t["uws"])
        t["o"] = ow[:, :dim]
        t["qt"] = t["f"] * qn - ow[:, dim:]
        t["qts"] = split(t["qt"])
    tl_copy.wait_recv()
    t1s = split(tl_pair[1, 0])
    t0s = split(tl_pair[0, 0])
    pair_t = mm(rows(t0s, tl_pair[0, 1]), t1s)
    tsend[...] = pair_t[:dim]
    tall[chip] = pair_t[:dim]
    pair_l = (pair_t[dim:] + tl_pair[1, 1]).reshape(n_chip, slice_rows, dim)
    lsend[...] = pair_l
    start_all(t_copy, n_chip)
    start_all(l_copy, n_chip)
    lslice[chip] = lsend[chip]

    recv_all(grad_copy, n_head)
    full_grad = gfull[...].reshape(tok, g_ref.shape[1])
    weight = w_ref[...]
    d_core = lax.dot_general(full_grad, weight, (((1,), (1,)), ((), ())), preferred_element_type=f32)
    for h in range(2):
        t = info[h]
        t["do"] = d_core[:, h * dim:(h + 1) * dim]
        t["dos"] = split(t["do"])
        a_own[h] = mm(t["dos"], t["qts"], 0, 0)
    a_pair[core] = a_own[core]
    ap_copy = pair_copy(1, a_own.at[1 - core], a_pair.at[core])
    ap_copy.start()
    for h in range(2):
        t = info[h]
        t["pd"] = mm(t["ps"], t["dos"], 0, 0)
    ap_copy.wait_recv()
    asend[...] = (mm(a_pair[1], t0s, 1, 1) + a_pair[0]).reshape(n_chip, slice_rows, dim)
    start_all(a_copy, n_chip)
    aslice[chip] = asend[chip]

    recv_all(t_copy, n_chip)
    recv_all(l_copy, n_chip)
    recv_all(a_copy, n_chip)
    state = jnp.zeros((slice_rows, dim), f32)
    adjoint = jnp.zeros((slice_rows, dim), f32)
    for i in range(n_chip):
        j = n_chip - 1 - i
        ret_out[i, 0] = state
        ret_out[j, 1] = adjoint
        if i < n_chip - 1:
            state = mm(state, tall[i]) + lslice[i]
            adjoint = mm(adjoint, tall[j], 1, 1) + aslice[j]
    start_all(r_copy, n_chip)
    ret_in[chip] = ret_out[chip]
    recv_all(r_copy, n_chip)
    state = ret_in[:, 0].reshape(dim, dim)
    adjoint = ret_in[:, 1].reshape(dim, dim)
    sg_pair[0, 0] = state
    sg_pair[1, 0] = mm(state, t0s) + tl_pair[0, 1]
    sg_pair[0, 1] = mm(adjoint, t1s, 1, 1) + a_pair[1]
    sg_pair[1, 1] = adjoint
    sg_fin[core] = sg_pair[core]
    sg_copy = pair_copy(2, sg_pair.at[1 - core], sg_fin.at[core])
    sg_copy.start()
    sg_copy.wait_recv()

    mixed = []
    for h in range(2):
        t = info[h]
        t["s"] = sg_fin[h, 0]
        t["g"] = sg_fin[h, 1]
        t["ss"], t["gs"] = split(t["s"]), split(t["g"])
        both = mm(rows(t["qts"], t["wks"]), t["ss"], 1, 1)
        mixed.append((t["o"] + both[:tok]).astype(bf16))
        t["p"] = t["u"] - both[tok:]
    mixed = jnp.concatenate(mixed, axis=1)
    partial = lax.dot_general(mixed, weight, (((1,), (0,)), ((), ())), preferred_element_type=f32)
    lpart[...] = partial.astype(bf16).reshape(lpart.shape)
    start_all(o_copy, n_head)
    wpartial = lax.dot_general(full_grad, mixed, (((0,), (0,)), ((), ())), preferred_element_type=f32)
    wpart[...] = wpartial.astype(bf16).reshape(wpart.shape)
    start_all(w_copy, n_ctx)
    lrecv[z] = lpart[z]
    wrecv[c] = wpart[c]

    dqk = jnp.zeros((tok, tok), f32)
    dkk = jnp.zeros((tok, tok), f32)
    dq = jnp.zeros((tok, dim), f32)
    dk = jnp.zeros((tok, dim), f32)
    before = jnp.where(ii < jj, 1.0, 0.0).astype(bf16)
    for h in range(2):
        t = info[h]
        b, f, e = t["b"], t["f"], t["e"]
        pps = split(t["p"])
        pg = mm(pps, t["gs"])
        dp = t["pd"] + mm(t["eks"], t["gs"], 1, 1)
        dr = mm(t["ms"], dp, 0, 0)
        both = rows(t["dos"], dr)
        dpn = mm(both, pps, 1, 1)
        dos_s = mm(both, t["ss"])
        d_o_s, d_r_s = dos_s[:tok], dos_s[tok:]
        xp = dpn[:tok] * t["ratio"]
        xr = -dpn[tok:] * t["kr"]
        xn = -dpn[tok:] * (b * t["ratio"] * strict)
        dqk = dqk + xp
        dkk = dkk + xn
        x = xp * qk + b * xr
        alpha = rowsum(qn * d_o_s)
        beta = rowsum(kn * d_r_s)
        db = rowsum(dr * t["v"]) - f * beta + rowsum(xr)
        gv_ref[:, h * dim:(h + 1) * dim] = b * dr
        grate_ref[h:h + 1, :] = jnp.sum(jnp.where(ii == jj, db, 0.0), axis=0, keepdims=True)
        fdf = f * (alpha - b * beta)
        ede = e * rowsum(kn * pg)
        y = mm(x, before)
        terms = jnp.where(ii >= jj, y + fdf, ede)
        wdw = t["w"] * jnp.sum(rowsum(t["s"] * t["g"]), axis=0, keepdims=True)
        gdecay_ref[h:h + 1, :] = jnp.sum(terms, axis=0, keepdims=True) + wdw
        dq = dq + f * d_o_s
        dk = dk + e * pg - (b * f) * d_r_s
    ds = rows(dqk, dkk)
    direct = mm(ds, ks)
    turned = mm(ds, rows(qs, ks), 0, 0)
    dq = dq + direct[:tok]
    dk = dk + direct[tok:] + turned
    gq_ref[...] = q_inv * (dq - qn * rowsum(qn * dq))
    gk_ref[...] = k_inv * (dk - kn * rowsum(kn * dk))

    recv_all(o_copy, n_head)
    out_ref[...] = jnp.sum(lrecv[...].astype(f32), axis=0)
    recv_all(w_copy, n_ctx)
    wg_ref[...] = jnp.sum(wrecv[...].astype(f32), axis=0)

    tl_copy.wait_send()
    ap_copy.wait_send()
    sg_copy.wait_send()
    sent_all(grad_copy, n_head)
    sent_all(t_copy, n_chip)
    sent_all(l_copy, n_chip)
    sent_all(a_copy, n_chip)
    sent_all(r_copy, n_chip)
    sent_all(o_copy, n_head)
    sent_all(w_copy, n_ctx)


def per_device(n_ctx, n_head, queries, key_vectors, value_rows, write_rate, log_decay, doc_offsets, out_weight, grad_out):
    n_chip = n_ctx // 2
    tok, dim = queries.shape
    width = grad_out.shape[1]
    share = grad_out.shape[0]
    sl = dim // n_chip
    wrows = width // n_ctx
    vmem = pl.BlockSpec(memory_space=pltpu.VMEM)
    dma = pltpu.SemaphoreType.DMA
    scratch = [
        pltpu.VMEM((n_head, share, width), bf16),
        pltpu.VMEM((2, 2, dim, dim), f32), pltpu.VMEM((2, 2, dim, dim), f32),
        pltpu.VMEM((2, dim, dim), f32), pltpu.VMEM((2, dim, dim), f32),
        pltpu.VMEM((n_chip, dim, dim), f32), pltpu.VMEM((dim, dim), f32),
        pltpu.VMEM((n_chip, sl, dim), f32), pltpu.VMEM((n_chip, sl, dim), f32),
        pltpu.VMEM((n_chip, sl, dim), f32), pltpu.VMEM((n_chip, sl, dim), f32),
        pltpu.VMEM((n_chip, 2, sl, dim), f32), pltpu.VMEM((n_chip, 2, sl, dim), f32),
        pltpu.VMEM((2, 2, dim, dim), f32), pltpu.VMEM((2, 2, dim, dim), f32),
        pltpu.VMEM((n_head, share, width), bf16), pltpu.VMEM((n_head, share, width), bf16),
        pltpu.VMEM((n_ctx, wrows, 2 * dim), bf16), pltpu.VMEM((n_ctx, wrows, 2 * dim), bf16),
        pltpu.VMEM((8, dim), f32),
        dma((n_head,)), dma((n_head,)), dma((3,)), dma((3,)),
        dma((n_chip,)), dma((n_chip,)), dma((n_chip,)), dma((n_chip,)),
        dma((n_chip,)), dma((n_chip,)), dma((n_chip,)), dma((n_chip,)),
        dma((n_head,)), dma((n_head,)), dma((n_ctx,)), dma((n_ctx,)),
    ]
    return pl.pallas_call(
        functools.partial(kernel, n_ctx, n_head),
        out_shape=(
            jax.ShapeDtypeStruct((share, width), f32),
            jax.ShapeDtypeStruct((tok, dim), f32),
            jax.ShapeDtypeStruct((tok, dim), f32),
            jax.ShapeDtypeStruct((tok, 2 * dim), f32),
            jax.ShapeDtypeStruct((2, tok), f32),
            jax.ShapeDtypeStruct((2, tok), f32),
            jax.ShapeDtypeStruct((wrows, 2 * dim), f32),
        ),
        in_specs=[pl.BlockSpec(memory_space=pltpu.SMEM)] + [vmem] * 7,
        out_specs=(vmem,) * 7,
        scratch_shapes=scratch,
        compiler_params=pltpu.CompilerParams(collective_id=0, has_side_effects=True,
                                             vmem_limit_bytes=48 * 1024 * 1024),
        name="layer",
    )(doc_offsets, queries, key_vectors, value_rows, write_rate, log_decay, out_weight, grad_out)


def solution(mesh):
    n_ctx, n_head = mesh.shape["ctx"], mesh.shape["head"]
    return jax.shard_map(
        functools.partial(per_device, n_ctx, n_head),
        mesh=mesh,
        in_specs=(
            P("ctx", "head"), P("ctx", "head"), P("ctx", "head"), P("head", "ctx"), P("head", "ctx"),
            P(), P("head", None), P(("ctx", "head"), None),
        ),
        out_specs=(
            P(("ctx", "head"), None), P("ctx", "head"), P("ctx", "head"), P("ctx", "head"),
            P("head", "ctx"), P("head", "ctx"), P("ctx", "head"),
        ),
        check_vma=False,
    )
```

```python
import functools

import jax
import jax.numpy as jnp
from jax import lax
from jax.experimental import pallas as pl
from jax.experimental.pallas import tpu as pltpu
from jax.sharding import PartitionSpec as P

f32 = jnp.float32
bf16 = jnp.bfloat16
MESH = pl.DeviceIdType.MESH


def split(x):
    hi = x.astype(bf16)
    return hi, (x - hi.astype(f32)).astype(bf16)


def mm(a, b, ca=1, cb=0):
    if not isinstance(a, tuple):
        a = (a,) if a.dtype == bf16 else split(a)
    if not isinstance(b, tuple):
        b = (b,) if b.dtype == bf16 else split(b)
    left, right = [a[0]], [b[0]]
    if len(a) == 2:
        left.append(a[1])
        right.append(b[0])
    if len(b) == 2:
        left.append(a[0])
        right.append(b[1])
    left = jnp.concatenate(left, axis=ca) if len(left) > 1 else left[0]
    right = jnp.concatenate(right, axis=cb) if len(right) > 1 else right[0]
    return lax.dot_general(left, right, (((ca,), (cb,)), ((), ())), preferred_element_type=f32)


def rows(*parts):
    parts = [p if isinstance(p, tuple) else split(p) for p in parts]
    return tuple(jnp.concatenate([p[i] for p in parts], axis=0) for i in range(2))


def cols(*parts):
    parts = [p if isinstance(p, tuple) else split(p) for p in parts]
    return tuple(jnp.concatenate([p[i] for p in parts], axis=1) for i in range(2))


def rowsum(x):
    return jnp.sum(x, axis=1, keepdims=True)


def kernel(
    n_ctx, n_head,
    docs_hbm, q_hbm, k_hbm, v_hbm, rate_hbm, decay_hbm, w_hbm, g_hbm,
    out_ref, gq_ref, gk_ref, gv_ref, grate_ref, gdecay_ref, wg_ref,
    docs_ref, q_ref, k_ref, v_ref, rate_ref, decay_ref, w_ref,
    gfull, tl_own, tl_pair, a_own, a_pair, tall, tsend, lslice, aslice, lsend, asend,
    ret_out, ret_in, sg_pair, sg_fin, lpart, lrecv, wpart, wrecv,
    i_s, g_ss, g_rs, p_ss, p_rs, t_ss, t_rs, l_ss, l_rs, a_ss, a_rs, r_ss, r_rs, o_ss, o_rs, w_ss, w_rs,
):
    n_chip = n_ctx // 2
    side = 4 if n_chip == 16 else 1
    c = lax.axis_index("ctx")
    z = lax.axis_index("head")
    chip = lax.div(c, 2)
    core = lax.rem(c, 2)
    partner = c + 1 - 2 * core
    row = lax.div(chip, side)
    col = lax.rem(chip, side)
    tok = q_ref.shape[0]
    dim = 128
    width = w_ref.shape[1]
    n_docs = docs_ref.shape[0] - 1
    slice_rows = dim // n_chip

    loads = [
        pltpu.make_async_copy(src, dst, i_s.at[i])
        for i, (src, dst) in enumerate((
            (g_hbm, gfull.at[z]), (q_hbm, q_ref), (k_hbm, k_ref), (docs_hbm, docs_ref),
            (rate_hbm, rate_ref), (decay_hbm, decay_ref), (v_hbm, v_ref), (w_hbm, w_ref),
        ))
    ]
    for load in loads:
        load.start()

    barrier = pltpu.get_barrier_semaphore()

    def greet_head(i, carry):
        pl.semaphore_signal(barrier, inc=1, device_id=(c, lax.rem(z + i, n_head)), device_id_type=MESH)
        return carry

    def greet_ctx(i, carry):
        pl.semaphore_signal(barrier, inc=1, device_id=(lax.rem(c + i, n_ctx), z), device_id_type=MESH)
        return carry

    lax.fori_loop(1, n_head, greet_head, 0)
    lax.fori_loop(1, n_ctx, greet_ctx, 0)

    halves = (pl.ds(0, width // 2), pl.ds(width // 2, width // 2))

    def grad_copy(block, shift, i, half=None):
        ref = gfull.at[block] if half is None else gfull.at[block, :, halves[half]]
        return pltpu.make_async_remote_copy(
            src_ref=ref, dst_ref=ref, send_sem=g_ss.at[i], recv_sem=g_rs.at[block, half or 0],
            device_id=(c, lax.rem(z + shift + n_head, n_head)), device_id_type=MESH)

    def zed(shift):
        return lax.rem(z + shift + n_head, n_head)

    def pair_copy(i, src, dst):
        return pltpu.make_async_remote_copy(
            src_ref=src, dst_ref=dst, send_sem=p_ss.at[i], recv_sem=p_rs.at[i],
            device_id=(partner, z), device_id_type=MESH)

    def peer(i):
        return lax.rem(chip + i, n_chip)

    def chip_at(first_shift, second_shift):
        to_col = lax.rem(col + (1 - core) * first_shift + core * second_shift, side)
        to_row = lax.rem(row + core * first_shift + (1 - core) * second_shift, side)
        return to_row * side + to_col

    upper, lower = pl.ds(0, dim // 2), pl.ds(dim // 2, dim // 2)
    t_sent = []

    def t_start(block, first_shift, second_shift, half=None):
        ref = tall.at[block] if half is None else tall.at[block, (upper, lower)[half]]
        copy = pltpu.make_async_remote_copy(
            src_ref=ref, dst_ref=ref,
            send_sem=t_ss.at[len(t_sent)], recv_sem=t_rs.at[block, half or 0],
            device_id=(chip_at(first_shift, second_shift) * 2 + core, z), device_id_type=MESH)
        copy.start()
        t_sent.append(copy)

    def t_wait(block, half=None):
        ref = tall.at[block] if half is None else tall.at[block, (upper, lower)[half]]
        pltpu.make_async_remote_copy(
            src_ref=ref, dst_ref=ref, send_sem=t_ss.at[0], recv_sem=t_rs.at[block, half or 0],
            device_id=(partner, z), device_id_type=MESH).wait_recv()

    def t_own():
        for shift in (1, 3, 2):
            t_start(chip, shift, 0)
            if shift != 2:
                t_start(chip, 0, shift)

    def t_first(*shifts):
        for shift in shifts:
            block = chip_at(shift, 0)
            t_wait(block)
            t_start(block, 0, 1)
            t_start(block, 0, 3)

    def t_second(*shifts):
        for shift in shifts:
            for came, to, half in ((3, 1, 0), (1, 3, 1)):
                block = chip_at(shift, came)
                t_wait(block)
                t_start(block, 0, to, half)

    def t_last():
        for shift in (0, 1, 3, 2):
            for half in range(2):
                t_wait(chip_at(shift, 2), half)

    def l_copy(i):
        return pltpu.make_async_remote_copy(
            src_ref=lsend.at[peer(i)], dst_ref=lslice.at[chip], send_sem=l_ss.at[i], recv_sem=l_rs.at[i],
            device_id=(peer(i) * 2 + core, z), device_id_type=MESH)

    def a_copy(i):
        return pltpu.make_async_remote_copy(
            src_ref=asend.at[peer(i)], dst_ref=aslice.at[chip], send_sem=a_ss.at[i], recv_sem=a_rs.at[i],
            device_id=(peer(i) * 2 + core, z), device_id_type=MESH)

    def r_copy(i):
        return pltpu.make_async_remote_copy(
            src_ref=ret_out.at[peer(i)], dst_ref=ret_in.at[chip], send_sem=r_ss.at[i], recv_sem=r_rs.at[i],
            device_id=(peer(i) * 2 + core, z), device_id_type=MESH)

    def o_copy(i):
        to = lax.rem(z + i, n_head)
        return pltpu.make_async_remote_copy(
            src_ref=lpart.at[to], dst_ref=lrecv.at[z], send_sem=o_ss.at[i], recv_sem=o_rs.at[i],
            device_id=(c, to), device_id_type=MESH)

    def w_copy(i):
        to = lax.rem(c + i, n_ctx)
        return pltpu.make_async_remote_copy(
            src_ref=wpart.at[to], dst_ref=wrecv.at[c], send_sem=w_ss.at[i], recv_sem=w_rs.at[i],
            device_id=(to, z), device_id_type=MESH)

    def start_all(copy, n):
        def body(i, carry):
            copy(i).start()
            return carry
        lax.fori_loop(1, n, body, 0)

    def recv_all(copy, n):
        def body(i, carry):
            copy(i).wait_recv()
            return carry
        lax.fori_loop(1, n, body, 0)

    def sent_all(copy, n):
        def body(i, carry):
            copy(i).wait_send()
            return carry
        lax.fori_loop(1, n, body, 0)

    for load in loads[1:6]:
        load.wait()
    q = q_ref[...].astype(f32)
    k = k_ref[...].astype(f32)
    q_inv = 1.0 / jnp.sqrt(rowsum(q * q) + 1e-6)
    k_inv = 1.0 / jnp.sqrt(rowsum(k * k) + 1e-6)
    qn = q * q_inv
    kn = k * k_inv
    ks, qs = split(kn), split(qn)
    dots = mm(rows(ks, qs), ks, 1, 1)
    kk, qk = dots[:tok], dots[tok:]
    ii = lax.broadcasted_iota(jnp.int32, (tok, tok), 0)
    jj = lax.broadcasted_iota(jnp.int32, (tok, tok), 1)
    first = c * tok
    seg_i = jnp.zeros((tok, tok), f32)
    seg_j = jnp.zeros((tok, tok), f32)
    seg_all = jnp.zeros((1, 1), f32)
    for d in range(n_docs):
        at = docs_ref[d] - first
        seg_i = seg_i + jnp.where((ii >= at) & (at >= 0), 1.0, 0.0)
        seg_j = seg_j + jnp.where((jj >= at) & (at >= 0), 1.0, 0.0)
    seg_all = seg_i[tok - 1:, :]
    same = jnp.where(seg_i == seg_j, 1.0, 0.0)
    low = jnp.where(ii >= jj, same, 0.0)
    strict = jnp.where(ii > jj, same, 0.0)
    eye = jnp.where(ii == jj, 1.0, 0.0)
    at_start = jnp.where(seg_i[:, :1] == 0.0, 1.0, 0.0)
    at_end = jnp.where(seg_i[:, :1] == seg_all[:, :1], 1.0, 0.0)
    no_reset = jnp.where(seg_all[:, :1] == 0.0, 1.0, 0.0)

    upto = jnp.where(ii <= jj, 1.0, 0.0)
    cum_rows = lax.dot_general(decay_ref[...], upto, (((1,), (0,)), ((), ())),
                               precision=lax.Precision.HIGHEST, preferred_element_type=f32)

    def column(row):
        return rowsum(jnp.where(ii == jj, row, 0.0))

    info = []
    for h in range(2):
        cr = cum_rows[h:h + 1]
        cc = column(cr)
        b = column(rate_ref[h:h + 1, :])
        last = cr[:, tok - 1:]
        info.append(dict(
            b=b,
            ratio=jnp.exp(jnp.where(low > 0.0, cc - cr, 0.0)) * low,
            f=jnp.exp(cc) * at_start,
            e=jnp.exp(last - cc) * at_end,
            w=jnp.exp(last) * no_reset,
        ))

    pl.semaphore_wait(barrier, n_head + n_ctx - 2)
    loads[0].wait()
    g_sent = []

    def g_start(*args):
        copy = grad_copy(*args)
        copy.start()
        g_sent.append(copy)

    if n_head > 1:
        for i, shift in enumerate((2, -2, 1, -1)):
            g_start(z, shift, i)

    def same_block(size):
        shift = size.bit_length() - 1
        return lax.shift_right_logical(ii, shift) == lax.shift_right_logical(jj, shift)

    for h in range(2):
        t = info[h]
        t["kr"] = kk * t["ratio"] * strict
        t["n"] = t["b"] * t["kr"]
    for h in range(2):
        t = info[h]
        x = jnp.where(same_block(16), -t["n"], 0.0)
        xs = split(x)
        x2 = mm(xs, xs)
        x2s = split(x2)
        x4 = mm(x2s, x2s)
        x4s = split(x4)
        x8s = split(mm(x4s, x4s))
        m = eye + x
        m = m + mm(m, x2s)
        m = m + mm(m, x4s)
        m = m + mm(m, x8s)
        t["m"] = m
    for size in (16, 32, 64):
        for h in range(2):
            t = info[h]
            off = jnp.where(same_block(2 * size) & ~same_block(size), t["n"], 0.0)
            ms = split(t["m"])
            t["m"] = t["m"] - mm(ms, mm(off, ms))
    if n_head > 1:
        for sign, half in ((1, 0), (-1, 1)):
            block = zed(-2 * sign)
            grad_copy(block, sign, 0).wait_recv()
            g_start(block, sign, len(g_sent))
            g_start(block, 2 * sign, len(g_sent), half)
    loads[6].wait()
    v_all = v_ref[...].astype(f32)
    for h in range(2):
        t = info[h]
        v = v_all[:, h * dim:(h + 1) * dim]
        t["v"] = v
        t["ms"] = split(t["m"])
        uw = mm(t["ms"], cols(t["b"] * v, (t["b"] * t["f"]) * kn))
        uws = split(uw)
        t["u"], t["wks"] = uw[:, :dim], (uws[0][:, dim:], uws[1][:, dim:])
        ek = t["e"] * kn
        t["eks"] = split(ek)
        lt = mm(uws, t["eks"], 0, 0)
        tl_own[h, 0] = t["w"] * eye - lt[dim:]
        tl_own[h, 1] = lt[:dim]
        t["uws"] = uws

    tl_pair[core] = tl_own[core]
    tl_copy = pair_copy(0, tl_own.at[1 - core], tl_pair.at[core])
    tl_copy.start()
    for h in range(2):
        t = info[h]
        p = qk * t["ratio"]
        t["ps"] = split(p)
        ow = mm(t["ps"], t["uws"])
        t["o"] = ow[:, :dim]
        t["qt"] = t["f"] * qn - ow[:, dim:]
        t["qts"] = split(t["qt"])
    tl_copy.wait_recv()
    t1s = split(tl_pair[1, 0])
    t0s = split(tl_pair[0, 0])
    pair_t = mm(rows(t0s, tl_pair[0, 1]), t1s)
    tall[chip] = pair_t[:dim]
    pair_l = (pair_t[dim:] + tl_pair[1, 1]).reshape(n_chip, slice_rows, dim)
    lsend[...] = pair_l
    if side > 1:
        t_own()
    start_all(l_copy, n_chip)
    lslice[chip] = lsend[chip]

    if n_head > 1:
        for shift in (1, -1, 3, -3):
            grad_copy(zed(shift), 1, 0).wait_recv()
        for half in range(2):
            grad_copy(zed(4), 1, 0, half).wait_recv()
    loads[7].wait()
    full_grad = gfull[...].reshape(tok, width)
    weight = w_ref[...]
    d_core = lax.dot_general(full_grad, weight, (((1,), (1,)), ((), ())), preferred_element_type=f32)
    for h in range(2):
        t = info[h]
        t["do"] = d_core[:, h * dim:(h + 1) * dim]
        t["dos"] = split(t["do"])
        a_own[h] = mm(t["dos"], t["qts"], 0, 0)
    a_pair[core] = a_own[core]
    ap_copy = pair_copy(1, a_own.at[1 - core], a_pair.at[core])
    ap_copy.start()
    if side > 1:
        t_first(1, 3)
        t_second(0)
        t_first(2)
    for h in range(2):
        t = info[h]
        t["pd"] = mm(t["ps"], t["dos"], 0, 0)
    ap_copy.wait_recv()
    asend[...] = (mm(a_pair[1], t0s, 1, 1) + a_pair[0]).reshape(n_chip, slice_rows, dim)
    start_all(a_copy, n_chip)
    aslice[chip] = asend[chip]

    if side > 1:
        t_second(1, 3)
        t_second(2)
        t_last()
    recv_all(l_copy, n_chip)
    recv_all(a_copy, n_chip)
    state = jnp.zeros((slice_rows, dim), f32)
    adjoint = jnp.zeros((slice_rows, dim), f32)
    for i in range(n_chip):
        j = n_chip - 1 - i
        ret_out[i, 0] = state
        ret_out[j, 1] = adjoint
        if i < n_chip - 1:
            state = mm(state, tall[i]) + lslice[i]
            adjoint = mm(adjoint, tall[j], 1, 1) + aslice[j]
    start_all(r_copy, n_chip)
    ret_in[chip] = ret_out[chip]
    recv_all(r_copy, n_chip)
    state = ret_in[:, 0].reshape(dim, dim)
    adjoint = ret_in[:, 1].reshape(dim, dim)
    sg_pair[0, 0] = state
    sg_pair[1, 0] = mm(state, t0s) + tl_pair[0, 1]
    sg_pair[0, 1] = mm(adjoint, t1s, 1, 1) + a_pair[1]
    sg_pair[1, 1] = adjoint
    sg_fin[core] = sg_pair[core]
    sg_copy = pair_copy(2, sg_pair.at[1 - core], sg_fin.at[core])
    sg_copy.start()
    sg_copy.wait_recv()

    mixed = []
    for h in range(2):
        t = info[h]
        t["s"] = sg_fin[h, 0]
        t["g"] = sg_fin[h, 1]
        t["ss"], t["gs"] = split(t["s"]), split(t["g"])
        both = mm(rows(t["qts"], t["wks"]), t["ss"], 1, 1)
        mixed.append((t["o"] + both[:tok]).astype(bf16))
        t["p"] = t["u"] - both[tok:]
    mixed = jnp.concatenate(mixed, axis=1)
    partial = lax.dot_general(mixed, weight, (((1,), (0,)), ((), ())), preferred_element_type=f32)
    lpart[...] = partial.astype(bf16).reshape(lpart.shape)
    start_all(o_copy, n_head)
    wpartial = lax.dot_general(full_grad, mixed, (((0,), (0,)), ((), ())), preferred_element_type=f32)
    wpart[...] = wpartial.astype(bf16).reshape(wpart.shape)
    start_all(w_copy, n_ctx)
    lrecv[z] = lpart[z]
    wrecv[c] = wpart[c]

    dqk = jnp.zeros((tok, tok), f32)
    dkk = jnp.zeros((tok, tok), f32)
    dq = jnp.zeros((tok, dim), f32)
    dk = jnp.zeros((tok, dim), f32)
    before = jnp.where(ii < jj, 1.0, 0.0).astype(bf16)
    for h in range(2):
        t = info[h]
        b, f, e = t["b"], t["f"], t["e"]
        pps = split(t["p"])
        pg = mm(pps, t["gs"])
        dp = t["pd"] + mm(t["eks"], t["gs"], 1, 1)
        dr = mm(t["ms"], dp, 0, 0)
        both = rows(t["dos"], dr)
        dpn = mm(both, pps, 1, 1)
        dos_s = mm(both, t["ss"])
        d_o_s, d_r_s = dos_s[:tok], dos_s[tok:]
        xp = dpn[:tok] * t["ratio"]
        xr = -dpn[tok:] * t["kr"]
        xn = -dpn[tok:] * (b * t["ratio"] * strict)
        dqk = dqk + xp
        dkk = dkk + xn
        x = xp * qk + b * xr
        alpha = rowsum(qn * d_o_s)
        beta = rowsum(kn * d_r_s)
        db = rowsum(dr * t["v"]) - f * beta + rowsum(xr)
        gv_ref[:, h * dim:(h + 1) * dim] = b * dr
        grate_ref[h:h + 1, :] = jnp.sum(jnp.where(ii == jj, db, 0.0), axis=0, keepdims=True)
        fdf = f * (alpha - b * beta)
        ede = e * rowsum(kn * pg)
        y = mm(x, before)
        terms = jnp.where(ii >= jj, y + fdf, ede)
        wdw = t["w"] * jnp.sum(rowsum(t["s"] * t["g"]), axis=0, keepdims=True)
        gdecay_ref[h:h + 1, :] = jnp.sum(terms, axis=0, keepdims=True) + wdw
        dq = dq + f * d_o_s
        dk = dk + e * pg - (b * f) * d_r_s
    ds = rows(dqk, dkk)
    direct = mm(ds, ks)
    turned = mm(ds, rows(qs, ks), 0, 0)
    dq = dq + direct[:tok]
    dk = dk + direct[tok:] + turned
    gq_ref[...] = q_inv * (dq - qn * rowsum(qn * dq))
    gk_ref[...] = k_inv * (dk - kn * rowsum(kn * dk))

    recv_all(o_copy, n_head)
    out_ref[...] = jnp.sum(lrecv[...].astype(f32), axis=0)
    recv_all(w_copy, n_ctx)
    wg_ref[...] = jnp.sum(wrecv[...].astype(f32), axis=0)

    tl_copy.wait_send()
    ap_copy.wait_send()
    sg_copy.wait_send()
    for copy in g_sent + t_sent:
        copy.wait_send()
    sent_all(l_copy, n_chip)
    sent_all(a_copy, n_chip)
    sent_all(r_copy, n_chip)
    sent_all(o_copy, n_head)
    sent_all(w_copy, n_ctx)


def per_device(n_ctx, n_head, queries, key_vectors, value_rows, write_rate, log_decay, doc_offsets, out_weight, grad_out):
    n_chip = n_ctx // 2
    tok, dim = queries.shape
    width = grad_out.shape[1]
    share = grad_out.shape[0]
    sl = dim // n_chip
    wrows = width // n_ctx
    vmem = pl.BlockSpec(memory_space=pltpu.VMEM)
    hbm = pl.BlockSpec(memory_space=pltpu.HBM)
    dma = pltpu.SemaphoreType.DMA
    scratch = [
        pltpu.SMEM(doc_offsets.shape, jnp.int32),
        pltpu.VMEM((tok, dim), bf16), pltpu.VMEM((tok, dim), bf16), pltpu.VMEM((tok, 2 * dim), bf16),
        pltpu.VMEM((2, tok), f32), pltpu.VMEM((2, tok), f32), pltpu.VMEM((2 * dim, width), bf16),
        pltpu.VMEM((n_head, share, width), bf16),
        pltpu.VMEM((2, 2, dim, dim), f32), pltpu.VMEM((2, 2, dim, dim), f32),
        pltpu.VMEM((2, dim, dim), f32), pltpu.VMEM((2, dim, dim), f32),
        pltpu.VMEM((n_chip, dim, dim), f32), pltpu.VMEM((dim, dim), f32),
        pltpu.VMEM((n_chip, sl, dim), f32), pltpu.VMEM((n_chip, sl, dim), f32),
        pltpu.VMEM((n_chip, sl, dim), f32), pltpu.VMEM((n_chip, sl, dim), f32),
        pltpu.VMEM((n_chip, 2, sl, dim), f32), pltpu.VMEM((n_chip, 2, sl, dim), f32),
        pltpu.VMEM((2, 2, dim, dim), f32), pltpu.VMEM((2, 2, dim, dim), f32),
        pltpu.VMEM((n_head, share, width), bf16), pltpu.VMEM((n_head, share, width), bf16),
        pltpu.VMEM((n_ctx, wrows, 2 * dim), bf16), pltpu.VMEM((n_ctx, wrows, 2 * dim), bf16),
        dma((8,)),
        dma((8,)), dma((n_head, 2)), dma((3,)), dma((3,)),
        dma((19,)), dma((n_chip, 2)), dma((n_chip,)), dma((n_chip,)),
        dma((n_chip,)), dma((n_chip,)), dma((n_chip,)), dma((n_chip,)),
        dma((n_head,)), dma((n_head,)), dma((n_ctx,)), dma((n_ctx,)),
    ]
    shapes = (
        jax.ShapeDtypeStruct((share, width), f32),
        jax.ShapeDtypeStruct((tok, dim), f32),
        jax.ShapeDtypeStruct((tok, dim), f32),
        jax.ShapeDtypeStruct((tok, 2 * dim), f32),
        jax.ShapeDtypeStruct((2, tok), f32),
        jax.ShapeDtypeStruct((2, tok), f32),
        jax.ShapeDtypeStruct((wrows, 2 * dim), f32),
    )
    results = pl.pallas_call(
        functools.partial(kernel, n_ctx, n_head),
        out_shape=shapes,
        in_specs=[hbm] * 8,
        out_specs=(vmem,) * 7,
        scratch_shapes=scratch,
        compiler_params=pltpu.CompilerParams(collective_id=0, has_side_effects=True,
                                             vmem_limit_bytes=60 * 1024 * 1024),
        name="layer",
    )(doc_offsets, queries, key_vectors, value_rows, write_rate, log_decay, out_weight, grad_out)
    return pl.pallas_call(
        emit,
        out_shape=shapes,
        in_specs=[vmem] * 7,
        out_specs=(hbm,) * 7,
        scratch_shapes=[dma((7,))],
        name="emit",
    )(*results)


def emit(*refs):
    copies = [pltpu.make_async_copy(refs[i], refs[7 + i], refs[14].at[i]) for i in range(7)]
    for copy in copies:
        copy.start()
    for copy in copies:
        copy.wait()


def solution(mesh):
    n_ctx, n_head = mesh.shape["ctx"], mesh.shape["head"]
    return jax.shard_map(
        functools.partial(per_device, n_ctx, n_head),
        mesh=mesh,
        in_specs=(
            P("ctx", "head"), P("ctx", "head"), P("ctx", "head"), P("head", "ctx"), P("head", "ctx"),
            P(), P("head", None), P(("ctx", "head"), None),
        ),
        out_specs=(
            P(("ctx", "head"), None), P("ctx", "head"), P("ctx", "head"), P("ctx", "head"),
            P("head", "ctx"), P("head", "ctx"), P("ctx", "head"),
        ),
        check_vma=False,
    )
```

```python
import functools

import jax
import jax.numpy as jnp
from jax import lax
from jax.experimental import pallas as pl
from jax.experimental.pallas import tpu as pltpu
from jax.sharding import PartitionSpec as P

f32 = jnp.float32
bf16 = jnp.bfloat16
MESH = pl.DeviceIdType.MESH


def split(x):
    hi = x.astype(bf16)
    return hi, (x - hi.astype(f32)).astype(bf16)


def mm(a, b, ca=1, cb=0):
    if not isinstance(a, tuple):
        a = (a,) if a.dtype == bf16 else split(a)
    if not isinstance(b, tuple):
        b = (b,) if b.dtype == bf16 else split(b)
    left, right = [a[0]], [b[0]]
    if len(a) == 2:
        left.append(a[1])
        right.append(b[0])
    if len(b) == 2:
        left.append(a[0])
        right.append(b[1])
    left = jnp.concatenate(left, axis=ca) if len(left) > 1 else left[0]
    right = jnp.concatenate(right, axis=cb) if len(right) > 1 else right[0]
    return lax.dot_general(left, right, (((ca,), (cb,)), ((), ())), preferred_element_type=f32)


def rows(*parts):
    parts = [p if isinstance(p, tuple) else split(p) for p in parts]
    return tuple(jnp.concatenate([p[i] for p in parts], axis=0) for i in range(2))


def cols(*parts):
    parts = [p if isinstance(p, tuple) else split(p) for p in parts]
    return tuple(jnp.concatenate([p[i] for p in parts], axis=1) for i in range(2))


def rowsum(x):
    return jnp.sum(x, axis=1, keepdims=True)


def kernel(
    n_ctx, n_head,
    docs_hbm, q_hbm, k_hbm, v_hbm, rate_hbm, decay_hbm, w_hbm, g_hbm,
    out_ref, gq_ref, gk_ref, gv_ref, grate_ref, gdecay_ref, wg_ref,
    docs_ref, q_ref, k_ref, v_ref, rate_ref, decay_ref, w_ref,
    gfull, gcol, gturn, tl_own, tl_oth, a_own, a_oth, tall, mall, lslice, aslice, lsend, asend,
    sret_out, sret_in, aret_out, aret_in, lpart, lrecv, wx_own, wx_oth,
    i_s, g_ss, g_rs, e_ss, e_rs, h_ss, h_rs, p_ss, p_rs, t_ss, t_rs, m_ss, m_rs,
    l_ss, l_rs, a_ss, a_rs, s_ss, s_rs, r_ss, r_rs, o_ss, o_rs,
):
    n_chip = n_ctx // 2
    side = 4 if n_chip == 16 else 1
    c = lax.axis_index("ctx")
    z = lax.axis_index("head")
    chip = lax.div(c, 2)
    core = lax.rem(c, 2)
    partner = c + 1 - 2 * core
    row = lax.div(chip, side)
    col = lax.rem(chip, side)
    tok = q_ref.shape[0]
    dim = 128
    width = w_ref.shape[1]
    n_docs = docs_ref.shape[0] - 1
    slice_rows = dim // n_chip

    loads = [
        pltpu.make_async_copy(src, dst, i_s.at[i])
        for i, (src, dst) in enumerate((
            (g_hbm, gfull.at[z]), (q_hbm, q_ref), (k_hbm, k_ref), (docs_hbm, docs_ref),
            (rate_hbm, rate_ref), (decay_hbm, decay_ref), (v_hbm, v_ref), (w_hbm, w_ref),
        ))
    ]
    for load in loads:
        load.start()

    barrier = pltpu.get_barrier_semaphore()

    def greet_head(i, carry):
        pl.semaphore_signal(barrier, inc=1, device_id=(c, lax.rem(z + i, n_head)), device_id_type=MESH)
        return carry

    def greet_ctx(i, carry):
        pl.semaphore_signal(barrier, inc=1, device_id=(lax.rem(c + i, n_ctx), z), device_id_type=MESH)
        return carry

    lax.fori_loop(1, n_head, greet_head, 0)
    lax.fori_loop(1, n_ctx, greet_ctx, 0)

    def zed(shift):
        return lax.rem(z + shift + n_head, n_head)

    def peer(i):
        return lax.rem(chip + i, n_chip)

    def fence(body):
        pl.when(c >= 0)(body)

    def across_head(buf, ss, rs, part):
        sends = [(0, 2, None), (0, -2, None), (0, 1, None), (0, -1, None),
                 (-2, 1, None), (-2, 2, 0), (2, -1, None), (2, -2, 1)]

        def copy(i, block, shift, half):
            ref = buf.at[block] if half is None else part(buf, block, half)
            return pltpu.make_async_remote_copy(
                src_ref=ref, dst_ref=ref, send_sem=ss.at[i], recv_sem=rs.at[block, half or 0],
                device_id=(c, zed(shift)), device_id_type=MESH)

        def start(*which):
            for i in which:
                origin, shift, half = sends[i]
                copy(i, zed(origin), shift, half).start()

        def received(*origins):
            for origin in origins:
                for half in ((0, 1) if origin == 4 else (None,)):
                    copy(0, zed(origin), 1, half).wait_recv()

        def relay():
            received(-2)
            start(4, 5)
            received(2)
            start(6, 7)

        def sent():
            for i, (origin, shift, half) in enumerate(sends):
                copy(i, zed(origin), shift, half).wait_send()

        return start, relay, received, sent

    def chip_at(first_shift, second_shift):
        to_col = lax.rem(col + (1 - core) * first_shift + core * second_shift, side)
        to_row = lax.rem(row + core * first_shift + (1 - core) * second_shift, side)
        return to_row * side + to_col

    def across_plane(buf, ss, rs):
        rows_of = buf.shape[1] // 2
        sends = []

        def copy(i, origin, to, half):
            block = chip_at(*origin)
            ref = buf.at[block] if half is None else buf.at[block, pl.ds(half * rows_of, rows_of)]
            return pltpu.make_async_remote_copy(
                src_ref=ref, dst_ref=ref, send_sem=ss.at[i], recv_sem=rs.at[block, half or 0],
                device_id=(chip_at(*to) * 2 + core, z), device_id_type=MESH)

        def start(origin, to, half=None):
            sends.append((origin, to, half))
            copy(len(sends) - 1, origin, to, half).start()

        def received(origin, half=None):
            copy(0, origin, (0, 1), half).wait_recv()

        def own():
            for shift in (1, 3, 2):
                start((0, 0), (shift, 0))
                if shift != 2:
                    start((0, 0), (0, shift))

        def first(*shifts):
            for shift in shifts:
                received((shift, 0))
                start((shift, 0), (0, 1))
                start((shift, 0), (0, 3))

        def second(*shifts):
            for shift in shifts:
                for came, to, half in ((3, 1, 0), (1, 3, 1)):
                    received((shift, came))
                    start((shift, came), (0, to), half)

        def last():
            for shift in (0, 1, 3, 2):
                for half in range(2):
                    received((shift, 2), half)

        def sent():
            for i, args in enumerate(sends):
                copy(i, *args).wait_send()

        return own, first, second, last, sent

    g_start, g_relay, g_received, g_sent = across_head(
        gfull, g_ss, g_rs, lambda buf, block, half: buf.at[block, :, pl.ds(half * (width // 2), width // 2)])
    h_start, h_relay, h_received, h_sent = across_head(
        gcol, h_ss, h_rs, lambda buf, block, half: (
            buf.at[block, pl.ds(half * (n_chip // 2), n_chip // 2)] if n_chip > 1
            else buf.at[block, :, :, pl.ds(half * 128, 128)]))
    t_own, t_first, t_second, t_last, t_sent = across_plane(tall, t_ss, t_rs)
    m_own, m_first, m_second, m_last, m_sent = across_plane(mall, m_ss, m_rs)

    def pair_copy(i, src, dst):
        return pltpu.make_async_remote_copy(
            src_ref=src, dst_ref=dst, send_sem=p_ss.at[i], recv_sem=p_rs.at[i],
            device_id=(partner, z), device_id_type=MESH)

    def to_chips(src_of, dst, ss, rs):
        def copy(i):
            return pltpu.make_async_remote_copy(
                src_ref=src_of(peer(i)), dst_ref=dst, send_sem=ss.at[i], recv_sem=rs.at[i],
                device_id=(peer(i) * 2 + core, z), device_id_type=MESH)
        return copy

    chip_width = width // n_chip
    e_copy = to_chips(lambda to: gfull.at[z, :, pl.ds(pl.multiple_of(to * chip_width, 128), chip_width)],
                      gcol.at[z, chip], e_ss, e_rs)
    l_copy = to_chips(lambda to: lsend.at[to], lslice.at[chip], l_ss, l_rs)
    a_copy = to_chips(lambda to: asend.at[to], aslice.at[chip], a_ss, a_rs)

    def to_plane(src, dst, ss, rs):
        def copy(i):
            to = lax.rem(c + i, n_ctx)
            return pltpu.make_async_remote_copy(
                src_ref=src.at[lax.div(to, 2)], dst_ref=dst.at[core, chip],
                send_sem=ss.at[i], recv_sem=rs.at[i], device_id=(to, z), device_id_type=MESH)
        return copy

    s_copy = to_plane(sret_out, sret_in, s_ss, s_rs)
    r_copy = to_plane(aret_out, aret_in, r_ss, r_rs)

    def o_copy(i):
        to = lax.rem(z + i, n_head)
        return pltpu.make_async_remote_copy(
            src_ref=lpart.at[to], dst_ref=lrecv.at[z], send_sem=o_ss.at[i], recv_sem=o_rs.at[i],
            device_id=(c, to), device_id_type=MESH)

    def start_all(copy, n):
        def body(i, carry):
            copy(i).start()
            return carry
        lax.fori_loop(1, n, body, 0)

    def recv_all(copy, n):
        def body(i, carry):
            copy(i).wait_recv()
            return carry
        lax.fori_loop(1, n, body, 0)

    def sent_all(copy, n):
        def body(i, carry):
            copy(i).wait_send()
            return carry
        lax.fori_loop(1, n, body, 0)

    for load in loads[1:6]:
        load.wait()
    q = q_ref[...].astype(f32)
    k = k_ref[...].astype(f32)
    q_inv = 1.0 / jnp.sqrt(rowsum(q * q) + 1e-6)
    k_inv = 1.0 / jnp.sqrt(rowsum(k * k) + 1e-6)
    qn = q * q_inv
    kn = k * k_inv
    ks, qs = split(kn), split(qn)
    dots = mm(rows(ks, qs), ks, 1, 1)
    kk, qk = dots[:tok], dots[tok:]
    ii = lax.broadcasted_iota(jnp.int32, (tok, tok), 0)
    jj = lax.broadcasted_iota(jnp.int32, (tok, tok), 1)
    first = c * tok
    seg_i = jnp.zeros((tok, tok), f32)
    seg_j = jnp.zeros((tok, tok), f32)
    seg_all = jnp.zeros((1, 1), f32)
    for d in range(n_docs):
        at = docs_ref[d] - first
        seg_i = seg_i + jnp.where((ii >= at) & (at >= 0), 1.0, 0.0)
        seg_j = seg_j + jnp.where((jj >= at) & (at >= 0), 1.0, 0.0)
    seg_all = seg_i[tok - 1:, :]
    same = jnp.where(seg_i == seg_j, 1.0, 0.0)
    low = jnp.where(ii >= jj, same, 0.0)
    strict = jnp.where(ii > jj, same, 0.0)
    eye = jnp.where(ii == jj, 1.0, 0.0)
    at_start = jnp.where(seg_i[:, :1] == 0.0, 1.0, 0.0)
    at_end = jnp.where(seg_i[:, :1] == seg_all[:, :1], 1.0, 0.0)
    no_reset = jnp.where(seg_all[:, :1] == 0.0, 1.0, 0.0)

    upto = jnp.where(ii <= jj, 1.0, 0.0)
    cum_rows = lax.dot_general(decay_ref[...], upto, (((1,), (0,)), ((), ())),
                               precision=lax.Precision.HIGHEST, preferred_element_type=f32)

    def column(row):
        return rowsum(jnp.where(ii == jj, row, 0.0))

    info = []
    for h in range(2):
        cr = cum_rows[h:h + 1]
        cc = column(cr)
        b = column(rate_ref[h:h + 1, :])
        last = cr[:, tok - 1:]
        info.append(dict(
            b=b,
            ratio=jnp.exp(jnp.where(low > 0.0, cc - cr, 0.0)) * low,
            f=jnp.exp(cc) * at_start,
            e=jnp.exp(last - cc) * at_end,
            w=jnp.exp(last) * no_reset,
        ))

    pl.semaphore_wait(barrier, n_head + n_ctx - 2)
    loads[0].wait()
    if n_head > 1:
        fence(lambda: g_start(0, 1, 2, 3))
    start_all(e_copy, n_chip)
    gcol[z, chip] = gfull[z, :, pl.ds(pl.multiple_of(chip * chip_width, 128), chip_width)]

    def same_block(size):
        shift = size.bit_length() - 1
        return lax.shift_right_logical(ii, shift) == lax.shift_right_logical(jj, shift)

    for h in range(2):
        t = info[h]
        t["kr"] = kk * t["ratio"] * strict
        t["n"] = t["b"] * t["kr"]
    for h in range(2):
        t = info[h]
        x = jnp.where(same_block(16), -t["n"], 0.0)
        xs = split(x)
        x2 = mm(xs, xs)
        x2s = split(x2)
        x4 = mm(x2s, x2s)
        x4s = split(x4)
        x8s = split(mm(x4s, x4s))
        m = eye + x
        m = m + mm(m, x2s)
        m = m + mm(m, x4s)
        m = m + mm(m, x8s)
        t["m"] = m
    for size in (16, 32, 64):
        for h in range(2):
            t = info[h]
            off = jnp.where(same_block(2 * size) & ~same_block(size), t["n"], 0.0)
            ms = split(t["m"])
            t["m"] = t["m"] - mm(ms, mm(off, ms))
    loads[6].wait()
    v_all = v_ref[...].astype(f32)
    for h in range(2):
        t = info[h]
        v = v_all[:, h * dim:(h + 1) * dim]
        t["v"] = v
        t["ms"] = split(t["m"])
        uw = mm(t["ms"], cols(t["b"] * v, (t["b"] * t["f"]) * kn))
        uws = split(uw)
        t["u"], t["wks"] = uw[:, :dim], (uws[0][:, dim:], uws[1][:, dim:])
        ek = t["e"] * kn
        t["eks"] = split(ek)
        lt = mm(uws, t["eks"], 0, 0)
        tl_own[h, 0] = t["w"] * eye - lt[dim:]
        tl_own[h, 1] = lt[:dim]
        t["uws"] = uws

    tl_copy = pair_copy(0, tl_own, tl_oth)
    fence(lambda: pair_copy(0, tl_own, tl_oth).start())
    for h in range(2):
        t = info[h]
        p = qk * t["ratio"]
        t["p_mat"] = p
        t["ps"] = split(p)
        ow = mm(t["ps"], t["uws"])
        t["o"] = ow[:, :dim]
        t["qt"] = t["f"] * qn - ow[:, dim:]
        t["qts"] = split(t["qt"])
    tl_copy.wait_recv()
    is_first = core == 0

    def ordered(own, other):
        return jnp.where(is_first, own, other), jnp.where(is_first, other, own)

    t0, t1 = ordered(tl_own[core, 0], tl_oth[core, 0])
    l0, l1 = ordered(tl_own[core, 1], tl_oth[core, 1])
    pair_t = mm(rows(t0, l0), t1)
    tall[chip] = pair_t[:dim]
    lsend[...] = (pair_t[dim:] + l1).reshape(n_chip, slice_rows, dim)
    if side > 1:
        fence(t_own)
    start_all(l_copy, n_chip)
    lslice[chip] = lsend[chip]
    if n_head > 1:
        fence(g_relay)
    recv_all(e_copy, n_chip)
    if n_head > 1:
        fence(lambda: h_start(0, 1, 2, 3))

    if side > 1:
        @fence
        def _():
            t_first(1, 3)
            t_second(0)
            t_first(2)
            t_second(1, 3)
            t_second(2)
            t_last()
    recv_all(l_copy, n_chip)
    state = jnp.zeros((slice_rows, dim), f32)
    for i in range(n_chip):
        sret_out[i] = state
        if i < n_chip - 1:
            state = mm(state, tall[i]) + lslice[i]
    start_all(s_copy, n_ctx)
    sret_in[core, chip] = sret_out[chip]

    if n_head > 1:
        g_received(1, -1, 3, -3, 4)
        fence(h_relay)
    loads[7].wait()
    full_grad = gfull[...].reshape(tok, width)
    weight = w_ref[...]
    d_core = lax.dot_general(full_grad, weight, (((1,), (1,)), ((), ())), preferred_element_type=f32)
    for h in range(2):
        t = info[h]
        t["do"] = d_core[:, h * dim:(h + 1) * dim]
        t["dos"] = split(t["do"])
        a_own[h] = mm(t["dos"], t["qts"], 0, 0)
    ap_copy = pair_copy(1, a_own, a_oth)
    fence(lambda: pair_copy(1, a_own, a_oth).start())

    recv_all(s_copy, n_ctx)
    mixed = []
    for h in range(2):
        t = info[h]
        state = sret_in[h].reshape(dim, dim)
        t["s"] = jnp.where(is_first, state, mm(state, tl_oth[h, 0]) + tl_oth[h, 1])
        t["ss"] = split(t["s"])
        both = mm(rows(t["qts"], t["wks"]), t["ss"], 1, 1)
        mixed.append((t["o"] + both[:tok]).astype(bf16))
        t["p"] = t["u"] - both[tok:]
    mixed = jnp.concatenate(mixed, axis=1)
    mall[chip] = mixed
    if side > 1:
        fence(m_own)
    partial = lax.dot_general(mixed, weight, (((1,), (0,)), ((), ())), preferred_element_type=f32)
    lpart[...] = partial.astype(bf16).reshape(lpart.shape)
    if n_head > 1:
        @fence
        def _():
            for i in (4, 3, 5, 2, 6, 1, 7):
                o_copy(i).start()
    lrecv[z] = lpart[z]

    ap_copy.wait_recv()
    a0, a1 = ordered(a_own[core], a_oth[core])
    asend[...] = (mm(a1, t0, 1, 1) + a0).reshape(n_chip, slice_rows, dim)
    start_all(a_copy, n_chip)
    aslice[chip] = asend[chip]
    if side > 1:
        @fence
        def _():
            m_first(1, 3)
            m_second(0)
    for h in range(2):
        t = info[h]
        t["pps"] = split(t["p"])
        t["pd"] = mm(t["ps"], t["dos"], 0, 0)
        t["xp"] = mm(t["dos"], t["pps"], 1, 1) * t["ratio"]
        t["d_o_s"] = mm(t["dos"], t["ss"])
    recv_all(a_copy, n_chip)
    adjoint = jnp.zeros((slice_rows, dim), f32)
    for j in reversed(range(n_chip)):
        aret_out[j] = adjoint
        if j > 0:
            adjoint = mm(adjoint, tall[j], 1, 1) + aslice[j]
    start_all(r_copy, n_ctx)
    aret_in[core, chip] = aret_out[chip]
    if side > 1:
        @fence
        def _():
            m_first(2)
            m_second(1, 3)
    if n_head > 1:
        h_received(1, -1, 3, -3, 4)
    for j in range(n_chip):
        gturn[j] = gcol[:, j].reshape(tok, chip_width).T
    if side > 1:
        fence(lambda: m_second(2))
    recv_all(r_copy, n_ctx)
    for h in range(2):
        t = info[h]
        adjoint = aret_in[h].reshape(dim, dim)
        t["g"] = jnp.where(is_first, mm(adjoint, tl_oth[h, 0], 1, 1) + a_oth[h], adjoint)
        t["gs"] = split(t["g"])

    dqk = jnp.zeros((tok, tok), f32)
    dkk = jnp.zeros((tok, tok), f32)
    dq = jnp.zeros((tok, dim), f32)
    dk = jnp.zeros((tok, dim), f32)
    before = jnp.where(ii < jj, 1.0, 0.0).astype(bf16)
    for h in range(2):
        t = info[h]
        b, f, e = t["b"], t["f"], t["e"]
        pps = t["pps"]
        pg = mm(pps, t["gs"])
        dp = t["pd"] + mm(t["eks"], t["gs"], 1, 1)
        dr = mm(t["ms"], dp, 0, 0)
        drs = split(dr)
        dn = -mm(drs, pps, 1, 1)
        d_o_s, d_r_s = t["d_o_s"], mm(drs, t["ss"])
        xp = t["xp"]
        xr = dn * t["kr"]
        xn = dn * (b * t["ratio"] * strict)
        dqk = dqk + xp
        dkk = dkk + xn
        x = xp * qk + b * xr
        alpha = rowsum(qn * d_o_s)
        beta = rowsum(kn * d_r_s)
        db = rowsum(dr * t["v"]) - f * beta + rowsum(xr)
        gv_ref[:, h * dim:(h + 1) * dim] = b * dr
        grate_ref[h:h + 1, :] = jnp.sum(jnp.where(ii == jj, db, 0.0), axis=0, keepdims=True)
        fdf = f * (alpha - b * beta)
        ede = e * rowsum(kn * pg)
        y = mm(x, before)
        terms = jnp.where(ii >= jj, y + fdf, ede)
        wdw = t["w"] * jnp.sum(rowsum(t["s"] * t["g"]), axis=0, keepdims=True)
        gdecay_ref[h:h + 1, :] = jnp.sum(terms, axis=0, keepdims=True) + wdw
        dq = dq + f * d_o_s
        dk = dk + e * pg - (b * f) * d_r_s
    ds = rows(dqk, dkk)
    direct = mm(ds, ks)
    turned = mm(ds, rows(qs, ks), 0, 0)
    dq = dq + direct[:tok]
    dk = dk + direct[tok:] + turned
    gq_ref[...] = q_inv * (dq - qn * rowsum(qn * dq))
    gk_ref[...] = k_inv * (dk - kn * rowsum(kn * dk))

    if side > 1:
        m_last()
    total = jnp.zeros((chip_width, 2 * dim), f32)
    for j in range(n_chip):
        total = total + lax.dot_general(gturn[j], mall[j], (((1,), (0,)), ((), ())), preferred_element_type=f32)
    half = chip_width // 2
    wx_own[0] = total[:half]
    wx_own[1] = total[half:]
    fence(lambda: pair_copy(2, wx_own.at[1 - core], wx_oth).start())
    recv_all(o_copy, n_head)
    out_ref[...] = jnp.sum(lrecv[...].astype(f32), axis=0)
    wx_copy = pair_copy(2, wx_own.at[1 - core], wx_oth)
    wx_copy.wait_recv()
    wg_ref[...] = wx_own[core] + wx_oth[...]

    tl_copy.wait_send()
    ap_copy.wait_send()
    wx_copy.wait_send()
    if n_head > 1:
        g_sent()
        h_sent()
    t_sent()
    m_sent()
    sent_all(e_copy, n_chip)
    sent_all(l_copy, n_chip)
    sent_all(a_copy, n_chip)
    sent_all(s_copy, n_ctx)
    sent_all(r_copy, n_ctx)
    sent_all(o_copy, n_head)


def per_device(n_ctx, n_head, queries, key_vectors, value_rows, write_rate, log_decay, doc_offsets, out_weight, grad_out):
    n_chip = n_ctx // 2
    tok, dim = queries.shape
    width = grad_out.shape[1]
    share = grad_out.shape[0]
    sl = dim // n_chip
    wrows = width // n_ctx
    vmem = pl.BlockSpec(memory_space=pltpu.VMEM)
    hbm = pl.BlockSpec(memory_space=pltpu.HBM)
    dma = pltpu.SemaphoreType.DMA
    scratch = [
        pltpu.SMEM(doc_offsets.shape, jnp.int32),
        pltpu.VMEM((tok, dim), bf16), pltpu.VMEM((tok, dim), bf16), pltpu.VMEM((tok, 2 * dim), bf16),
        pltpu.VMEM((2, tok), f32), pltpu.VMEM((2, tok), f32), pltpu.VMEM((2 * dim, width), bf16),
        pltpu.VMEM((n_head, share, width), bf16),
        pltpu.VMEM((n_head, n_chip, share, width // n_chip), bf16),
        pltpu.VMEM((n_chip, width // n_chip, tok), bf16),
        pltpu.VMEM((2, 2, dim, dim), f32), pltpu.VMEM((2, 2, dim, dim), f32),
        pltpu.VMEM((2, dim, dim), f32), pltpu.VMEM((2, dim, dim), f32),
        pltpu.VMEM((n_chip, dim, dim), f32), pltpu.VMEM((n_chip, tok, 2 * dim), bf16),
        pltpu.VMEM((n_chip, sl, dim), f32), pltpu.VMEM((n_chip, sl, dim), f32),
        pltpu.VMEM((n_chip, sl, dim), f32), pltpu.VMEM((n_chip, sl, dim), f32),
        pltpu.VMEM((n_chip, sl, dim), f32), pltpu.VMEM((2, n_chip, sl, dim), f32),
        pltpu.VMEM((n_chip, sl, dim), f32), pltpu.VMEM((2, n_chip, sl, dim), f32),
        pltpu.VMEM((n_head, share, width), bf16), pltpu.VMEM((n_head, share, width), bf16),
        pltpu.VMEM((2, wrows, 2 * dim), f32), pltpu.VMEM((wrows, 2 * dim), f32),
        dma((8,)),
        dma((8,)), dma((n_head, 2)), dma((n_chip,)), dma((n_chip,)), dma((8,)), dma((n_head, 2)), dma((3,)), dma((3,)),
        dma((19,)), dma((n_chip, 2)), dma((19,)), dma((n_chip, 2)),
        dma((n_chip,)), dma((n_chip,)), dma((n_chip,)), dma((n_chip,)),
        dma((n_ctx,)), dma((n_ctx,)), dma((n_ctx,)), dma((n_ctx,)), dma((n_head,)), dma((n_head,)),
    ]
    shapes = (
        jax.ShapeDtypeStruct((share, width), f32),
        jax.ShapeDtypeStruct((tok, dim), f32),
        jax.ShapeDtypeStruct((tok, dim), f32),
        jax.ShapeDtypeStruct((tok, 2 * dim), f32),
        jax.ShapeDtypeStruct((2, tok), f32),
        jax.ShapeDtypeStruct((2, tok), f32),
        jax.ShapeDtypeStruct((wrows, 2 * dim), f32),
    )
    results = pl.pallas_call(
        functools.partial(kernel, n_ctx, n_head),
        out_shape=shapes,
        in_specs=[hbm] * 8,
        out_specs=(vmem,) * 7,
        scratch_shapes=scratch,
        compiler_params=pltpu.CompilerParams(collective_id=0, has_side_effects=True,
                                             vmem_limit_bytes=60 * 1024 * 1024),
        name="layer",
    )(doc_offsets, queries, key_vectors, value_rows, write_rate, log_decay, out_weight, grad_out)
    return pl.pallas_call(
        emit,
        out_shape=shapes,
        in_specs=[vmem] * 7,
        out_specs=(hbm,) * 7,
        scratch_shapes=[dma((7,))],
        name="emit",
    )(*results)


def emit(*refs):
    copies = [pltpu.make_async_copy(refs[i], refs[7 + i], refs[14].at[i]) for i in range(7)]
    for copy in copies:
        copy.start()
    for copy in copies:
        copy.wait()


def solution(mesh):
    n_ctx, n_head = mesh.shape["ctx"], mesh.shape["head"]
    return jax.shard_map(
        functools.partial(per_device, n_ctx, n_head),
        mesh=mesh,
        in_specs=(
            P("ctx", "head"), P("ctx", "head"), P("ctx", "head"), P("head", "ctx"), P("head", "ctx"),
            P(), P("head", None), P(("ctx", "head"), None),
        ),
        out_specs=(
            P(("ctx", "head"), None), P("ctx", "head"), P("ctx", "head"), P("ctx", "head"),
            P("head", "ctx"), P("head", "ctx"), P("ctx", "head"),
        ),
        check_vma=False,
    )
```

```python
import functools

import jax
import jax.numpy as jnp
from jax import lax
from jax.experimental import pallas as pl
from jax.experimental.pallas import tpu as pltpu
from jax.sharding import PartitionSpec as P

f32 = jnp.float32
bf16 = jnp.bfloat16
MESH = pl.DeviceIdType.MESH


def split(x):
    hi = x.astype(bf16)
    return hi, (x - hi.astype(f32)).astype(bf16)


def mm(a, b, ca=1, cb=0):
    if not isinstance(a, tuple):
        a = (a,) if a.dtype == bf16 else split(a)
    if not isinstance(b, tuple):
        b = (b,) if b.dtype == bf16 else split(b)
    left, right = [a[0]], [b[0]]
    if len(a) == 2:
        left.append(a[1])
        right.append(b[0])
    if len(b) == 2:
        left.append(a[0])
        right.append(b[1])
    left = jnp.concatenate(left, axis=ca) if len(left) > 1 else left[0]
    right = jnp.concatenate(right, axis=cb) if len(right) > 1 else right[0]
    return lax.dot_general(left, right, (((ca,), (cb,)), ((), ())), preferred_element_type=f32)


def rows(*parts):
    parts = [p if isinstance(p, tuple) else split(p) for p in parts]
    return tuple(jnp.concatenate([p[i] for p in parts], axis=0) for i in range(2))


def cols(*parts):
    parts = [p if isinstance(p, tuple) else split(p) for p in parts]
    return tuple(jnp.concatenate([p[i] for p in parts], axis=1) for i in range(2))


def rowsum(x):
    return jnp.sum(x, axis=1, keepdims=True)


def kernel(
    n_ctx, n_head,
    docs_hbm, q_hbm, k_hbm, v_hbm, rate_hbm, decay_hbm, w_hbm, g_hbm,
    out_ref, gq_ref, gk_ref, gv_ref, grate_ref, gdecay_ref, wg_ref,
    docs_ref, q_ref, k_ref, v_ref, rate_ref, decay_ref, w_ref,
    gfull, gcol, gturn, tl_own, tl_oth, a_own, a_oth, tall, mall, lslice, aslice, lsend, asend,
    sret_out, sret_in, aret_out, aret_in, lpart, lfull, lsum, lrecv, wx_own, wx_oth,
    i_s, g_ss, g_rs, e_ss, e_rs, h_ss, h_rs, p_ss, p_rs, t_ss, t_rs, m_ss, m_rs,
    l_ss, l_rs, a_ss, a_rs, s_ss, s_rs, r_ss, r_rs, o_ss, o_rs,
):
    n_chip = n_ctx // 2
    side = 4 if n_chip == 16 else 1
    c = lax.axis_index("ctx")
    z = lax.axis_index("head")
    chip = lax.div(c, 2)
    core = lax.rem(c, 2)
    partner = c + 1 - 2 * core
    row = lax.div(chip, side)
    col = lax.rem(chip, side)
    tok = q_ref.shape[0]
    dim = 128
    width = w_ref.shape[1]
    n_docs = docs_ref.shape[0] - 1
    slice_rows = dim // n_chip

    loads = [
        pltpu.make_async_copy(src, dst, i_s.at[i])
        for i, (src, dst) in enumerate((
            (g_hbm, gfull.at[z]), (q_hbm, q_ref), (k_hbm, k_ref), (docs_hbm, docs_ref),
            (rate_hbm, rate_ref), (decay_hbm, decay_ref), (v_hbm, v_ref), (w_hbm, w_ref),
        ))
    ]
    for load in loads:
        load.start()

    barrier = pltpu.get_barrier_semaphore()

    def greet_head(i, carry):
        pl.semaphore_signal(barrier, inc=1, device_id=(c, lax.rem(z + i, n_head)), device_id_type=MESH)
        return carry

    def greet_ctx(i, carry):
        pl.semaphore_signal(barrier, inc=1, device_id=(lax.rem(c + i, n_ctx), z), device_id_type=MESH)
        return carry

    lax.fori_loop(1, n_head, greet_head, 0)
    lax.fori_loop(1, n_ctx, greet_ctx, 0)

    def zed(shift):
        return lax.rem(z + shift + n_head, n_head)

    def peer(i):
        return lax.rem(chip + i, n_chip)

    def fence(body):
        pl.when(c >= 0)(body)

    def across_head(buf, ss, rs, part):
        sends = [(0, 2, None), (0, -2, None), (0, 1, None), (0, -1, None),
                 (-2, 1, None), (-2, 2, 0), (2, -1, None), (2, -2, 1)]

        def copy(i, block, shift, half):
            ref = buf.at[block] if half is None else part(buf, block, half)
            return pltpu.make_async_remote_copy(
                src_ref=ref, dst_ref=ref, send_sem=ss.at[i], recv_sem=rs.at[block, half or 0],
                device_id=(c, zed(shift)), device_id_type=MESH)

        def start(*which):
            for i in which:
                origin, shift, half = sends[i]
                copy(i, zed(origin), shift, half).start()

        def received(*origins):
            for origin in origins:
                for half in ((0, 1) if origin == 4 else (None,)):
                    copy(0, zed(origin), 1, half).wait_recv()

        def relay():
            received(-2)
            start(4, 5)
            received(2)
            start(6, 7)

        def sent():
            for i, (origin, shift, half) in enumerate(sends):
                copy(i, zed(origin), shift, half).wait_send()

        return start, relay, received, sent

    def chip_at(first_shift, second_shift):
        to_col = lax.rem(col + (1 - core) * first_shift + core * second_shift, side)
        to_row = lax.rem(row + core * first_shift + (1 - core) * second_shift, side)
        return to_row * side + to_col

    def across_plane(buf, ss, rs):
        rows_of = buf.shape[1] // 2
        sends = []

        def copy(i, origin, to, half):
            block = chip_at(*origin)
            ref = buf.at[block] if half is None else buf.at[block, pl.ds(half * rows_of, rows_of)]
            return pltpu.make_async_remote_copy(
                src_ref=ref, dst_ref=ref, send_sem=ss.at[i], recv_sem=rs.at[block, half or 0],
                device_id=(chip_at(*to) * 2 + core, z), device_id_type=MESH)

        def start(origin, to, half=None):
            sends.append((origin, to, half))
            copy(len(sends) - 1, origin, to, half).start()

        def received(origin, half=None):
            copy(0, origin, (0, 1), half).wait_recv()

        def own():
            for shift in (1, 3, 2):
                start((0, 0), (shift, 0))
                if shift != 2:
                    start((0, 0), (0, shift))

        def first(*shifts):
            for shift in shifts:
                received((shift, 0))
                start((shift, 0), (0, 1))
                start((shift, 0), (0, 3))

        def second(*shifts):
            for shift in shifts:
                for came, to, half in ((3, 1, 0), (1, 3, 1)):
                    received((shift, came))
                    start((shift, came), (0, to), half)

        def last():
            for shift in (0, 1, 3, 2):
                for half in range(2):
                    received((shift, 2), half)

        def sent():
            for i, args in enumerate(sends):
                copy(i, *args).wait_send()

        return own, first, second, last, sent

    g_start, g_relay, g_received, g_sent = across_head(
        gfull, g_ss, g_rs, lambda buf, block, half: buf.at[block, :, pl.ds(half * (width // 2), width // 2)])
    h_start, h_relay, h_received, h_sent = across_head(
        gcol, h_ss, h_rs, lambda buf, block, half: (
            buf.at[block, pl.ds(half * (n_chip // 2), n_chip // 2)] if n_chip > 1
            else buf.at[block, :, :, pl.ds(half * 128, 128)]))
    t_own, t_first, t_second, t_last, t_sent = across_plane(tall, t_ss, t_rs)
    m_own, m_first, m_second, m_last, m_sent = across_plane(mall, m_ss, m_rs)

    def pair_copy(i, src, dst):
        return pltpu.make_async_remote_copy(
            src_ref=src, dst_ref=dst, send_sem=p_ss.at[i], recv_sem=p_rs.at[i],
            device_id=(partner, z), device_id_type=MESH)

    def to_chips(src_of, dst, ss, rs):
        def copy(i):
            return pltpu.make_async_remote_copy(
                src_ref=src_of(peer(i)), dst_ref=dst, send_sem=ss.at[i], recv_sem=rs.at[i],
                device_id=(peer(i) * 2 + core, z), device_id_type=MESH)
        return copy

    chip_width = width // n_chip
    e_copy = to_chips(lambda to: gfull.at[z, :, pl.ds(pl.multiple_of(to * chip_width, 128), chip_width)],
                      gcol.at[z, chip], e_ss, e_rs)
    l_copy = to_chips(lambda to: lsend.at[to], lslice.at[chip], l_ss, l_rs)
    a_copy = to_chips(lambda to: asend.at[to], aslice.at[chip], a_ss, a_rs)

    def to_plane(src, dst, ss, rs):
        def copy(i):
            to = lax.rem(c + i, n_ctx)
            return pltpu.make_async_remote_copy(
                src_ref=src.at[lax.div(to, 2)], dst_ref=dst.at[core, chip],
                send_sem=ss.at[i], recv_sem=rs.at[i], device_id=(to, z), device_id_type=MESH)
        return copy

    s_copy = to_plane(sret_out, sret_in, s_ss, s_rs)
    r_copy = to_plane(aret_out, aret_in, r_ss, r_rs)

    def o_copy(i):
        to, of, half = ((1, 1, None), (-1, -1, None), (1, 3, None), (-1, -3, None), (2, 4, 0), (-2, 4, 1),
                        (2, 2, None), (-2, -2, None))[i]
        src, dst = (lpart.at[zed(of)] if i < 6 else lsum.at[i - 6]), lrecv.at[i]
        if half is not None:
            part = pl.ds(half * (width // 2), width // 2)
            src, dst = lpart.at[zed(of), :, part], lrecv.at[i, :, part]
        return pltpu.make_async_remote_copy(
            src_ref=src, dst_ref=dst, send_sem=o_ss.at[i], recv_sem=o_rs.at[i],
            device_id=(c, zed(to)), device_id_type=MESH)

    def start_all(copy, n):
        def body(i, carry):
            copy(i).start()
            return carry
        lax.fori_loop(1, n, body, 0)

    def recv_all(copy, n):
        def body(i, carry):
            copy(i).wait_recv()
            return carry
        lax.fori_loop(1, n, body, 0)

    def sent_all(copy, n):
        def body(i, carry):
            copy(i).wait_send()
            return carry
        lax.fori_loop(1, n, body, 0)

    for load in loads[1:6]:
        load.wait()
    q = q_ref[...].astype(f32)
    k = k_ref[...].astype(f32)
    q_inv = 1.0 / jnp.sqrt(rowsum(q * q) + 1e-6)
    k_inv = 1.0 / jnp.sqrt(rowsum(k * k) + 1e-6)
    qn = q * q_inv
    kn = k * k_inv
    ks, qs = split(kn), split(qn)
    dots = mm(rows(ks, qs), ks, 1, 1)
    kk, qk = dots[:tok], dots[tok:]
    ii = lax.broadcasted_iota(jnp.int32, (tok, tok), 0)
    jj = lax.broadcasted_iota(jnp.int32, (tok, tok), 1)
    first = c * tok
    seg_i = jnp.zeros((tok, tok), f32)
    seg_j = jnp.zeros((tok, tok), f32)
    seg_all = jnp.zeros((1, 1), f32)
    for d in range(n_docs):
        at = docs_ref[d] - first
        seg_i = seg_i + jnp.where((ii >= at) & (at >= 0), 1.0, 0.0)
        seg_j = seg_j + jnp.where((jj >= at) & (at >= 0), 1.0, 0.0)
    seg_all = seg_i[tok - 1:, :]
    same = jnp.where(seg_i == seg_j, 1.0, 0.0)
    low = jnp.where(ii >= jj, same, 0.0)
    strict = jnp.where(ii > jj, same, 0.0)
    eye = jnp.where(ii == jj, 1.0, 0.0)
    at_start = jnp.where(seg_i[:, :1] == 0.0, 1.0, 0.0)
    at_end = jnp.where(seg_i[:, :1] == seg_all[:, :1], 1.0, 0.0)
    no_reset = jnp.where(seg_all[:, :1] == 0.0, 1.0, 0.0)

    upto = jnp.where(ii <= jj, 1.0, 0.0)
    cum_rows = lax.dot_general(decay_ref[...], upto, (((1,), (0,)), ((), ())),
                               precision=lax.Precision.HIGHEST, preferred_element_type=f32)

    def column(row):
        return rowsum(jnp.where(ii == jj, row, 0.0))

    info = []
    for h in range(2):
        cr = cum_rows[h:h + 1]
        cc = column(cr)
        b = column(rate_ref[h:h + 1, :])
        last = cr[:, tok - 1:]
        info.append(dict(
            b=b,
            ratio=jnp.exp(jnp.where(low > 0.0, cc - cr, 0.0)) * low,
            f=jnp.exp(cc) * at_start,
            e=jnp.exp(last - cc) * at_end,
            w=jnp.exp(last) * no_reset,
        ))

    def same_block(size):
        shift = size.bit_length() - 1
        return lax.shift_right_logical(ii, shift) == lax.shift_right_logical(jj, shift)

    for h in range(2):
        t = info[h]
        t["kr"] = kk * t["ratio"] * strict
        t["n"] = t["b"] * t["kr"]
    for h in range(2):
        t = info[h]
        x = jnp.where(same_block(16), -t["n"], 0.0)
        xs = split(x)
        x2 = mm(xs, xs)
        x2s = split(x2)
        x4 = mm(x2s, x2s)
        x4s = split(x4)
        x8s = split(mm(x4s, x4s))
        m = eye + x
        m = m + mm(m, x2s)
        m = m + mm(m, x4s)
        m = m + mm(m, x8s)
        t["m"] = m
    for size in (16, 32, 64):
        for h in range(2):
            t = info[h]
            off = jnp.where(same_block(2 * size) & ~same_block(size), t["n"], 0.0)
            ms = split(t["m"])
            t["m"] = t["m"] - mm(ms, mm(off, ms))
    loads[6].wait()
    v_all = v_ref[...].astype(f32)
    for h in range(2):
        t = info[h]
        v = v_all[:, h * dim:(h + 1) * dim]
        t["v"] = v
        t["ms"] = split(t["m"])
        uw = mm(t["ms"], cols(t["b"] * v, (t["b"] * t["f"]) * kn))
        uws = split(uw)
        t["u"], t["wks"] = uw[:, :dim], (uws[0][:, dim:], uws[1][:, dim:])
        ek = t["e"] * kn
        t["eks"] = split(ek)
        lt = mm(uws, t["eks"], 0, 0)
        tl_own[h, 0] = t["w"] * eye - lt[dim:]
        tl_own[h, 1] = lt[:dim]
        t["uws"] = uws

    tl_copy = pair_copy(0, tl_own, tl_oth)
    pl.semaphore_wait(barrier, n_head + n_ctx - 2)
    fence(lambda: pair_copy(0, tl_own, tl_oth).start())
    loads[0].wait()
    if n_head > 1:
        fence(lambda: g_start(0, 1, 2, 3))
    start_all(e_copy, n_chip)
    gcol[z, chip] = gfull[z, :, pl.ds(pl.multiple_of(chip * chip_width, 128), chip_width)]

    for h in range(2):
        t = info[h]
        p = qk * t["ratio"]
        t["p_mat"] = p
        t["ps"] = split(p)
        ow = mm(t["ps"], t["uws"])
        t["o"] = ow[:, :dim]
        t["qt"] = t["f"] * qn - ow[:, dim:]
        t["qts"] = split(t["qt"])
    tl_copy.wait_recv()
    is_first = core == 0

    def ordered(own, other):
        return jnp.where(is_first, own, other), jnp.where(is_first, other, own)

    t0, t1 = ordered(tl_own[core, 0], tl_oth[core, 0])
    l0, l1 = ordered(tl_own[core, 1], tl_oth[core, 1])
    pair_t = mm(rows(t0, l0), t1)
    tall[chip] = pair_t[:dim]
    lsend[...] = (pair_t[dim:] + l1).reshape(n_chip, slice_rows, dim)
    if side > 1:
        fence(t_own)
    start_all(l_copy, n_chip)
    lslice[chip] = lsend[chip]

    if side > 1:
        @fence
        def _():
            t_first(1, 3)
            t_second(0)
            t_first(2)
    if n_head > 1:
        fence(g_relay)
    recv_all(e_copy, n_chip)
    if n_head > 1:
        fence(lambda: h_start(0, 1, 2, 3))
    if side > 1:
        @fence
        def _():
            t_second(1, 3)
            t_second(2)
            t_last()
    recv_all(l_copy, n_chip)
    state = jnp.zeros((slice_rows, dim), f32)
    for i in range(n_chip):
        sret_out[i] = state
        if i < n_chip - 1:
            state = mm(state, tall[i]) + lslice[i]
    start_all(s_copy, n_ctx)
    sret_in[core, chip] = sret_out[chip]

    if n_head > 1:
        g_received(1, -1, 3, -3, 4)
    loads[7].wait()
    full_grad = gfull[...].reshape(tok, width)
    weight = w_ref[...]
    d_core = lax.dot_general(full_grad, weight, (((1,), (1,)), ((), ())), preferred_element_type=f32)
    for h in range(2):
        t = info[h]
        t["do"] = d_core[:, h * dim:(h + 1) * dim]
        t["dos"] = split(t["do"])
        a_own[h] = mm(t["dos"], t["qts"], 0, 0)
    ap_copy = pair_copy(1, a_own, a_oth)
    fence(lambda: pair_copy(1, a_own, a_oth).start())

    for h in range(2):
        t = info[h]
        t["pd"] = mm(t["ps"], t["dos"], 0, 0)
    ap_copy.wait_recv()
    a0, a1 = ordered(a_own[core], a_oth[core])
    asend[...] = (mm(a1, t0, 1, 1) + a0).reshape(n_chip, slice_rows, dim)
    start_all(a_copy, n_chip)
    aslice[chip] = asend[chip]
    if n_head > 1:
        fence(h_relay)

    recv_all(s_copy, n_ctx)
    mixed = []
    for h in range(2):
        t = info[h]
        state = sret_in[h].reshape(dim, dim)
        t["s"] = jnp.where(is_first, state, mm(state, tl_oth[h, 0]) + tl_oth[h, 1])
        t["ss"] = split(t["s"])
        both = mm(rows(t["qts"], t["wks"]), t["ss"], 1, 1)
        mixed.append((t["o"] + both[:tok]).astype(bf16))
        t["p"] = t["u"] - both[tok:]
    mixed = jnp.concatenate(mixed, axis=1)
    mall[chip] = mixed
    if side > 1:
        fence(m_own)
    partial = lax.dot_general(mixed, weight, (((1,), (0,)), ((), ())), preferred_element_type=f32)
    partial = partial.reshape(lpart.shape)
    lpart[...] = partial.astype(bf16)
    lfull[...] = partial
    if n_head > 1:
        @fence
        def _():
            for i in (4, 5, 2, 3, 0, 1):
                o_copy(i).start()

    if side > 1:
        @fence
        def _():
            m_first(1, 3)
            m_second(0)
    for h in range(2):
        t = info[h]
        t["pps"] = split(t["p"])
        t["xp"] = mm(t["dos"], t["pps"], 1, 1) * t["ratio"]
        t["d_o_s"] = mm(t["dos"], t["ss"])
    recv_all(a_copy, n_chip)
    adjoint = jnp.zeros((slice_rows, dim), f32)
    for j in reversed(range(n_chip)):
        aret_out[j] = adjoint
        if j > 0:
            adjoint = mm(adjoint, tall[j], 1, 1) + aslice[j]
    start_all(r_copy, n_ctx)
    aret_in[core, chip] = aret_out[chip]
    if n_head > 1:
        for i in range(2, 6):
            o_copy(i).wait_recv()
        mid = width // 2
        for i in range(2):
            on = lfull[zed(2 - 4 * i)] + lrecv[2 + i].astype(f32)
            more = lrecv[4 + i, :, i * mid:(i + 1) * mid].astype(f32)
            lsum[i, :, i * mid:(i + 1) * mid] = (on[:, i * mid:(i + 1) * mid] + more).astype(bf16)
            lsum[i, :, (1 - i) * mid:(2 - i) * mid] = on[:, (1 - i) * mid:(2 - i) * mid].astype(bf16)

        @fence
        def _():
            o_copy(6).start()
            o_copy(7).start()
    if side > 1:
        @fence
        def _():
            m_first(2)
            m_second(1, 3)
    if n_head > 1:
        h_received(1, -1, 3, -3, 4)
    for j in range(n_chip):
        gturn[j] = gcol[:, j].reshape(tok, chip_width).T
    if side > 1:
        fence(lambda: m_second(2))
    recv_all(r_copy, n_ctx)
    for h in range(2):
        t = info[h]
        adjoint = aret_in[h].reshape(dim, dim)
        t["g"] = jnp.where(is_first, mm(adjoint, tl_oth[h, 0], 1, 1) + a_oth[h], adjoint)
        t["gs"] = split(t["g"])

    dqk = jnp.zeros((tok, tok), f32)
    dkk = jnp.zeros((tok, tok), f32)
    dq = jnp.zeros((tok, dim), f32)
    dk = jnp.zeros((tok, dim), f32)
    before = jnp.where(ii < jj, 1.0, 0.0).astype(bf16)
    for h in range(2):
        t = info[h]
        b, f, e = t["b"], t["f"], t["e"]
        pps = t["pps"]
        pg = mm(pps, t["gs"])
        dp = t["pd"] + mm(t["eks"], t["gs"], 1, 1)
        dr = mm(t["ms"], dp, 0, 0)
        drs = split(dr)
        dn = -mm(drs, pps, 1, 1)
        d_o_s, d_r_s = t["d_o_s"], mm(drs, t["ss"])
        xp = t["xp"]
        xr = dn * t["kr"]
        xn = dn * (b * t["ratio"] * strict)
        dqk = dqk + xp
        dkk = dkk + xn
        x = xp * qk + b * xr
        alpha = rowsum(qn * d_o_s)
        beta = rowsum(kn * d_r_s)
        db = rowsum(dr * t["v"]) - f * beta + rowsum(xr)
        gv_ref[:, h * dim:(h + 1) * dim] = b * dr
        grate_ref[h:h + 1, :] = jnp.sum(jnp.where(ii == jj, db, 0.0), axis=0, keepdims=True)
        fdf = f * (alpha - b * beta)
        ede = e * rowsum(kn * pg)
        y = mm(x, before)
        terms = jnp.where(ii >= jj, y + fdf, ede)
        wdw = t["w"] * jnp.sum(rowsum(t["s"] * t["g"]), axis=0, keepdims=True)
        gdecay_ref[h:h + 1, :] = jnp.sum(terms, axis=0, keepdims=True) + wdw
        dq = dq + f * d_o_s
        dk = dk + e * pg - (b * f) * d_r_s
    ds = rows(dqk, dkk)
    direct = mm(ds, ks)
    turned = mm(ds, rows(qs, ks), 0, 0)
    dq = dq + direct[:tok]
    dk = dk + direct[tok:] + turned
    gq_ref[...] = q_inv * (dq - qn * rowsum(qn * dq))
    gk_ref[...] = k_inv * (dk - kn * rowsum(kn * dk))

    if side > 1:
        m_last()
    total = jnp.zeros((chip_width, 2 * dim), f32)
    for j in range(n_chip):
        total = total + lax.dot_general(gturn[j], mall[j], (((1,), (0,)), ((), ())), preferred_element_type=f32)
    half = chip_width // 2
    wx_own[0] = total[:half]
    wx_own[1] = total[half:]
    fence(lambda: pair_copy(2, wx_own.at[1 - core], wx_oth).start())
    result = lfull[z]
    if n_head > 1:
        for i in (0, 1, 6, 7):
            o_copy(i).wait_recv()
            result = result + lrecv[i].astype(f32)
    out_ref[...] = result
    wx_copy = pair_copy(2, wx_own.at[1 - core], wx_oth)
    wx_copy.wait_recv()
    wg_ref[...] = wx_own[core] + wx_oth[...]

    tl_copy.wait_send()
    ap_copy.wait_send()
    wx_copy.wait_send()
    if n_head > 1:
        g_sent()
        h_sent()
    t_sent()
    m_sent()
    sent_all(e_copy, n_chip)
    sent_all(l_copy, n_chip)
    sent_all(a_copy, n_chip)
    sent_all(s_copy, n_ctx)
    sent_all(r_copy, n_ctx)
    if n_head > 1:
        for i in range(8):
            o_copy(i).wait_send()


def per_device(n_ctx, n_head, queries, key_vectors, value_rows, write_rate, log_decay, doc_offsets, out_weight, grad_out):
    n_chip = n_ctx // 2
    tok, dim = queries.shape
    width = grad_out.shape[1]
    share = grad_out.shape[0]
    sl = dim // n_chip
    wrows = width // n_ctx
    vmem = pl.BlockSpec(memory_space=pltpu.VMEM)
    hbm = pl.BlockSpec(memory_space=pltpu.HBM)
    dma = pltpu.SemaphoreType.DMA
    scratch = [
        pltpu.SMEM(doc_offsets.shape, jnp.int32),
        pltpu.VMEM((tok, dim), bf16), pltpu.VMEM((tok, dim), bf16), pltpu.VMEM((tok, 2 * dim), bf16),
        pltpu.VMEM((2, tok), f32), pltpu.VMEM((2, tok), f32), pltpu.VMEM((2 * dim, width), bf16),
        pltpu.VMEM((n_head, share, width), bf16),
        pltpu.VMEM((n_head, n_chip, share, width // n_chip), bf16),
        pltpu.VMEM((n_chip, width // n_chip, tok), bf16),
        pltpu.VMEM((2, 2, dim, dim), f32), pltpu.VMEM((2, 2, dim, dim), f32),
        pltpu.VMEM((2, dim, dim), f32), pltpu.VMEM((2, dim, dim), f32),
        pltpu.VMEM((n_chip, dim, dim), f32), pltpu.VMEM((n_chip, tok, 2 * dim), bf16),
        pltpu.VMEM((n_chip, sl, dim), f32), pltpu.VMEM((n_chip, sl, dim), f32),
        pltpu.VMEM((n_chip, sl, dim), f32), pltpu.VMEM((n_chip, sl, dim), f32),
        pltpu.VMEM((n_chip, sl, dim), f32), pltpu.VMEM((2, n_chip, sl, dim), f32),
        pltpu.VMEM((n_chip, sl, dim), f32), pltpu.VMEM((2, n_chip, sl, dim), f32),
        pltpu.VMEM((n_head, share, width), bf16), pltpu.VMEM((n_head, share, width), f32),
        pltpu.VMEM((2, share, width), bf16), pltpu.VMEM((8, share, width), bf16),
        pltpu.VMEM((2, wrows, 2 * dim), f32), pltpu.VMEM((wrows, 2 * dim), f32),
        dma((8,)),
        dma((8,)), dma((n_head, 2)), dma((n_chip,)), dma((n_chip,)), dma((8,)), dma((n_head, 2)), dma((3,)), dma((3,)),
        dma((19,)), dma((n_chip, 2)), dma((19,)), dma((n_chip, 2)),
        dma((n_chip,)), dma((n_chip,)), dma((n_chip,)), dma((n_chip,)),
        dma((n_ctx,)), dma((n_ctx,)), dma((n_ctx,)), dma((n_ctx,)), dma((8,)), dma((8,)),
    ]
    shapes = (
        jax.ShapeDtypeStruct((share, width), f32),
        jax.ShapeDtypeStruct((tok, dim), f32),
        jax.ShapeDtypeStruct((tok, dim), f32),
        jax.ShapeDtypeStruct((tok, 2 * dim), f32),
        jax.ShapeDtypeStruct((2, tok), f32),
        jax.ShapeDtypeStruct((2, tok), f32),
        jax.ShapeDtypeStruct((wrows, 2 * dim), f32),
    )
    results = pl.pallas_call(
        functools.partial(kernel, n_ctx, n_head),
        out_shape=shapes,
        in_specs=[hbm] * 8,
        out_specs=(vmem,) * 7,
        scratch_shapes=scratch,
        compiler_params=pltpu.CompilerParams(collective_id=0, has_side_effects=True,
                                             vmem_limit_bytes=60 * 1024 * 1024),
        name="layer",
    )(doc_offsets, queries, key_vectors, value_rows, write_rate, log_decay, out_weight, grad_out)
    return pl.pallas_call(
        emit,
        out_shape=shapes,
        in_specs=[vmem] * 7,
        out_specs=(hbm,) * 7,
        scratch_shapes=[dma((7,))],
        name="emit",
    )(*results)


def emit(*refs):
    copies = [pltpu.make_async_copy(refs[i], refs[7 + i], refs[14].at[i]) for i in range(7)]
    for copy in copies:
        copy.start()
    for copy in copies:
        copy.wait()


def solution(mesh):
    n_ctx, n_head = mesh.shape["ctx"], mesh.shape["head"]
    return jax.shard_map(
        functools.partial(per_device, n_ctx, n_head),
        mesh=mesh,
        in_specs=(
            P("ctx", "head"), P("ctx", "head"), P("ctx", "head"), P("head", "ctx"), P("head", "ctx"),
            P(), P("head", None), P(("ctx", "head"), None),
        ),
        out_specs=(
            P(("ctx", "head"), None), P("ctx", "head"), P("ctx", "head"), P("ctx", "head"),
            P("head", "ctx"), P("head", "ctx"), P("ctx", "head"),
        ),
        check_vma=False,
    )
```

```python
import functools

import jax
import jax.numpy as jnp
from jax import lax
from jax.experimental import pallas as pl
from jax.experimental.pallas import tpu as pltpu
from jax.sharding import PartitionSpec as P

f32 = jnp.float32
bf16 = jnp.bfloat16
MESH = pl.DeviceIdType.MESH


def split(x):
    hi = x.astype(bf16)
    return hi, (x - hi.astype(f32)).astype(bf16)


def mm(a, b, ca=1, cb=0):
    if not isinstance(a, tuple):
        a = (a,) if a.dtype == bf16 else split(a)
    if not isinstance(b, tuple):
        b = (b,) if b.dtype == bf16 else split(b)
    left, right = [a[0]], [b[0]]
    if len(a) == 2:
        left.append(a[1])
        right.append(b[0])
    if len(b) == 2:
        left.append(a[0])
        right.append(b[1])
    left = jnp.concatenate(left, axis=ca) if len(left) > 1 else left[0]
    right = jnp.concatenate(right, axis=cb) if len(right) > 1 else right[0]
    return lax.dot_general(left, right, (((ca,), (cb,)), ((), ())), preferred_element_type=f32)


def rows(*parts):
    parts = [p if isinstance(p, tuple) else split(p) for p in parts]
    return tuple(jnp.concatenate([p[i] for p in parts], axis=0) for i in range(2))


def cols(*parts):
    parts = [p if isinstance(p, tuple) else split(p) for p in parts]
    return tuple(jnp.concatenate([p[i] for p in parts], axis=1) for i in range(2))


def rowsum(x):
    return jnp.sum(x, axis=1, keepdims=True)


def kernel(
    n_ctx, n_head,
    docs_hbm, q_hbm, k_hbm, v_hbm, rate_hbm, decay_hbm, w_hbm, g_hbm,
    out_ref, gq_ref, gk_ref, gv_ref, grate_ref, gdecay_ref, wg_ref,
    docs_ref, q_ref, k_ref, v_ref, rate_ref, decay_ref, w_ref,
    gfull, gcol, gturn, tl_own, tl_oth, a_own, a_oth, tall, mall, lslice, aslice, lsend, asend,
    sret_out, sret_in, aret_out, aret_in, lpart, lfull, lsum, lrecv, wfull, wsend, wrecv,
    i_s, g_ss, g_rs, e_ss, e_rs, h_ss, h_rs, p_ss, p_rs, t_ss, t_rs, m_ss, m_rs, n_ss, n_rs,
    l_ss, l_rs, a_ss, a_rs, s_ss, s_rs, r_ss, r_rs, o_ss, o_rs,
):
    n_chip = n_ctx // 2
    side = 4 if n_chip == 16 else 1
    c = lax.axis_index("ctx")
    z = lax.axis_index("head")
    chip = lax.div(c, 2)
    core = lax.rem(c, 2)
    partner = c + 1 - 2 * core
    row = lax.div(chip, side)
    col = lax.rem(chip, side)
    tok = q_ref.shape[0]
    dim = 128
    width = w_ref.shape[1]
    n_docs = docs_ref.shape[0] - 1
    slice_rows = dim // n_chip

    loads = [
        pltpu.make_async_copy(src, dst, i_s.at[i])
        for i, (src, dst) in enumerate((
            (g_hbm, gfull.at[z]), (q_hbm, q_ref), (k_hbm, k_ref), (docs_hbm, docs_ref),
            (rate_hbm, rate_ref), (decay_hbm, decay_ref), (v_hbm, v_ref), (w_hbm, w_ref),
        ))
    ]
    for load in loads:
        load.start()

    barrier = pltpu.get_barrier_semaphore()

    def greet_head(i, carry):
        pl.semaphore_signal(barrier, inc=1, device_id=(c, lax.rem(z + i, n_head)), device_id_type=MESH)
        return carry

    def greet_ctx(i, carry):
        pl.semaphore_signal(barrier, inc=1, device_id=(lax.rem(c + i, n_ctx), z), device_id_type=MESH)
        return carry

    lax.fori_loop(1, n_head, greet_head, 0)
    lax.fori_loop(1, n_ctx, greet_ctx, 0)

    def zed(shift):
        return lax.rem(z + shift + n_head, n_head)

    def peer(i):
        return lax.rem(chip + i, n_chip)

    def fence(body):
        pl.when(c >= 0)(body)

    def across_head(buf, ss, rs, part):
        sends = [(0, 2, None), (0, -2, None), (0, 1, None), (0, -1, None),
                 (-2, 1, None), (-2, 2, 0), (2, -1, None), (2, -2, 1)]

        def copy(i, block, shift, half):
            ref = buf.at[block] if half is None else part(buf, block, half)
            return pltpu.make_async_remote_copy(
                src_ref=ref, dst_ref=ref, send_sem=ss.at[i], recv_sem=rs.at[block, half or 0],
                device_id=(c, zed(shift)), device_id_type=MESH)

        def start(*which):
            for i in which:
                origin, shift, half = sends[i]
                copy(i, zed(origin), shift, half).start()

        def received(*origins):
            for origin in origins:
                for half in ((0, 1) if origin == 4 else (None,)):
                    copy(0, zed(origin), 1, half).wait_recv()

        def relay():
            received(-2)
            start(4, 5)
            received(2)
            start(6, 7)

        def sent():
            for i, (origin, shift, half) in enumerate(sends):
                copy(i, zed(origin), shift, half).wait_send()

        return start, relay, received, sent

    def chip_at(first_shift, second_shift):
        to_col = lax.rem(col + (1 - core) * first_shift + core * second_shift, side)
        to_row = lax.rem(row + core * first_shift + (1 - core) * second_shift, side)
        return to_row * side + to_col

    def across_plane(buf, ss, rs):
        rows_of = buf.shape[1] // 2
        sends = []

        def copy(i, origin, to, half):
            block = chip_at(*origin)
            ref = buf.at[block] if half is None else buf.at[block, pl.ds(half * rows_of, rows_of)]
            return pltpu.make_async_remote_copy(
                src_ref=ref, dst_ref=ref, send_sem=ss.at[i], recv_sem=rs.at[block, half or 0],
                device_id=(chip_at(*to) * 2 + core, z), device_id_type=MESH)

        def start(origin, to, half=None):
            sends.append((origin, to, half))
            copy(len(sends) - 1, origin, to, half).start()

        def received(origin, half=None):
            copy(0, origin, (0, 1), half).wait_recv()

        def own():
            for shift in (1, 3, 2):
                start((0, 0), (shift, 0))
                if shift != 2:
                    start((0, 0), (0, shift))

        def first(*shifts):
            for shift in shifts:
                received((shift, 0))
                start((shift, 0), (0, 1))
                start((shift, 0), (0, 3))

        def second(*shifts):
            for shift in shifts:
                for came, to, half in ((3, 1, 0), (1, 3, 1)):
                    received((shift, came))
                    start((shift, came), (0, to), half)

        def last():
            for shift in (0, 1, 3, 2):
                for half in range(2):
                    received((shift, 2), half)

        def sent():
            for i, args in enumerate(sends):
                copy(i, *args).wait_send()

        return own, first, second, last, sent

    g_start, g_relay, g_received, g_sent = across_head(
        gfull, g_ss, g_rs, lambda buf, block, half: buf.at[block, :, pl.ds(half * (width // 2), width // 2)])
    h_start, h_relay, h_received, h_sent = across_head(
        gcol, h_ss, h_rs, lambda buf, block, half: (
            buf.at[block, pl.ds(half * (side // 2), side // 2)] if n_chip > 1
            else buf.at[block, :, :, :, pl.ds(half * 128, 128)]))
    t_own, t_first, t_second, t_last, t_sent = across_plane(tall, t_ss, t_rs)

    def pair_copy(i, src, dst):
        return pltpu.make_async_remote_copy(
            src_ref=src, dst_ref=dst, send_sem=p_ss.at[i], recv_sem=p_rs.at[i],
            device_id=(partner, z), device_id_type=MESH)

    def to_chips(src_of, dst, ss, rs):
        def copy(i):
            return pltpu.make_async_remote_copy(
                src_ref=src_of(peer(i)), dst_ref=dst, send_sem=ss.at[i], recv_sem=rs.at[i],
                device_id=(peer(i) * 2 + core, z), device_id_type=MESH)
        return copy

    chip_width = width // n_chip
    first_at = (1 - core) * col + core * row
    second_at = (1 - core) * row + core * col

    def columns(first, second):
        of = (1 - core) * (second * side + first) + core * (first * side + second)
        return pl.ds(pl.multiple_of(of * chip_width, 128), chip_width)

    def e_copy(i):
        shift, second = lax.div(i, side), lax.rem(i, side)
        return pltpu.make_async_remote_copy(
            src_ref=gfull.at[z, :, columns(lax.rem(first_at + shift, side), second)],
            dst_ref=gcol.at[z, first_at, second], send_sem=e_ss.at[i], recv_sem=e_rs.at[i],
            device_id=(chip_at(shift, 0) * 2 + core, z), device_id_type=MESH)

    def m_copy(shift):
        return pltpu.make_async_remote_copy(
            src_ref=mall.at[first_at], dst_ref=mall.at[first_at], send_sem=m_ss.at[shift], recv_sem=m_rs.at[shift],
            device_id=(chip_at(shift, 0) * 2 + core, z), device_id_type=MESH)

    def n_copy(shift, to_core):
        return pltpu.make_async_remote_copy(
            src_ref=wsend.at[lax.rem(second_at + shift, side), to_core], dst_ref=wrecv.at[core, second_at],
            send_sem=n_ss.at[shift, to_core], recv_sem=n_rs.at[core, second_at],
            device_id=(chip_at(0, shift) * 2 + to_core, z), device_id_type=MESH)

    def n_received(of_core, at):
        pltpu.make_async_remote_copy(
            src_ref=wsend.at[0, 0], dst_ref=wrecv.at[of_core, at], send_sem=n_ss.at[0, 0],
            recv_sem=n_rs.at[of_core, at], device_id=(partner, z), device_id_type=MESH).wait_recv()

    l_copy = to_chips(lambda to: lsend.at[to], lslice.at[chip], l_ss, l_rs)
    a_copy = to_chips(lambda to: asend.at[to], aslice.at[chip], a_ss, a_rs)

    s_copy = to_chips(lambda to: sret_out.at[to], sret_in.at[core, chip], s_ss, s_rs)
    r_copy = to_chips(lambda to: aret_out.at[to], aret_in.at[core, chip], r_ss, r_rs)

    def o_copy(i):
        to, of, half = ((1, 1, None), (-1, -1, None), (1, 3, None), (-1, -3, None), (2, 4, 0), (-2, 4, 1),
                        (2, 2, None), (-2, -2, None))[i]
        src, dst = (lpart.at[zed(of)] if i < 6 else lsum.at[i - 6]), lrecv.at[i]
        if half is not None:
            part = pl.ds(half * (width // 2), width // 2)
            src, dst = lpart.at[zed(of), :, part], lrecv.at[i, :, part]
        return pltpu.make_async_remote_copy(
            src_ref=src, dst_ref=dst, send_sem=o_ss.at[i], recv_sem=o_rs.at[i],
            device_id=(c, zed(to)), device_id_type=MESH)

    def start_all(copy, n, low=1):
        def body(i, carry):
            copy(i).start()
            return carry
        lax.fori_loop(low, n, body, 0)

    def recv_all(copy, n, low=1):
        def body(i, carry):
            copy(i).wait_recv()
            return carry
        lax.fori_loop(low, n, body, 0)

    def sent_all(copy, n, low=1):
        def body(i, carry):
            copy(i).wait_send()
            return carry
        lax.fori_loop(low, n, body, 0)

    for load in loads[1:6]:
        load.wait()
    q = q_ref[...].astype(f32)
    k = k_ref[...].astype(f32)
    q_inv = 1.0 / jnp.sqrt(rowsum(q * q) + 1e-6)
    k_inv = 1.0 / jnp.sqrt(rowsum(k * k) + 1e-6)
    qn = q * q_inv
    kn = k * k_inv
    ks, qs = split(kn), split(qn)
    dots = mm(rows(ks, qs), ks, 1, 1)
    kk, qk = dots[:tok], dots[tok:]
    ii = lax.broadcasted_iota(jnp.int32, (tok, tok), 0)
    jj = lax.broadcasted_iota(jnp.int32, (tok, tok), 1)
    first = c * tok
    seg_i = jnp.zeros((tok, tok), f32)
    seg_j = jnp.zeros((tok, tok), f32)
    seg_all = jnp.zeros((1, 1), f32)
    for d in range(n_docs):
        at = docs_ref[d] - first
        seg_i = seg_i + jnp.where((ii >= at) & (at >= 0), 1.0, 0.0)
        seg_j = seg_j + jnp.where((jj >= at) & (at >= 0), 1.0, 0.0)
    seg_all = seg_i[tok - 1:, :]
    same = jnp.where(seg_i == seg_j, 1.0, 0.0)
    low = jnp.where(ii >= jj, same, 0.0)
    strict = jnp.where(ii > jj, same, 0.0)
    eye = jnp.where(ii == jj, 1.0, 0.0)
    at_start = jnp.where(seg_i[:, :1] == 0.0, 1.0, 0.0)
    at_end = jnp.where(seg_i[:, :1] == seg_all[:, :1], 1.0, 0.0)
    no_reset = jnp.where(seg_all[:, :1] == 0.0, 1.0, 0.0)

    upto = jnp.where(ii <= jj, 1.0, 0.0)
    cum_rows = lax.dot_general(decay_ref[...], upto, (((1,), (0,)), ((), ())),
                               precision=lax.Precision.HIGHEST, preferred_element_type=f32)

    def column(row):
        return rowsum(jnp.where(ii == jj, row, 0.0))

    info = []
    for h in range(2):
        cr = cum_rows[h:h + 1]
        cc = column(cr)
        b = column(rate_ref[h:h + 1, :])
        last = cr[:, tok - 1:]
        info.append(dict(
            b=b,
            ratio=jnp.exp(jnp.where(low > 0.0, cc - cr, 0.0)) * low,
            f=jnp.exp(cc) * at_start,
            e=jnp.exp(last - cc) * at_end,
            w=jnp.exp(last) * no_reset,
        ))

    def same_block(size):
        shift = size.bit_length() - 1
        return lax.shift_right_logical(ii, shift) == lax.shift_right_logical(jj, shift)

    for h in range(2):
        t = info[h]
        t["kr"] = kk * t["ratio"] * strict
        t["n"] = t["b"] * t["kr"]
    for h in range(2):
        t = info[h]
        x = jnp.where(same_block(16), -t["n"], 0.0)
        xs = split(x)
        x2 = mm(xs, xs)
        x2s = split(x2)
        x4 = mm(x2s, x2s)
        x4s = split(x4)
        x8s = split(mm(x4s, x4s))
        m = eye + x
        m = m + mm(m, x2s)
        m = m + mm(m, x4s)
        m = m + mm(m, x8s)
        t["m"] = m
    for size in (16, 32, 64):
        for h in range(2):
            t = info[h]
            off = jnp.where(same_block(2 * size) & ~same_block(size), t["n"], 0.0)
            ms = split(t["m"])
            t["m"] = t["m"] - mm(ms, mm(off, ms))
    loads[6].wait()
    v_all = v_ref[...].astype(f32)
    for h in range(2):
        t = info[h]
        v = v_all[:, h * dim:(h + 1) * dim]
        t["v"] = v
        t["ms"] = split(t["m"])
        uw = mm(t["ms"], cols(t["b"] * v, (t["b"] * t["f"]) * kn))
        uws = split(uw)
        t["u"], t["wks"] = uw[:, :dim], (uws[0][:, dim:], uws[1][:, dim:])
        ek = t["e"] * kn
        t["eks"] = split(ek)
        lt = mm(uws, t["eks"], 0, 0)
        tl_own[h, 0] = t["w"] * eye - lt[dim:]
        tl_own[h, 1] = lt[:dim]
        t["uws"] = uws

    tl_copy = pair_copy(0, tl_own, tl_oth)
    pl.semaphore_wait(barrier, n_head + n_ctx - 2)
    fence(lambda: pair_copy(0, tl_own, tl_oth).start())
    loads[0].wait()
    if n_head > 1:
        fence(lambda: g_start(0, 1, 2, 3))
    start_all(e_copy, n_chip, side)
    for second in range(side):
        gcol[z, first_at, second] = gfull[z, :, columns(first_at, second)]

    for h in range(2):
        t = info[h]
        p = qk * t["ratio"]
        t["p_mat"] = p
        t["ps"] = split(p)
        ow = mm(t["ps"], t["uws"])
        t["o"] = ow[:, :dim]
        t["qt"] = t["f"] * qn - ow[:, dim:]
        t["qts"] = split(t["qt"])
    tl_copy.wait_recv()
    is_first = core == 0

    def ordered(own, other):
        return jnp.where(is_first, own, other), jnp.where(is_first, other, own)

    t0, t1 = ordered(tl_own[core, 0], tl_oth[core, 0])
    l0, l1 = ordered(tl_own[core, 1], tl_oth[core, 1])
    pair_t = mm(rows(t0, l0), t1)
    tall[chip] = pair_t[:dim]
    lsend[...] = (pair_t[dim:] + l1).reshape(n_chip, slice_rows, dim)
    if side > 1:
        fence(t_own)
    start_all(l_copy, n_chip)
    lslice[chip] = lsend[chip]

    for h in range(2):
        t = info[h]
        through = mm(t["qts"], rows(tl_oth[h, 0], tl_oth[h, 1]), 1, 1)
        t["qfs"] = split(jnp.where(is_first, t["qt"], through[:, :dim]))
        t["of"] = t["o"] + jnp.where(is_first, 0.0, through[:, dim:])

    if side > 1:
        @fence
        def _():
            t_first(1, 3)
            t_second(0)
            t_first(2)
    if n_head > 1:
        fence(g_relay)
    recv_all(e_copy, n_chip, side)
    if n_head > 1:
        fence(lambda: h_start(0, 1, 2, 3))
    if side > 1:
        @fence
        def _():
            t_second(1, 3)
            t_second(2)
            t_last()
    recv_all(l_copy, n_chip)
    state = jnp.zeros((slice_rows, dim), f32)
    for i in range(n_chip):
        sret_out[i] = state
        if i < n_chip - 1:
            state = mm(state, tall[i]) + lslice[i]
    start_all(s_copy, n_chip)
    sret_in[core, chip] = sret_out[chip]

    if n_head > 1:
        g_received(1, -1, 3, -3, 4)
    loads[7].wait()
    full_grad = gfull[...].reshape(tok, width)
    weight = w_ref[...]
    d_core = lax.dot_general(full_grad, weight, (((1,), (1,)), ((), ())), preferred_element_type=f32)
    for h in range(2):
        t = info[h]
        t["do"] = d_core[:, h * dim:(h + 1) * dim]
        t["dos"] = split(t["do"])
        a_own[h] = mm(t["dos"], t["qts"], 0, 0)
    ap_copy = pair_copy(1, a_own, a_oth)
    fence(lambda: pair_copy(1, a_own, a_oth).start())

    for h in range(2):
        t = info[h]
        t["pd"] = mm(t["ps"], t["dos"], 0, 0)
    ap_copy.wait_recv()
    a0, a1 = ordered(a_own[core], a_oth[core])
    asend[...] = (mm(a1, t0, 1, 1) + a0).reshape(n_chip, slice_rows, dim)
    start_all(a_copy, n_chip)
    aslice[chip] = asend[chip]
    if n_head > 1:
        fence(h_relay)

    tl_copy.wait_send()
    t_sent()
    sent_all(e_copy, n_chip, side)
    sent_all(l_copy, n_chip)
    recv_all(s_copy, n_chip)
    fence(lambda: pair_copy(2, sret_in.at[core], sret_in.at[core]).start())
    pair_copy(2, sret_in.at[core], sret_in.at[1 - core]).wait_recv()
    mixed = []
    for h in range(2):
        t = info[h]
        t["ps_in"] = split(sret_in[h].reshape(dim, dim))
        mixed.append((t["of"] + mm(t["qfs"], t["ps_in"], 1, 1)).astype(bf16))
    mixed = jnp.concatenate(mixed, axis=1)
    mall[first_at] = mixed
    if side > 1:
        @fence
        def _():
            for shift in (2, 1, 3):
                m_copy(shift).start()
    partial = lax.dot_general(mixed, weight, (((1,), (0,)), ((), ())), preferred_element_type=f32)
    partial = partial.reshape(lpart.shape)
    lpart[...] = partial.astype(bf16)
    if n_head > 1:
        @fence
        def _():
            for i in (4, 5, 2, 3, 0, 1):
                o_copy(i).start()
    lfull[...] = partial

    recv_all(a_copy, n_chip)
    adjoint = jnp.zeros((slice_rows, dim), f32)
    for j in reversed(range(n_chip)):
        aret_out[j] = adjoint
        if j > 0:
            adjoint = mm(adjoint, tall[j], 1, 1) + aslice[j]
    start_all(r_copy, n_chip)
    aret_in[core, chip] = aret_out[chip]
    if n_head > 1:
        h_received(1, -1, 3, -3, 4)
    for second in range(side):
        for first_of in range(side):
            gturn[second * chip_width:(second + 1) * chip_width, first_of * tok:(first_of + 1) * tok] = (
                gcol[:, first_of, second].reshape(tok, chip_width).T)
    if side > 1:
        for shift in (1, 3, 2):
            m_copy(shift).wait_recv()
    product = lax.dot_general(gturn[...], mall[...].reshape(side * tok, 2 * dim), (((1,), (0,)), ((), ())),
                              preferred_element_type=f32).reshape(wfull.shape)
    wsend[...] = product.astype(bf16)

    @fence
    def _():
        for shift in (2, 1, 3)[:side - 1]:
            for to_core in range(2):
                n_copy(shift, to_core).start()
        n_copy(0, 1 - core).start()
    wfull[...] = product

    if n_head > 1:
        for i in range(2, 6):
            o_copy(i).wait_recv()
        mid = width // 2
        for i in range(2):
            on = lfull[zed(2 - 4 * i)] + lrecv[2 + i].astype(f32)
            more = lrecv[4 + i, :, i * mid:(i + 1) * mid].astype(f32)
            lsum[i, :, i * mid:(i + 1) * mid] = (on[:, i * mid:(i + 1) * mid] + more).astype(bf16)
            lsum[i, :, (1 - i) * mid:(2 - i) * mid] = on[:, (1 - i) * mid:(2 - i) * mid].astype(bf16)

        @fence
        def _():
            o_copy(6).start()
            o_copy(7).start()
    dqk = jnp.zeros((tok, tok), f32)
    dq = jnp.zeros((tok, dim), f32)
    for h in range(2):
        t = info[h]
        state = sret_in[h].reshape(dim, dim)
        t["s"] = jnp.where(is_first, state, mm(t["ps_in"], tl_oth[h, 0]) + tl_oth[h, 1])
        t["ss"] = split(t["s"])
        t["p"] = t["u"] - mm(t["wks"], t["ss"], 1, 1)
        t["pps"] = split(t["p"])
        t["xp"] = mm(t["dos"], t["pps"], 1, 1) * t["ratio"]
        t["d_o_s"] = mm(t["dos"], t["ss"])
        turned = mm(t["ms"], cols(t["pd"], t["eks"]), 0, 0)
        t["dr0"], t["mes"] = turned[:, :dim], split(turned[:, dim:])
        dqk = dqk + t["xp"]
        dq = dq + t["f"] * t["d_o_s"]
    dqks = split(dqk)
    dq = dq + mm(dqks, ks)
    dk = mm(dqks, qs, 0, 0)
    gq_ref[...] = q_inv * (dq - qn * rowsum(qn * dq))
    sent_all(s_copy, n_chip)
    sent_all(a_copy, n_chip)
    ap_copy.wait_send()
    if n_head > 1:
        g_sent()
        h_sent()
    recv_all(r_copy, n_chip)
    fence(lambda: pair_copy(3, aret_in.at[core], aret_in.at[core]).start())
    pair_copy(3, aret_in.at[core], aret_in.at[1 - core]).wait_recv()
    for h in range(2):
        t = info[h]
        adjoint = aret_in[h].reshape(dim, dim)
        t["g"] = jnp.where(is_first, mm(adjoint, tl_oth[h, 0], 1, 1) + a_oth[h], adjoint)
        t["gs"] = split(t["g"])

    dkk = jnp.zeros((tok, tok), f32)
    before = jnp.where(ii < jj, 1.0, 0.0).astype(bf16)
    for h in range(2):
        t = info[h]
        b, f, e = t["b"], t["f"], t["e"]
        pps = t["pps"]
        pg = mm(pps, t["gs"])
        dr = t["dr0"] + mm(t["mes"], t["gs"], 1, 1)
        drs = split(dr)
        dn = -mm(drs, pps, 1, 1)
        d_o_s, d_r_s = t["d_o_s"], mm(drs, t["ss"])
        xp = t["xp"]
        xr = dn * t["kr"]
        xn = dn * (b * t["ratio"] * strict)
        dkk = dkk + xn
        x = xp * qk + b * xr
        alpha = rowsum(qn * d_o_s)
        beta = rowsum(kn * d_r_s)
        db = rowsum(dr * t["v"]) - f * beta + rowsum(xr)
        gv_ref[:, h * dim:(h + 1) * dim] = b * dr
        grate_ref[h:h + 1, :] = jnp.sum(jnp.where(ii == jj, db, 0.0), axis=0, keepdims=True)
        fdf = f * (alpha - b * beta)
        ede = e * rowsum(kn * pg)
        y = mm(x, before)
        terms = jnp.where(ii >= jj, y + fdf, ede)
        wdw = t["w"] * jnp.sum(rowsum(t["s"] * t["g"]), axis=0, keepdims=True)
        gdecay_ref[h:h + 1, :] = jnp.sum(terms, axis=0, keepdims=True) + wdw
        dk = dk + e * pg - (b * f) * d_r_s
    ds = split(dkk)
    dk = dk + mm(ds, ks) + mm(ds, ks, 0, 0)
    gk_ref[...] = k_inv * (dk - kn * rowsum(kn * dk))

    result = lfull[z]
    if n_head > 1:
        for i in (0, 1, 6, 7):
            o_copy(i).wait_recv()
            result = result + lrecv[i].astype(f32)
    out_ref[...] = result
    total = wfull[second_at, core]
    for shift in range(1, side):
        at = lax.rem(second_at + shift, side)
        n_received(core, at)
        total = total + wrecv[core, at].astype(f32)
    for at in range(side):
        n_received(1 - core, at)
        total = total + wrecv[1 - core, at].astype(f32)
    wg_ref[...] = total

    pair_copy(2, sret_in.at[core], sret_in.at[core]).wait_send()
    pair_copy(3, aret_in.at[core], aret_in.at[core]).wait_send()
    for shift in range(1, side):
        m_copy(shift).wait_send()
        for to_core in range(2):
            n_copy(shift, to_core).wait_send()
    n_copy(0, 1 - core).wait_send()
    sent_all(r_copy, n_chip)
    if n_head > 1:
        for i in range(8):
            o_copy(i).wait_send()


def per_device(n_ctx, n_head, queries, key_vectors, value_rows, write_rate, log_decay, doc_offsets, out_weight, grad_out):
    n_chip = n_ctx // 2
    side = 4 if n_chip == 16 else 1
    tok, dim = queries.shape
    width = grad_out.shape[1]
    share = grad_out.shape[0]
    sl = dim // n_chip
    wrows = width // n_ctx
    vmem = pl.BlockSpec(memory_space=pltpu.VMEM)
    hbm = pl.BlockSpec(memory_space=pltpu.HBM)
    dma = pltpu.SemaphoreType.DMA
    scratch = [
        pltpu.SMEM(doc_offsets.shape, jnp.int32),
        pltpu.VMEM((tok, dim), bf16), pltpu.VMEM((tok, dim), bf16), pltpu.VMEM((tok, 2 * dim), bf16),
        pltpu.VMEM((2, tok), f32), pltpu.VMEM((2, tok), f32), pltpu.VMEM((2 * dim, width), bf16),
        pltpu.VMEM((n_head, share, width), bf16),
        pltpu.VMEM((n_head, side, side, share, width // n_chip), bf16),
        pltpu.VMEM((side * (width // n_chip), side * tok), bf16),
        pltpu.VMEM((2, 2, dim, dim), f32), pltpu.VMEM((2, 2, dim, dim), f32),
        pltpu.VMEM((2, dim, dim), f32), pltpu.VMEM((2, dim, dim), f32),
        pltpu.VMEM((n_chip, dim, dim), f32), pltpu.VMEM((side, tok, 2 * dim), bf16),
        pltpu.VMEM((n_chip, sl, dim), f32), pltpu.VMEM((n_chip, sl, dim), f32),
        pltpu.VMEM((n_chip, sl, dim), f32), pltpu.VMEM((n_chip, sl, dim), f32),
        pltpu.VMEM((n_chip, sl, dim), f32), pltpu.VMEM((2, n_chip, sl, dim), f32),
        pltpu.VMEM((n_chip, sl, dim), f32), pltpu.VMEM((2, n_chip, sl, dim), f32),
        pltpu.VMEM((n_head, share, width), bf16), pltpu.VMEM((n_head, share, width), f32),
        pltpu.VMEM((2, share, width), bf16), pltpu.VMEM((8, share, width), bf16),
        pltpu.VMEM((side, 2, wrows, 2 * dim), f32), pltpu.VMEM((side, 2, wrows, 2 * dim), bf16),
        pltpu.VMEM((2, side, wrows, 2 * dim), bf16),
        dma((8,)),
        dma((8,)), dma((n_head, 2)), dma((n_chip,)), dma((n_chip,)), dma((8,)), dma((n_head, 2)), dma((4,)), dma((4,)),
        dma((19,)), dma((n_chip, 2)), dma((side,)), dma((side,)), dma((side, 2)), dma((2, side)),
        dma((n_chip,)), dma((n_chip,)), dma((n_chip,)), dma((n_chip,)),
        dma((n_chip,)), dma((n_chip,)), dma((n_chip,)), dma((n_chip,)), dma((8,)), dma((8,)),
    ]
    shapes = (
        jax.ShapeDtypeStruct((share, width), f32),
        jax.ShapeDtypeStruct((tok, dim), f32),
        jax.ShapeDtypeStruct((tok, dim), f32),
        jax.ShapeDtypeStruct((tok, 2 * dim), f32),
        jax.ShapeDtypeStruct((2, tok), f32),
        jax.ShapeDtypeStruct((2, tok), f32),
        jax.ShapeDtypeStruct((wrows, 2 * dim), f32),
    )
    results = pl.pallas_call(
        functools.partial(kernel, n_ctx, n_head),
        out_shape=shapes,
        in_specs=[hbm] * 8,
        out_specs=(vmem,) * 7,
        scratch_shapes=scratch,
        compiler_params=pltpu.CompilerParams(collective_id=0, has_side_effects=True,
                                             vmem_limit_bytes=60 * 1024 * 1024),
        name="layer",
    )(doc_offsets, queries, key_vectors, value_rows, write_rate, log_decay, out_weight, grad_out)
    return pl.pallas_call(
        emit,
        out_shape=shapes,
        in_specs=[vmem] * 7,
        out_specs=(hbm,) * 7,
        scratch_shapes=[dma((7,))],
        name="emit",
    )(*results)


def emit(*refs):
    copies = [pltpu.make_async_copy(refs[i], refs[7 + i], refs[14].at[i]) for i in range(7)]
    for copy in copies:
        copy.start()
    for copy in copies:
        copy.wait()


def solution(mesh):
    n_ctx, n_head = mesh.shape["ctx"], mesh.shape["head"]
    return jax.shard_map(
        functools.partial(per_device, n_ctx, n_head),
        mesh=mesh,
        in_specs=(
            P("ctx", "head"), P("ctx", "head"), P("ctx", "head"), P("head", "ctx"), P("head", "ctx"),
            P(), P("head", None), P(("ctx", "head"), None),
        ),
        out_specs=(
            P(("ctx", "head"), None), P("ctx", "head"), P("ctx", "head"), P("ctx", "head"),
            P("head", "ctx"), P("head", "ctx"), P("ctx", "head"),
        ),
        check_vma=False,
    )
```

```python
import functools

import jax
import jax.numpy as jnp
from jax import lax
from jax.experimental import pallas as pl
from jax.experimental.pallas import tpu as pltpu
from jax.sharding import PartitionSpec as P

f32 = jnp.float32
bf16 = jnp.bfloat16
MESH = pl.DeviceIdType.MESH


def split(x):
    hi = x.astype(bf16)
    return hi, (x - hi.astype(f32)).astype(bf16)


def mm(a, b, ca=1, cb=0):
    if not isinstance(a, tuple):
        a = (a,) if a.dtype == bf16 else split(a)
    if not isinstance(b, tuple):
        b = (b,) if b.dtype == bf16 else split(b)
    left, right = [a[0]], [b[0]]
    if len(a) == 2:
        left.append(a[1])
        right.append(b[0])
    if len(b) == 2:
        left.append(a[0])
        right.append(b[1])
    left = jnp.concatenate(left, axis=ca) if len(left) > 1 else left[0]
    right = jnp.concatenate(right, axis=cb) if len(right) > 1 else right[0]
    return lax.dot_general(left, right, (((ca,), (cb,)), ((), ())), preferred_element_type=f32)


def rows(*parts):
    parts = [p if isinstance(p, tuple) else split(p) for p in parts]
    return tuple(jnp.concatenate([p[i] for p in parts], axis=0) for i in range(2))


def cols(*parts):
    parts = [p if isinstance(p, tuple) else split(p) for p in parts]
    return tuple(jnp.concatenate([p[i] for p in parts], axis=1) for i in range(2))


def rowsum(x):
    return jnp.sum(x, axis=1, keepdims=True)


def kernel(
    n_ctx, n_head,
    docs_hbm, q_hbm, k_hbm, v_hbm, rate_hbm, decay_hbm, w_hbm, g_hbm,
    out_ref, gq_ref, gk_ref, gv_ref, grate_ref, gdecay_ref, wg_ref,
    docs_ref, q_ref, k_ref, v_ref, rate_ref, decay_ref, w_ref,
    gfull, gcol, gturn, tl_own, tl_oth, a_own, a_oth, tall, mall, lslice, aslice, lsend, asend,
    sret_out, sret_in, aret_out, aret_in, lpart, lfull, lsum, lrecv, wfull, wsend, wrecv,
    i_s, g_ss, g_rs, e_ss, e_rs, h_ss, h_rs, p_ss, p_rs, t_ss, t_rs, m_ss, m_rs, n_ss, n_rs,
    l_ss, l_rs, a_ss, a_rs, s_ss, s_rs, r_ss, r_rs, o_ss, o_rs,
):
    n_chip = n_ctx // 2
    side = 4 if n_chip == 16 else 1
    c = lax.axis_index("ctx")
    z = lax.axis_index("head")
    chip = lax.div(c, 2)
    core = lax.rem(c, 2)
    partner = c + 1 - 2 * core
    row = lax.div(chip, side)
    col = lax.rem(chip, side)
    tok = q_ref.shape[0]
    dim = 128
    width = w_ref.shape[1]
    n_docs = docs_ref.shape[0] - 1
    slice_rows = dim // n_chip

    loads = [
        pltpu.make_async_copy(src, dst, i_s.at[i])
        for i, (src, dst) in enumerate((
            (g_hbm, gfull.at[z]), (q_hbm, q_ref), (k_hbm, k_ref), (docs_hbm, docs_ref),
            (rate_hbm, rate_ref), (decay_hbm, decay_ref), (v_hbm, v_ref), (w_hbm, w_ref),
        ))
    ]
    for load in loads:
        load.start()

    barrier = pltpu.get_barrier_semaphore()

    def greet_head(i, carry):
        pl.semaphore_signal(barrier, inc=1, device_id=(c, lax.rem(z + i, n_head)), device_id_type=MESH)
        return carry

    def greet_ctx(i, carry):
        pl.semaphore_signal(barrier, inc=1, device_id=(lax.rem(c + i, n_ctx), z), device_id_type=MESH)
        return carry

    lax.fori_loop(1, n_head, greet_head, 0)
    lax.fori_loop(1, n_ctx, greet_ctx, 0)

    def zed(shift):
        return lax.rem(z + shift + n_head, n_head)

    def peer(i):
        return lax.rem(chip + i, n_chip)

    def fence(body):
        pl.when(c >= 0)(body)

    def across_head(buf, ss, rs, part):
        sends = [(0, 2, None), (0, -2, None), (0, 1, None), (0, -1, None),
                 (-2, 1, None), (-2, 2, 0), (2, -1, None), (2, -2, 1)]

        def copy(i, block, shift, half):
            ref = buf.at[block] if half is None else part(buf, block, half)
            return pltpu.make_async_remote_copy(
                src_ref=ref, dst_ref=ref, send_sem=ss.at[0], recv_sem=rs.at[block, half or 0],
                device_id=(c, zed(shift)), device_id_type=MESH)

        def start(*which):
            for i in which:
                origin, shift, half = sends[i]
                copy(i, zed(origin), shift, half).start()

        def received(*origins):
            for origin in origins:
                for half in ((0, 1) if origin == 4 else (None,)):
                    copy(0, zed(origin), 1, half).wait_recv()

        def relay():
            received(-2)
            start(4, 5)
            received(2)
            start(6, 7)

        def sent():
            all_sent(buf.at[pl.ds(0, 7)], ss)

        return start, relay, received, sent

    def chip_at(first_shift, second_shift):
        to_col = lax.rem(col + (1 - core) * first_shift + core * second_shift, side)
        to_row = lax.rem(row + core * first_shift + (1 - core) * second_shift, side)
        return to_row * side + to_col

    def across_plane(buf, ss, rs):
        rows_of = buf.shape[1] // 2
        sends = []

        def copy(i, origin, to, half):
            block = chip_at(*origin)
            ref = buf.at[block] if half is None else buf.at[block, pl.ds(half * rows_of, rows_of)]
            return pltpu.make_async_remote_copy(
                src_ref=ref, dst_ref=ref, send_sem=ss.at[0], recv_sem=rs.at[block, half or 0],
                device_id=(chip_at(*to) * 2 + core, z), device_id_type=MESH)

        def start(origin, to, half=None):
            sends.append((origin, to, half))
            copy(len(sends) - 1, origin, to, half).start()

        def received(origin, half=None):
            copy(0, origin, (0, 1), half).wait_recv()

        def own():
            for shift in (1, 3, 2):
                start((0, 0), (shift, 0))
                if shift != 2:
                    start((0, 0), (0, shift))

        def first(*shifts):
            for shift in shifts:
                received((shift, 0))
                start((shift, 0), (0, 1))
                start((shift, 0), (0, 3))

        def second(*shifts):
            for shift in shifts:
                for came, to, half in ((3, 1, 0), (1, 3, 1)):
                    received((shift, came))
                    start((shift, came), (0, to), half)

        def last():
            for shift in (0, 1, 3, 2):
                for half in range(2):
                    received((shift, 2), half)

        def sent():
            all_sent(buf.at[pl.ds(0, n_chip - 1)], ss)

        return own, first, second, last, sent

    g_start, g_relay, g_received, g_sent = across_head(
        gfull, g_ss, g_rs, lambda buf, block, half: buf.at[block, :, pl.ds(half * (width // 2), width // 2)])
    h_start, h_relay, h_received, h_sent = across_head(
        gcol, h_ss, h_rs, lambda buf, block, half: (
            buf.at[block, pl.ds(half * (side // 2), side // 2)] if n_chip > 1
            else buf.at[block, :, :, :, pl.ds(half * 128, 128)]))
    t_own, t_first, t_second, t_last, t_sent = across_plane(tall, t_ss, t_rs)

    def pair_copy(i, src, dst):
        return pltpu.make_async_remote_copy(
            src_ref=src, dst_ref=dst, send_sem=p_ss.at[i], recv_sem=p_rs.at[i],
            device_id=(partner, z), device_id_type=MESH)

    def all_sent(ref, sem):
        pltpu.make_async_remote_copy(src_ref=ref, dst_ref=ref, send_sem=sem.at[0], recv_sem=p_rs.at[0],
                                     device_id=(partner, z), device_id_type=MESH).wait_send()

    def all_received(ref, sem):
        pltpu.make_async_remote_copy(src_ref=ref, dst_ref=ref, send_sem=p_ss.at[0], recv_sem=sem,
                                     device_id=(partner, z), device_id_type=MESH).wait_recv()

    def to_chips(src_of, dst, ss, rs):
        def copy(i):
            return pltpu.make_async_remote_copy(
                src_ref=src_of(peer(i)), dst_ref=dst, send_sem=ss.at[0], recv_sem=rs.at[0],
                device_id=(peer(i) * 2 + core, z), device_id_type=MESH)
        return copy

    chip_width = width // n_chip
    first_at = (1 - core) * col + core * row
    second_at = (1 - core) * row + core * col

    def columns(first, second):
        of = (1 - core) * (second * side + first) + core * (first * side + second)
        return pl.ds(pl.multiple_of(of * chip_width, 128), chip_width)

    def e_copy(i):
        shift, second = lax.div(i, side), lax.rem(i, side)
        return pltpu.make_async_remote_copy(
            src_ref=gfull.at[z, :, columns(lax.rem(first_at + shift, side), second)],
            dst_ref=gcol.at[z, first_at, second], send_sem=e_ss.at[0], recv_sem=e_rs.at[0],
            device_id=(chip_at(shift, 0) * 2 + core, z), device_id_type=MESH)

    def m_copy(shift):
        return pltpu.make_async_remote_copy(
            src_ref=mall.at[first_at], dst_ref=mall.at[first_at], send_sem=m_ss.at[0], recv_sem=m_rs.at[0],
            device_id=(chip_at(shift, 0) * 2 + core, z), device_id_type=MESH)

    def n_copy(shift, to_core):
        return pltpu.make_async_remote_copy(
            src_ref=wsend.at[lax.rem(second_at + shift, side), to_core], dst_ref=wrecv.at[core, second_at],
            send_sem=n_ss.at[0 if shift else 1], recv_sem=n_rs.at[core],
            device_id=(chip_at(0, shift) * 2 + to_core, z), device_id_type=MESH)

    l_copy = to_chips(lambda to: lsend.at[to], lslice.at[chip], l_ss, l_rs)
    a_copy = to_chips(lambda to: asend.at[to], aslice.at[chip], a_ss, a_rs)

    s_copy = to_chips(lambda to: sret_out.at[to], sret_in.at[core, chip], s_ss, s_rs)
    r_copy = to_chips(lambda to: aret_out.at[to], aret_in.at[core, chip], r_ss, r_rs)

    def o_copy(i):
        to, of, half = ((1, 1, None), (-1, -1, None), (1, 3, None), (-1, -3, None), (2, 4, 0), (-2, 4, 1),
                        (2, 2, None), (-2, -2, None))[i]
        src, dst = (lpart.at[zed(of)] if i < 6 else lsum.at[i - 6]), lrecv.at[i]
        if half is not None:
            part = pl.ds(half * (width // 2), width // 2)
            src, dst = lpart.at[zed(of), :, part], lrecv.at[i, :, part]
        return pltpu.make_async_remote_copy(
            src_ref=src, dst_ref=dst, send_sem=o_ss.at[0], recv_sem=o_rs.at[i],
            device_id=(c, zed(to)), device_id_type=MESH)

    def start_all(copy, n, low=1):
        def body(i, carry):
            copy(i).start()
            return carry
        lax.fori_loop(low, n, body, 0)

    def recv_all(copy, n, low=1):
        def body(i, carry):
            copy(i).wait_recv()
            return carry
        lax.fori_loop(low, n, body, 0)

    def sent_all(copy, n, low=1):
        def body(i, carry):
            copy(i).wait_send()
            return carry
        lax.fori_loop(low, n, body, 0)

    for load in loads[1:6]:
        load.wait()
    q = q_ref[...].astype(f32)
    k = k_ref[...].astype(f32)
    q_inv = 1.0 / jnp.sqrt(rowsum(q * q) + 1e-6)
    k_inv = 1.0 / jnp.sqrt(rowsum(k * k) + 1e-6)
    qn = q * q_inv
    kn = k * k_inv
    ks, qs = split(kn), split(qn)
    dots = mm(rows(ks, qs), ks, 1, 1)
    kk, qk = dots[:tok], dots[tok:]
    ii = lax.broadcasted_iota(jnp.int32, (tok, tok), 0)
    jj = lax.broadcasted_iota(jnp.int32, (tok, tok), 1)
    first = c * tok
    seg_i = jnp.zeros((tok, tok), f32)
    seg_j = jnp.zeros((tok, tok), f32)
    seg_all = jnp.zeros((1, 1), f32)
    for d in range(n_docs):
        at = docs_ref[d] - first
        seg_i = seg_i + jnp.where((ii >= at) & (at >= 0), 1.0, 0.0)
        seg_j = seg_j + jnp.where((jj >= at) & (at >= 0), 1.0, 0.0)
    seg_all = seg_i[tok - 1:, :]
    same = jnp.where(seg_i == seg_j, 1.0, 0.0)
    low = jnp.where(ii >= jj, same, 0.0)
    strict = jnp.where(ii > jj, same, 0.0)
    eye = jnp.where(ii == jj, 1.0, 0.0)
    at_start = jnp.where(seg_i[:, :1] == 0.0, 1.0, 0.0)
    at_end = jnp.where(seg_i[:, :1] == seg_all[:, :1], 1.0, 0.0)
    no_reset = jnp.where(seg_all[:, :1] == 0.0, 1.0, 0.0)

    upto = jnp.where(ii <= jj, 1.0, 0.0)
    cum_rows = lax.dot_general(decay_ref[...], upto, (((1,), (0,)), ((), ())),
                               precision=lax.Precision.HIGHEST, preferred_element_type=f32)

    def column(row):
        return rowsum(jnp.where(ii == jj, row, 0.0))

    info = []
    for h in range(2):
        cr = cum_rows[h:h + 1]
        cc = column(cr)
        b = column(rate_ref[h:h + 1, :])
        last = cr[:, tok - 1:]
        info.append(dict(
            b=b,
            ratio=jnp.exp(jnp.where(low > 0.0, cc - cr, 0.0)) * low,
            f=jnp.exp(cc) * at_start,
            e=jnp.exp(last - cc) * at_end,
            w=jnp.exp(last) * no_reset,
        ))

    def same_block(size):
        shift = size.bit_length() - 1
        return lax.shift_right_logical(ii, shift) == lax.shift_right_logical(jj, shift)

    for h in range(2):
        t = info[h]
        t["kr"] = kk * t["ratio"] * strict
        t["n"] = t["b"] * t["kr"]
    for h in range(2):
        t = info[h]
        x = jnp.where(same_block(16), -t["n"], 0.0)
        xs = split(x)
        x2 = mm(xs, xs)
        x2s = split(x2)
        x4 = mm(x2s, x2s)
        x4s = split(x4)
        x8s = split(mm(x4s, x4s))
        m = eye + x
        m = m + mm(m, x2s)
        m = m + mm(m, x4s)
        m = m + mm(m, x8s)
        t["m"] = m
    for size in (16, 32, 64):
        for h in range(2):
            t = info[h]
            off = jnp.where(same_block(2 * size) & ~same_block(size), t["n"], 0.0)
            ms = split(t["m"])
            t["m"] = t["m"] - mm(ms, mm(off, ms))
    loads[6].wait()
    v_all = v_ref[...].astype(f32)
    for h in range(2):
        t = info[h]
        v = v_all[:, h * dim:(h + 1) * dim]
        t["v"] = v
        t["ms"] = split(t["m"])
        uw = mm(t["ms"], cols(t["b"] * v, (t["b"] * t["f"]) * kn))
        uws = split(uw)
        t["u"], t["wks"] = uw[:, :dim], (uws[0][:, dim:], uws[1][:, dim:])
        ek = t["e"] * kn
        t["eks"] = split(ek)
        lt = mm(uws, t["eks"], 0, 0)
        tl_own[h, 0] = t["w"] * eye - lt[dim:]
        tl_own[h, 1] = lt[:dim]
        t["uws"] = uws

    tl_copy = pair_copy(0, tl_own, tl_oth)
    pl.semaphore_wait(barrier, n_head + n_ctx - 2)
    fence(lambda: pair_copy(0, tl_own, tl_oth).start())
    loads[0].wait()
    if n_head > 1:
        fence(lambda: g_start(0, 1, 2, 3))
    start_all(e_copy, n_chip, side)
    for second in range(side):
        gcol[z, first_at, second] = gfull[z, :, columns(first_at, second)]

    for h in range(2):
        t = info[h]
        p = qk * t["ratio"]
        t["p_mat"] = p
        t["ps"] = split(p)
        ow = mm(t["ps"], t["uws"])
        t["o"] = ow[:, :dim]
        t["qt"] = t["f"] * qn - ow[:, dim:]
        t["qts"] = split(t["qt"])
    tl_copy.wait_recv()
    is_first = core == 0

    def ordered(own, other):
        return jnp.where(is_first, own, other), jnp.where(is_first, other, own)

    t0, t1 = ordered(tl_own[core, 0], tl_oth[core, 0])
    l0, l1 = ordered(tl_own[core, 1], tl_oth[core, 1])
    pair_t = mm(rows(t0, l0), t1)
    tall[chip] = pair_t[:dim]
    lsend[...] = (pair_t[dim:] + l1).reshape(n_chip, slice_rows, dim)
    if side > 1:
        fence(t_own)
    start_all(l_copy, n_chip)
    lslice[chip] = lsend[chip]

    for h in range(2):
        t = info[h]
        through = mm(t["qts"], rows(tl_oth[h, 0], tl_oth[h, 1]), 1, 1)
        t["qfs"] = split(jnp.where(is_first, t["qt"], through[:, :dim]))
        t["of"] = t["o"] + jnp.where(is_first, 0.0, through[:, dim:])

    if side > 1:
        @fence
        def _():
            t_first(1, 3)
            t_second(0)
            t_first(2)
    if n_head > 1:
        fence(g_relay)
    if side > 1:
        all_received(gcol.at[z, pl.ds(0, side - 1)], e_rs.at[0])
    if n_head > 1:
        fence(lambda: h_start(0, 1, 2, 3))
    if side > 1:
        @fence
        def _():
            t_second(1, 3)
            t_second(2)
            t_last()
    if side > 1:
        all_received(lslice.at[pl.ds(0, n_chip - 1)], l_rs.at[0])
    state = jnp.zeros((slice_rows, dim), f32)
    for i in range(n_chip):
        sret_out[i] = state
        if i < n_chip - 1:
            state = mm(state, tall[i]) + lslice[i]
    start_all(s_copy, n_chip)
    sret_in[core, chip] = sret_out[chip]

    if n_head > 1:
        g_received(1, -1, 3, -3, 4)
    loads[7].wait()
    full_grad = gfull[...].reshape(tok, width)
    weight = w_ref[...]
    d_core = lax.dot_general(full_grad, weight, (((1,), (1,)), ((), ())), preferred_element_type=f32)
    for h in range(2):
        t = info[h]
        t["do"] = d_core[:, h * dim:(h + 1) * dim]
        t["dos"] = split(t["do"])
        a_own[h] = mm(t["dos"], t["qts"], 0, 0)
    ap_copy = pair_copy(1, a_own, a_oth)
    fence(lambda: pair_copy(1, a_own, a_oth).start())

    for h in range(2):
        t = info[h]
        t["pd"] = mm(t["ps"], t["dos"], 0, 0)
    ap_copy.wait_recv()
    a0, a1 = ordered(a_own[core], a_oth[core])
    asend[...] = (mm(a1, t0, 1, 1) + a0).reshape(n_chip, slice_rows, dim)
    start_all(a_copy, n_chip)
    aslice[chip] = asend[chip]
    if n_head > 1:
        fence(h_relay)

    tl_copy.wait_send()
    if side > 1:
        t_sent()
        all_sent(gcol.at[0, pl.ds(0, side - 1)], e_ss)
        all_sent(lsend.at[pl.ds(0, n_chip - 1)], l_ss)
    if side > 1:
        all_received(sret_in.at[core, pl.ds(0, n_chip - 1)], s_rs.at[0])
    fence(lambda: pair_copy(2, sret_in.at[core], sret_in.at[core]).start())
    pair_copy(2, sret_in.at[core], sret_in.at[1 - core]).wait_recv()
    mixed = []
    for h in range(2):
        t = info[h]
        t["ps_in"] = split(sret_in[h].reshape(dim, dim))
        mixed.append((t["of"] + mm(t["qfs"], t["ps_in"], 1, 1)).astype(bf16))
    mixed = jnp.concatenate(mixed, axis=1)
    mall[first_at] = mixed
    if side > 1:
        @fence
        def _():
            for shift in (2, 1, 3):
                m_copy(shift).start()
    partial = lax.dot_general(mixed, weight, (((1,), (0,)), ((), ())), preferred_element_type=f32)
    partial = partial.reshape(lpart.shape)
    lpart[...] = partial.astype(bf16)
    if n_head > 1:
        @fence
        def _():
            for i in (4, 5, 2, 3, 0, 1):
                o_copy(i).start()
    lfull[...] = partial

    if side > 1:
        all_received(aslice.at[pl.ds(0, n_chip - 1)], a_rs.at[0])
    adjoint = jnp.zeros((slice_rows, dim), f32)
    for j in reversed(range(n_chip)):
        aret_out[j] = adjoint
        if j > 0:
            adjoint = mm(adjoint, tall[j], 1, 1) + aslice[j]
    start_all(r_copy, n_chip)
    aret_in[core, chip] = aret_out[chip]
    if n_head > 1:
        h_received(1, -1, 3, -3, 4)
    for second in range(side):
        for first_of in range(side):
            gturn[second * chip_width:(second + 1) * chip_width, first_of * tok:(first_of + 1) * tok] = (
                gcol[:, first_of, second].reshape(tok, chip_width).T)
    if side > 1:
        all_received(mall.at[pl.ds(0, side - 1)], m_rs.at[0])
    product = lax.dot_general(gturn[...], mall[...].reshape(side * tok, 2 * dim), (((1,), (0,)), ((), ())),
                              preferred_element_type=f32).reshape(wfull.shape)
    wsend[...] = product.astype(bf16)

    @fence
    def _():
        for shift in (2, 1, 3)[:side - 1]:
            for to_core in range(2):
                n_copy(shift, to_core).start()
        n_copy(0, 1 - core).start()
    wfull[...] = product

    if n_head > 1:
        for i in range(2, 6):
            o_copy(i).wait_recv()
        mid = width // 2
        for i in range(2):
            on = lfull[zed(2 - 4 * i)] + lrecv[2 + i].astype(f32)
            more = lrecv[4 + i, :, i * mid:(i + 1) * mid].astype(f32)
            lsum[i, :, i * mid:(i + 1) * mid] = (on[:, i * mid:(i + 1) * mid] + more).astype(bf16)
            lsum[i, :, (1 - i) * mid:(2 - i) * mid] = on[:, (1 - i) * mid:(2 - i) * mid].astype(bf16)

        @fence
        def _():
            o_copy(6).start()
            o_copy(7).start()
    dqk = jnp.zeros((tok, tok), f32)
    dq = jnp.zeros((tok, dim), f32)
    for h in range(2):
        t = info[h]
        state = sret_in[h].reshape(dim, dim)
        t["s"] = jnp.where(is_first, state, mm(t["ps_in"], tl_oth[h, 0]) + tl_oth[h, 1])
        t["ss"] = split(t["s"])
        t["p"] = t["u"] - mm(t["wks"], t["ss"], 1, 1)
        t["pps"] = split(t["p"])
        t["xp"] = mm(t["dos"], t["pps"], 1, 1) * t["ratio"]
        t["d_o_s"] = mm(t["dos"], t["ss"])
        turned = mm(t["ms"], cols(t["pd"], t["eks"]), 0, 0)
        t["dr0"], t["mes"] = turned[:, :dim], split(turned[:, dim:])
        dqk = dqk + t["xp"]
        dq = dq + t["f"] * t["d_o_s"]
    dqks = split(dqk)
    dq = dq + mm(dqks, ks)
    dk = mm(dqks, qs, 0, 0)
    gq_ref[...] = q_inv * (dq - qn * rowsum(qn * dq))
    if side > 1:
        all_sent(sret_out.at[pl.ds(0, n_chip - 1)], s_ss)
        all_sent(asend.at[pl.ds(0, n_chip - 1)], a_ss)
    ap_copy.wait_send()
    if n_head > 1:
        g_sent()
        h_sent()
    if side > 1:
        all_received(aret_in.at[core, pl.ds(0, n_chip - 1)], r_rs.at[0])
    fence(lambda: pair_copy(3, aret_in.at[core], aret_in.at[core]).start())
    pair_copy(3, aret_in.at[core], aret_in.at[1 - core]).wait_recv()
    for h in range(2):
        t = info[h]
        adjoint = aret_in[h].reshape(dim, dim)
        t["g"] = jnp.where(is_first, mm(adjoint, tl_oth[h, 0], 1, 1) + a_oth[h], adjoint)
        t["gs"] = split(t["g"])

    dkk = jnp.zeros((tok, tok), f32)
    before = jnp.where(ii < jj, 1.0, 0.0).astype(bf16)
    for h in range(2):
        t = info[h]
        b, f, e = t["b"], t["f"], t["e"]
        pps = t["pps"]
        pg = mm(pps, t["gs"])
        dr = t["dr0"] + mm(t["mes"], t["gs"], 1, 1)
        drs = split(dr)
        dn = -mm(drs, pps, 1, 1)
        d_o_s, d_r_s = t["d_o_s"], mm(drs, t["ss"])
        xp = t["xp"]
        xr = dn * t["kr"]
        xn = dn * (b * t["ratio"] * strict)
        dkk = dkk + xn
        x = xp * qk + b * xr
        alpha = rowsum(qn * d_o_s)
        beta = rowsum(kn * d_r_s)
        db = rowsum(dr * t["v"]) - f * beta + rowsum(xr)
        gv_ref[:, h * dim:(h + 1) * dim] = b * dr
        grate_ref[h:h + 1, :] = jnp.sum(jnp.where(ii == jj, db, 0.0), axis=0, keepdims=True)
        fdf = f * (alpha - b * beta)
        ede = e * rowsum(kn * pg)
        y = mm(x, before)
        terms = jnp.where(ii >= jj, y + fdf, ede)
        wdw = t["w"] * jnp.sum(rowsum(t["s"] * t["g"]), axis=0, keepdims=True)
        gdecay_ref[h:h + 1, :] = jnp.sum(terms, axis=0, keepdims=True) + wdw
        dk = dk + e * pg - (b * f) * d_r_s
    ds = split(dkk)
    dk = dk + mm(ds, ks) + mm(ds, ks, 0, 0)
    gk_ref[...] = k_inv * (dk - kn * rowsum(kn * dk))

    result = lfull[z]
    if n_head > 1:
        for i in (0, 1, 6, 7):
            o_copy(i).wait_recv()
            result = result + lrecv[i].astype(f32)
    out_ref[...] = result
    total = wfull[second_at, core]
    if side > 1:
        all_received(wrecv.at[core, pl.ds(0, side - 1)], n_rs.at[core])
    all_received(wrecv.at[1 - core], n_rs.at[1 - core])
    for shift in range(1, side):
        at = lax.rem(second_at + shift, side)
        total = total + wrecv[core, at].astype(f32)
    for at in range(side):
        total = total + wrecv[1 - core, at].astype(f32)
    wg_ref[...] = total

    pair_copy(2, sret_in.at[core], sret_in.at[core]).wait_send()
    pair_copy(3, aret_in.at[core], aret_in.at[core]).wait_send()
    n_copy(0, 1 - core).wait_send()
    if side > 1:
        all_sent(mall.at[pl.ds(0, side - 1)], m_ss)
        all_sent(wsend.at[pl.ds(0, side - 1)], n_ss)
        all_sent(aret_out.at[pl.ds(0, n_chip - 1)], r_ss)
    if n_head > 1:
        all_sent(lrecv.at[pl.ds(0, 7)], o_ss)


def per_device(n_ctx, n_head, queries, key_vectors, value_rows, write_rate, log_decay, doc_offsets, out_weight, grad_out):
    n_chip = n_ctx // 2
    side = 4 if n_chip == 16 else 1
    tok, dim = queries.shape
    width = grad_out.shape[1]
    share = grad_out.shape[0]
    sl = dim // n_chip
    wrows = width // n_ctx
    vmem = pl.BlockSpec(memory_space=pltpu.VMEM)
    hbm = pl.BlockSpec(memory_space=pltpu.HBM)
    dma = pltpu.SemaphoreType.DMA
    scratch = [
        pltpu.SMEM(doc_offsets.shape, jnp.int32),
        pltpu.VMEM((tok, dim), bf16), pltpu.VMEM((tok, dim), bf16), pltpu.VMEM((tok, 2 * dim), bf16),
        pltpu.VMEM((2, tok), f32), pltpu.VMEM((2, tok), f32), pltpu.VMEM((2 * dim, width), bf16),
        pltpu.VMEM((n_head, share, width), bf16),
        pltpu.VMEM((n_head, side, side, share, width // n_chip), bf16),
        pltpu.VMEM((side * (width // n_chip), side * tok), bf16),
        pltpu.VMEM((2, 2, dim, dim), f32), pltpu.VMEM((2, 2, dim, dim), f32),
        pltpu.VMEM((2, dim, dim), f32), pltpu.VMEM((2, dim, dim), f32),
        pltpu.VMEM((n_chip, dim, dim), f32), pltpu.VMEM((side, tok, 2 * dim), bf16),
        pltpu.VMEM((n_chip, sl, dim), f32), pltpu.VMEM((n_chip, sl, dim), f32),
        pltpu.VMEM((n_chip, sl, dim), f32), pltpu.VMEM((n_chip, sl, dim), f32),
        pltpu.VMEM((n_chip, sl, dim), f32), pltpu.VMEM((2, n_chip, sl, dim), f32),
        pltpu.VMEM((n_chip, sl, dim), f32), pltpu.VMEM((2, n_chip, sl, dim), f32),
        pltpu.VMEM((n_head, share, width), bf16), pltpu.VMEM((n_head, share, width), f32),
        pltpu.VMEM((2, share, width), bf16), pltpu.VMEM((8, share, width), bf16),
        pltpu.VMEM((side, 2, wrows, 2 * dim), f32), pltpu.VMEM((side, 2, wrows, 2 * dim), bf16),
        pltpu.VMEM((2, side, wrows, 2 * dim), bf16),
        dma((8,)),
        dma((1,)), dma((n_head, 2)), dma((1,)), dma((1,)), dma((1,)), dma((n_head, 2)), dma((4,)), dma((4,)),
        dma((1,)), dma((n_chip, 2)), dma((1,)), dma((1,)), dma((2,)), dma((2,)),
        dma((1,)), dma((1,)), dma((1,)), dma((1,)),
        dma((1,)), dma((1,)), dma((1,)), dma((1,)), dma((1,)), dma((8,)),
    ]
    shapes = (
        jax.ShapeDtypeStruct((share, width), f32),
        jax.ShapeDtypeStruct((tok, dim), f32),
        jax.ShapeDtypeStruct((tok, dim), f32),
        jax.ShapeDtypeStruct((tok, 2 * dim), f32),
        jax.ShapeDtypeStruct((2, tok), f32),
        jax.ShapeDtypeStruct((2, tok), f32),
        jax.ShapeDtypeStruct((wrows, 2 * dim), f32),
    )
    results = pl.pallas_call(
        functools.partial(kernel, n_ctx, n_head),
        out_shape=shapes,
        in_specs=[hbm] * 8,
        out_specs=(vmem,) * 7,
        scratch_shapes=scratch,
        compiler_params=pltpu.CompilerParams(collective_id=0, has_side_effects=True,
                                             vmem_limit_bytes=60 * 1024 * 1024),
        name="layer",
    )(doc_offsets, queries, key_vectors, value_rows, write_rate, log_decay, out_weight, grad_out)
    return pl.pallas_call(
        emit,
        out_shape=shapes,
        in_specs=[vmem] * 7,
        out_specs=(hbm,) * 7,
        scratch_shapes=[dma((7,))],
        name="emit",
    )(*results)


def emit(*refs):
    copies = [pltpu.make_async_copy(refs[i], refs[7 + i], refs[14].at[i]) for i in range(7)]
    for copy in copies:
        copy.start()
    for copy in copies:
        copy.wait()


def solution(mesh):
    n_ctx, n_head = mesh.shape["ctx"], mesh.shape["head"]
    return jax.shard_map(
        functools.partial(per_device, n_ctx, n_head),
        mesh=mesh,
        in_specs=(
            P("ctx", "head"), P("ctx", "head"), P("ctx", "head"), P("head", "ctx"), P("head", "ctx"),
            P(), P("head", None), P(("ctx", "head"), None),
        ),
        out_specs=(
            P(("ctx", "head"), None), P("ctx", "head"), P("ctx", "head"), P("ctx", "head"),
            P("head", "ctx"), P("head", "ctx"), P("ctx", "head"),
        ),
        check_vma=False,
    )
```

```python
import functools

import jax
import jax.numpy as jnp
from jax import lax
from jax.experimental import pallas as pl
from jax.experimental.pallas import tpu as pltpu
from jax.sharding import PartitionSpec as P

f32 = jnp.float32
bf16 = jnp.bfloat16
MESH = pl.DeviceIdType.MESH


def split(x):
    hi = x.astype(bf16)
    return hi, (x - hi.astype(f32)).astype(bf16)


def mm(a, b, ca=1, cb=0):
    if not isinstance(a, tuple):
        a = (a,) if a.dtype == bf16 else split(a)
    if not isinstance(b, tuple):
        b = (b,) if b.dtype == bf16 else split(b)
    left, right = [a[0]], [b[0]]
    if len(a) == 2:
        left.append(a[1])
        right.append(b[0])
    if len(b) == 2:
        left.append(a[0])
        right.append(b[1])
    left = jnp.concatenate(left, axis=ca) if len(left) > 1 else left[0]
    right = jnp.concatenate(right, axis=cb) if len(right) > 1 else right[0]
    return lax.dot_general(left, right, (((ca,), (cb,)), ((), ())), preferred_element_type=f32)


def rows(*parts):
    parts = [p if isinstance(p, tuple) else split(p) for p in parts]
    return tuple(jnp.concatenate([p[i] for p in parts], axis=0) for i in range(2))


def cols(*parts):
    parts = [p if isinstance(p, tuple) else split(p) for p in parts]
    return tuple(jnp.concatenate([p[i] for p in parts], axis=1) for i in range(2))


def rowsum(x):
    return jnp.sum(x, axis=1, keepdims=True)


def kernel(
    n_ctx, n_head,
    docs_hbm, q_hbm, k_hbm, v_hbm, rate_hbm, decay_hbm, w_hbm, g_hbm,
    out_ref, gq_ref, gk_ref, gv_ref, grate_ref, gdecay_ref, wg_ref,
    docs_ref, q_ref, k_ref, v_ref, rate_ref, decay_ref, w_ref,
    gfull, gcol, gturn, tl_own, tl_oth, a_own, a_oth, tall, mall, lslice, aslice, lsend, asend,
    sret_out, sret_in, aret_out, aret_in, lpart, lfull, lsum, lrecv, wfull, wsend, wrecv,
    i_s, g_ss, g_rs, e_ss, e_rs, h_ss, h_rs, p_ss, p_rs, t_ss, t_rs, m_ss, m_rs, n_ss, n_rs,
    l_ss, l_rs, a_ss, a_rs, s_ss, s_rs, r_ss, r_rs, o_ss, o_rs,
):
    n_chip = n_ctx // 2
    side = 4 if n_chip == 16 else 1
    c = lax.axis_index("ctx")
    z = lax.axis_index("head")
    chip = lax.div(c, 2)
    core = lax.rem(c, 2)
    partner = c + 1 - 2 * core
    row = lax.div(chip, side)
    col = lax.rem(chip, side)
    tok = q_ref.shape[0]
    dim = 128
    width = w_ref.shape[1]
    n_docs = docs_ref.shape[0] - 1
    slice_rows = dim // n_chip

    loads = [
        pltpu.make_async_copy(src, dst, i_s.at[i])
        for i, (src, dst) in enumerate((
            (g_hbm, gfull.at[z]), (q_hbm, q_ref), (k_hbm, k_ref), (docs_hbm, docs_ref),
            (rate_hbm, rate_ref), (decay_hbm, decay_ref), (v_hbm, v_ref), (w_hbm, w_ref),
        ))
    ]
    for load in loads:
        load.start()

    barrier = pltpu.get_barrier_semaphore()

    def greet_head(i, carry):
        pl.semaphore_signal(barrier, inc=1, device_id=(c, lax.rem(z + i, n_head)), device_id_type=MESH)
        return carry

    def greet_ctx(i, carry):
        pl.semaphore_signal(barrier, inc=1, device_id=(lax.rem(c + i, n_ctx), z), device_id_type=MESH)
        return carry

    lax.fori_loop(1, n_ctx, greet_ctx, 0, unroll=True)
    lax.fori_loop(1, n_head, greet_head, 0, unroll=True)

    def zed(shift):
        return lax.rem(z + shift + n_head, n_head)

    def peer(i):
        return lax.rem(chip + i, n_chip)

    def fence(body):
        pl.when(c >= 0)(body)

    def across_head(buf, ss, rs, part):
        sends = [(0, 2, None), (0, -2, None), (0, 1, None), (0, -1, None),
                 (-2, 1, None), (-2, 2, 0), (2, -1, None), (2, -2, 1)]

        def copy(i, block, shift, half):
            ref = buf.at[block] if half is None else part(buf, block, half)
            return pltpu.make_async_remote_copy(
                src_ref=ref, dst_ref=ref, send_sem=ss.at[0], recv_sem=rs.at[block],
                device_id=(c, zed(shift)), device_id_type=MESH)

        def start(*which):
            for i in which:
                origin, shift, half = sends[i]
                copy(i, zed(origin), shift, half).start()

        def received(*origins):
            for origin in origins:
                copy(0, zed(origin), 1, None).wait_recv()

        def relay():
            received(-2)
            start(4, 5)
            received(2)
            start(6, 7)

        def sent():
            all_sent(buf.at[pl.ds(0, 7)], ss)

        return start, relay, received, sent

    def chip_at(first_shift, second_shift):
        to_col = lax.rem(col + (1 - core) * first_shift + core * second_shift, side)
        to_row = lax.rem(row + core * first_shift + (1 - core) * second_shift, side)
        return to_row * side + to_col

    def across_plane(buf, ss, rs):
        rows_of = buf.shape[1] // 2
        sends = []

        def copy(i, origin, to, half):
            block = chip_at(*origin)
            ref = buf.at[block] if half is None else buf.at[block, pl.ds(half * rows_of, rows_of)]
            return pltpu.make_async_remote_copy(
                src_ref=ref, dst_ref=ref, send_sem=ss.at[0], recv_sem=rs.at[block],
                device_id=(chip_at(*to) * 2 + core, z), device_id_type=MESH)

        def start(origin, to, half=None):
            sends.append((origin, to, half))
            copy(len(sends) - 1, origin, to, half).start()

        def received(origin, half=None):
            copy(0, origin, (0, 1), half).wait_recv()

        def own():
            for shift in (1, 3, 2):
                start((0, 0), (shift, 0))
                if shift != 2:
                    start((0, 0), (0, shift))

        def first(*shifts):
            for shift in shifts:
                received((shift, 0))
                start((shift, 0), (0, 1))
                start((shift, 0), (0, 3))

        def second(*shifts):
            for shift in shifts:
                for came, to, half in ((3, 1, 0), (1, 3, 1)):
                    received((shift, came))
                    start((shift, came), (0, to), half)

        def last():
            for shift in (0, 1, 3, 2):
                received((shift, 2))

        def sent():
            all_sent(buf.at[pl.ds(0, n_chip - 1)], ss)

        return own, first, second, last, sent

    g_start, g_relay, g_received, g_sent = across_head(
        gfull, g_ss, g_rs, lambda buf, block, half: buf.at[block, :, pl.ds(half * (width // 2), width // 2)])
    h_start, h_relay, h_received, h_sent = across_head(
        gcol, h_ss, h_rs, lambda buf, block, half: (
            buf.at[block, pl.ds(half * (side // 2), side // 2)] if n_chip > 1
            else buf.at[block, :, :, :, pl.ds(half * 128, 128)]))
    t_own, t_first, t_second, t_last, t_sent = across_plane(tall, t_ss, t_rs)

    def pair_copy(i, src, dst):
        return pltpu.make_async_remote_copy(
            src_ref=src, dst_ref=dst, send_sem=p_ss.at[i], recv_sem=p_rs.at[i],
            device_id=(partner, z), device_id_type=MESH)

    def all_sent(ref, sem):
        pltpu.make_async_remote_copy(src_ref=ref, dst_ref=ref, send_sem=sem.at[0], recv_sem=p_rs.at[0],
                                     device_id=(partner, z), device_id_type=MESH).wait_send()

    def all_received(ref, sem):
        pltpu.make_async_remote_copy(src_ref=ref, dst_ref=ref, send_sem=p_ss.at[0], recv_sem=sem,
                                     device_id=(partner, z), device_id_type=MESH).wait_recv()

    def to_chips(src_of, dst, ss, rs):
        def copy(i):
            return pltpu.make_async_remote_copy(
                src_ref=src_of(peer(i)), dst_ref=dst, send_sem=ss.at[0], recv_sem=rs.at[0],
                device_id=(peer(i) * 2 + core, z), device_id_type=MESH)
        return copy

    chip_width = width // n_chip
    first_at = (1 - core) * col + core * row
    second_at = (1 - core) * row + core * col

    def columns(first, second):
        of = (1 - core) * (second * side + first) + core * (first * side + second)
        return pl.ds(pl.multiple_of(of * chip_width, 128), chip_width)

    def e_copy(i):
        shift, second = lax.div(i, side), lax.rem(i, side)
        return pltpu.make_async_remote_copy(
            src_ref=gfull.at[z, :, columns(lax.rem(first_at + shift, side), second)],
            dst_ref=gcol.at[z, first_at, second], send_sem=e_ss.at[0], recv_sem=e_rs.at[0],
            device_id=(chip_at(shift, 0) * 2 + core, z), device_id_type=MESH)

    def m_copy(shift):
        return pltpu.make_async_remote_copy(
            src_ref=mall.at[first_at], dst_ref=mall.at[first_at], send_sem=m_ss.at[0], recv_sem=m_rs.at[0],
            device_id=(chip_at(shift, 0) * 2 + core, z), device_id_type=MESH)

    def n_copy(shift, to_core):
        return pltpu.make_async_remote_copy(
            src_ref=wsend.at[lax.rem(second_at + shift, side), to_core], dst_ref=wrecv.at[core, second_at],
            send_sem=n_ss.at[0 if shift else 1], recv_sem=n_rs.at[core],
            device_id=(chip_at(0, shift) * 2 + to_core, z), device_id_type=MESH)

    l_copy = to_chips(lambda to: lsend.at[to], lslice.at[chip], l_ss, l_rs)
    a_copy = to_chips(lambda to: asend.at[to], aslice.at[chip], a_ss, a_rs)

    s_copy = to_chips(lambda to: sret_out.at[to], sret_in.at[core, chip], s_ss, s_rs)
    r_copy = to_chips(lambda to: aret_out.at[to], aret_in.at[core, chip], r_ss, r_rs)

    def o_copy(i):
        to, of, half = ((1, 1, None), (-1, -1, None), (1, 3, None), (-1, -3, None), (2, 4, 0), (-2, 4, 1),
                        (2, 2, None), (-2, -2, None))[i]
        src, dst = (lpart.at[zed(of)] if i < 6 else lsum.at[i - 6]), lrecv.at[i]
        if half is not None:
            part = pl.ds(half * (width // 2), width // 2)
            src, dst = lpart.at[zed(of), :, part], lrecv.at[i, :, part]
        return pltpu.make_async_remote_copy(
            src_ref=src, dst_ref=dst, send_sem=o_ss.at[0], recv_sem=o_rs.at[i],
            device_id=(c, zed(to)), device_id_type=MESH)

    def start_all(copy, n, low=1):
        def body(i, carry):
            copy(i).start()
            return carry
        lax.fori_loop(low, n, body, 0, unroll=True)

    for load in loads[1:6]:
        load.wait()
    q = q_ref[...].astype(f32)
    k = k_ref[...].astype(f32)
    q_inv = 1.0 / jnp.sqrt(rowsum(q * q) + 1e-6)
    k_inv = 1.0 / jnp.sqrt(rowsum(k * k) + 1e-6)
    qn = q * q_inv
    kn = k * k_inv
    ks, qs = split(kn), split(qn)
    dots = mm(rows(ks, qs), ks, 1, 1)
    kk, qk = dots[:tok], dots[tok:]
    ii = lax.broadcasted_iota(jnp.int32, (tok, tok), 0)
    jj = lax.broadcasted_iota(jnp.int32, (tok, tok), 1)
    first = c * tok
    seg_i = jnp.zeros((tok, tok), f32)
    seg_j = jnp.zeros((tok, tok), f32)
    seg_all = jnp.zeros((1, 1), f32)
    for d in range(n_docs):
        at = docs_ref[d] - first
        seg_i = seg_i + jnp.where((ii >= at) & (at >= 0), 1.0, 0.0)
        seg_j = seg_j + jnp.where((jj >= at) & (at >= 0), 1.0, 0.0)
    seg_all = seg_i[tok - 1:, :]
    same = jnp.where(seg_i == seg_j, 1.0, 0.0)
    low = jnp.where(ii >= jj, same, 0.0)
    strict = jnp.where(ii > jj, same, 0.0)
    eye = jnp.where(ii == jj, 1.0, 0.0)
    at_start = jnp.where(seg_i[:, :1] == 0.0, 1.0, 0.0)
    at_end = jnp.where(seg_i[:, :1] == seg_all[:, :1], 1.0, 0.0)
    no_reset = jnp.where(seg_all[:, :1] == 0.0, 1.0, 0.0)

    upto = jnp.where(ii <= jj, 1.0, 0.0)
    cum_rows = lax.dot_general(decay_ref[...], upto, (((1,), (0,)), ((), ())),
                               precision=lax.Precision.HIGHEST, preferred_element_type=f32)

    def column(row):
        return rowsum(jnp.where(ii == jj, row, 0.0))

    info = []
    for h in range(2):
        cr = cum_rows[h:h + 1]
        cc = column(cr)
        b = column(rate_ref[h:h + 1, :])
        last = cr[:, tok - 1:]
        info.append(dict(
            b=b,
            ratio=jnp.exp(jnp.where(low > 0.0, cc - cr, 0.0)) * low,
            f=jnp.exp(cc) * at_start,
            e=jnp.exp(last - cc) * at_end,
            w=jnp.exp(last) * no_reset,
        ))

    def same_block(size):
        shift = size.bit_length() - 1
        return lax.shift_right_logical(ii, shift) == lax.shift_right_logical(jj, shift)

    for h in range(2):
        t = info[h]
        t["kr"] = kk * t["ratio"] * strict
        t["n"] = t["b"] * t["kr"]
    for h in range(2):
        t = info[h]
        x = jnp.where(same_block(16), -t["n"], 0.0)
        xs = split(x)
        x2 = mm(xs, xs)
        x2s = split(x2)
        x4 = mm(x2s, x2s)
        x4s = split(x4)
        x8s = split(mm(x4s, x4s))
        m = eye + x
        m = m + mm(m, x2s)
        m = m + mm(m, x4s)
        m = m + mm(m, x8s)
        t["m"] = m
    for size in (16, 32, 64):
        for h in range(2):
            t = info[h]
            off = jnp.where(same_block(2 * size) & ~same_block(size), t["n"], 0.0)
            ms = split(t["m"])
            t["m"] = t["m"] - mm(ms, mm(off, ms))
    loads[6].wait()
    v_all = v_ref[...].astype(f32)
    for h in range(2):
        t = info[h]
        v = v_all[:, h * dim:(h + 1) * dim]
        t["v"] = v
        t["ms"] = split(t["m"])
        uw = mm(t["ms"], cols(t["b"] * v, (t["b"] * t["f"]) * kn))
        uws = split(uw)
        t["u"], t["wks"] = uw[:, :dim], (uws[0][:, dim:], uws[1][:, dim:])
        ek = t["e"] * kn
        t["eks"] = split(ek)
        lt = mm(uws, t["eks"], 0, 0)
        tl_own[h, 0] = t["w"] * eye - lt[dim:]
        tl_own[h, 1] = lt[:dim]
        t["uws"] = uws

    tl_copy = pair_copy(0, tl_own, tl_oth)
    pl.semaphore_wait(barrier, n_head + n_ctx - 2)
    fence(lambda: pair_copy(0, tl_own, tl_oth).start())
    loads[0].wait()
    if n_head > 1:
        fence(lambda: g_start(0, 1, 2, 3))
    start_all(e_copy, n_chip, side)
    for second in range(side):
        gcol[z, first_at, second] = gfull[z, :, columns(first_at, second)]

    for h in range(2):
        t = info[h]
        p = qk * t["ratio"]
        t["p_mat"] = p
        t["ps"] = split(p)
        ow = mm(t["ps"], t["uws"])
        t["o"] = ow[:, :dim]
        t["qt"] = t["f"] * qn - ow[:, dim:]
        t["qts"] = split(t["qt"])
    tl_copy.wait_recv()
    is_first = core == 0

    def ordered(own, other):
        return jnp.where(is_first, own, other), jnp.where(is_first, other, own)

    t0, t1 = ordered(tl_own[core, 0], tl_oth[core, 0])
    l0, l1 = ordered(tl_own[core, 1], tl_oth[core, 1])
    pair_t = mm(rows(t0, l0), t1)
    tall[chip] = pair_t[:dim]
    lsend[...] = (pair_t[dim:] + l1).reshape(n_chip, slice_rows, dim)
    if side > 1:
        fence(t_own)
    start_all(l_copy, n_chip)
    lslice[chip] = lsend[chip]

    for h in range(2):
        t = info[h]
        through = mm(t["qts"], rows(tl_oth[h, 0], tl_oth[h, 1]), 1, 1)
        t["qfs"] = split(jnp.where(is_first, t["qt"], through[:, :dim]))
        t["mes"] = split(mm(t["ms"], t["eks"], 0, 0))
        t["of"] = t["o"] + jnp.where(is_first, 0.0, through[:, dim:])

    if side > 1:
        @fence
        def _():
            t_first(1, 3)
            t_second(0)
            t_first(2)
    if n_head > 1:
        fence(g_relay)
    if side > 1:
        all_received(gcol.at[z, pl.ds(0, side - 1)], e_rs.at[0])
    if n_head > 1:
        fence(lambda: h_start(0, 1, 2, 3))
    if side > 1:
        @fence
        def _():
            t_second(1, 3)
            t_second(2)
            t_last()
    if side > 1:
        all_received(lslice.at[pl.ds(0, n_chip - 1)], l_rs.at[0])
    state = jnp.zeros((slice_rows, dim), f32)
    for i in range(n_chip):
        sret_out[i] = state
        if i < n_chip - 1:
            state = mm(state, tall[i]) + lslice[i]
    start_all(s_copy, n_chip)
    sret_in[core, chip] = sret_out[chip]

    if n_head > 1:
        g_received(1, -1, 3, -3, 4)
    loads[7].wait()
    full_grad = gfull[...].reshape(tok, width)
    weight = w_ref[...]
    d_core = lax.dot_general(full_grad, weight, (((1,), (1,)), ((), ())), preferred_element_type=f32)
    for h in range(2):
        t = info[h]
        t["do"] = d_core[:, h * dim:(h + 1) * dim]
        t["dos"] = split(t["do"])
        a_own[h] = mm(t["dos"], t["qts"], 0, 0)
    ap_copy = pair_copy(1, a_own, a_oth)
    fence(lambda: pair_copy(1, a_own, a_oth).start())
    if n_head > 1:
        fence(h_relay)

    for h in range(2):
        t = info[h]
        t["pd"] = mm(t["ps"], t["dos"], 0, 0)
    ap_copy.wait_recv()
    a0, a1 = ordered(a_own[core], a_oth[core])
    asend[...] = (mm(a1, t0, 1, 1) + a0).reshape(n_chip, slice_rows, dim)
    start_all(a_copy, n_chip)
    aslice[chip] = asend[chip]

    tl_copy.wait_send()
    if side > 1:
        t_sent()
        all_sent(gcol.at[0, pl.ds(0, side - 1)], e_ss)
        all_sent(lsend.at[pl.ds(0, n_chip - 1)], l_ss)
    if side > 1:
        all_received(sret_in.at[core, pl.ds(0, n_chip - 1)], s_rs.at[0])
    fence(lambda: pair_copy(2, sret_in.at[core], sret_in.at[core]).start())
    pair_copy(2, sret_in.at[core], sret_in.at[1 - core]).wait_recv()
    mixed = []
    for h in range(2):
        t = info[h]
        t["ps_in"] = split(sret_in[h].reshape(dim, dim))
        mixed.append((t["of"] + mm(t["qfs"], t["ps_in"], 1, 1)).astype(bf16))
    mixed = jnp.concatenate(mixed, axis=1)
    mall[first_at] = mixed
    if side > 1:
        @fence
        def _():
            for shift in (2, 1, 3):
                m_copy(shift).start()
    partial = lax.dot_general(mixed, weight, (((1,), (0,)), ((), ())), preferred_element_type=f32)
    partial = partial.reshape(lpart.shape)
    lpart[...] = partial.astype(bf16)
    if n_head > 1:
        @fence
        def _():
            for i in (4, 5, 2, 3, 0, 1):
                o_copy(i).start()
    lfull[...] = partial

    if side > 1:
        all_received(aslice.at[pl.ds(0, n_chip - 1)], a_rs.at[0])
    adjoint = jnp.zeros((slice_rows, dim), f32)
    for j in reversed(range(n_chip)):
        aret_out[j] = adjoint
        if j > 0:
            adjoint = mm(adjoint, tall[j], 1, 1) + aslice[j]
    start_all(r_copy, n_chip)
    aret_in[core, chip] = aret_out[chip]
    if n_head > 1:
        h_received(1, -1, 3, -3, 4)
    for second in range(side):
        for first_of in range(side):
            gturn[second * chip_width:(second + 1) * chip_width, first_of * tok:(first_of + 1) * tok] = (
                gcol[:, first_of, second].reshape(tok, chip_width).T)
    if side > 1:
        all_received(mall.at[pl.ds(0, side - 1)], m_rs.at[0])
    product = lax.dot_general(gturn[...], mall[...].reshape(side * tok, 2 * dim), (((1,), (0,)), ((), ())),
                              preferred_element_type=f32).reshape(wfull.shape)
    wsend[...] = product.astype(bf16)

    @fence
    def _():
        for shift in (2, 1, 3)[:side - 1]:
            for to_core in range(2):
                n_copy(shift, to_core).start()
        n_copy(0, 1 - core).start()
    wfull[...] = product

    if n_head > 1:
        for i in range(2, 6):
            o_copy(i).wait_recv()
        mid = width // 2
        for i in range(2):
            on = lfull[zed(2 - 4 * i)] + lrecv[2 + i].astype(f32)
            more = lrecv[4 + i, :, i * mid:(i + 1) * mid].astype(f32)
            lsum[i, :, i * mid:(i + 1) * mid] = (on[:, i * mid:(i + 1) * mid] + more).astype(bf16)
            lsum[i, :, (1 - i) * mid:(2 - i) * mid] = on[:, (1 - i) * mid:(2 - i) * mid].astype(bf16)

        @fence
        def _():
            o_copy(6).start()
            o_copy(7).start()
    dqk = jnp.zeros((tok, tok), f32)
    dq = jnp.zeros((tok, dim), f32)
    for h in range(2):
        t = info[h]
        state = sret_in[h].reshape(dim, dim)
        t["s"] = jnp.where(is_first, state, mm(t["ps_in"], tl_oth[h, 0]) + tl_oth[h, 1])
        t["ss"] = split(t["s"])
        t["p"] = t["u"] - mm(t["wks"], t["ss"], 1, 1)
        t["pps"] = split(t["p"])
        t["xp"] = mm(t["dos"], t["pps"], 1, 1) * t["ratio"]
        t["d_o_s"] = mm(t["dos"], t["ss"])
        t["dr0"] = mm(t["ms"], t["pd"], 0, 0)
        dqk = dqk + t["xp"]
        dq = dq + t["f"] * t["d_o_s"]
    dqks = split(dqk)
    dq = dq + mm(dqks, ks)
    dk = mm(dqks, qs, 0, 0)
    gq_ref[...] = q_inv * (dq - qn * rowsum(qn * dq))
    if side > 1:
        all_sent(sret_out.at[pl.ds(0, n_chip - 1)], s_ss)
        all_sent(asend.at[pl.ds(0, n_chip - 1)], a_ss)
    ap_copy.wait_send()
    if n_head > 1:
        g_sent()
        h_sent()
    if side > 1:
        all_received(aret_in.at[core, pl.ds(0, n_chip - 1)], r_rs.at[0])
    fence(lambda: pair_copy(3, aret_in.at[core], aret_in.at[core]).start())
    pair_copy(3, aret_in.at[core], aret_in.at[1 - core]).wait_recv()
    for h in range(2):
        t = info[h]
        adjoint = aret_in[h].reshape(dim, dim)
        t["g"] = jnp.where(is_first, mm(adjoint, tl_oth[h, 0], 1, 1) + a_oth[h], adjoint)
        t["gs"] = split(t["g"])

    dkk = jnp.zeros((tok, tok), f32)
    before = jnp.where(ii < jj, 1.0, 0.0).astype(bf16)
    for h in range(2):
        t = info[h]
        b, f, e = t["b"], t["f"], t["e"]
        pps = t["pps"]
        pg = mm(pps, t["gs"])
        dr = t["dr0"] + mm(t["mes"], t["gs"], 1, 1)
        drs = split(dr)
        dn = -mm(drs, pps, 1, 1)
        d_o_s, d_r_s = t["d_o_s"], mm(drs, t["ss"])
        xp = t["xp"]
        xr = dn * t["kr"]
        xn = dn * (b * t["ratio"] * strict)
        dkk = dkk + xn
        x = xp * qk + b * xr
        alpha = rowsum(qn * d_o_s)
        beta = rowsum(kn * d_r_s)
        db = rowsum(dr * t["v"]) - f * beta + rowsum(xr)
        gv_ref[:, h * dim:(h + 1) * dim] = b * dr
        grate_ref[h:h + 1, :] = jnp.sum(jnp.where(ii == jj, db, 0.0), axis=0, keepdims=True)
        fdf = f * (alpha - b * beta)
        ede = e * rowsum(kn * pg)
        y = mm(x, before)
        terms = jnp.where(ii >= jj, y + fdf, ede)
        wdw = t["w"] * jnp.sum(rowsum(t["s"] * t["g"]), axis=0, keepdims=True)
        gdecay_ref[h:h + 1, :] = jnp.sum(terms, axis=0, keepdims=True) + wdw
        dk = dk + e * pg - (b * f) * d_r_s
    ds = split(dkk)
    dk = dk + mm(ds, ks) + mm(ds, ks, 0, 0)
    gk_ref[...] = k_inv * (dk - kn * rowsum(kn * dk))

    result = lfull[z]
    if n_head > 1:
        for i in (0, 1, 6, 7):
            o_copy(i).wait_recv()
            result = result + lrecv[i].astype(f32)
    out_ref[...] = result
    total = wfull[second_at, core]
    if side > 1:
        all_received(wrecv.at[core, pl.ds(0, side - 1)], n_rs.at[core])
    all_received(wrecv.at[1 - core], n_rs.at[1 - core])
    for shift in range(1, side):
        at = lax.rem(second_at + shift, side)
        total = total + wrecv[core, at].astype(f32)
    for at in range(side):
        total = total + wrecv[1 - core, at].astype(f32)
    wg_ref[...] = total

    pair_copy(2, sret_in.at[core], sret_in.at[core]).wait_send()
    pair_copy(3, aret_in.at[core], aret_in.at[core]).wait_send()
    n_copy(0, 1 - core).wait_send()
    if side > 1:
        all_sent(mall.at[pl.ds(0, side - 1)], m_ss)
        all_sent(wsend.at[pl.ds(0, side - 1)], n_ss)
        all_sent(aret_out.at[pl.ds(0, n_chip - 1)], r_ss)
    if n_head > 1:
        all_sent(lrecv.at[pl.ds(0, 7)], o_ss)


def per_device(n_ctx, n_head, queries, key_vectors, value_rows, write_rate, log_decay, doc_offsets, out_weight, grad_out):
    n_chip = n_ctx // 2
    side = 4 if n_chip == 16 else 1
    tok, dim = queries.shape
    width = grad_out.shape[1]
    share = grad_out.shape[0]
    sl = dim // n_chip
    wrows = width // n_ctx
    vmem = pl.BlockSpec(memory_space=pltpu.VMEM)
    hbm = pl.BlockSpec(memory_space=pltpu.HBM)
    dma = pltpu.SemaphoreType.DMA
    scratch = [
        pltpu.SMEM(doc_offsets.shape, jnp.int32),
        pltpu.VMEM((tok, dim), bf16), pltpu.VMEM((tok, dim), bf16), pltpu.VMEM((tok, 2 * dim), bf16),
        pltpu.VMEM((2, tok), f32), pltpu.VMEM((2, tok), f32), pltpu.VMEM((2 * dim, width), bf16),
        pltpu.VMEM((n_head, share, width), bf16),
        pltpu.VMEM((n_head, side, side, share, width // n_chip), bf16),
        pltpu.VMEM((side * (width // n_chip), side * tok), bf16),
        pltpu.VMEM((2, 2, dim, dim), f32), pltpu.VMEM((2, 2, dim, dim), f32),
        pltpu.VMEM((2, dim, dim), f32), pltpu.VMEM((2, dim, dim), f32),
        pltpu.VMEM((n_chip, dim, dim), f32), pltpu.VMEM((side, tok, 2 * dim), bf16),
        pltpu.VMEM((n_chip, sl, dim), f32), pltpu.VMEM((n_chip, sl, dim), f32),
        pltpu.VMEM((n_chip, sl, dim), f32), pltpu.VMEM((n_chip, sl, dim), f32),
        pltpu.VMEM((n_chip, sl, dim), f32), pltpu.VMEM((2, n_chip, sl, dim), f32),
        pltpu.VMEM((n_chip, sl, dim), f32), pltpu.VMEM((2, n_chip, sl, dim), f32),
        pltpu.VMEM((n_head, share, width), bf16), pltpu.VMEM((n_head, share, width), f32),
        pltpu.VMEM((2, share, width), bf16), pltpu.VMEM((8, share, width), bf16),
        pltpu.VMEM((side, 2, wrows, 2 * dim), f32), pltpu.VMEM((side, 2, wrows, 2 * dim), bf16),
        pltpu.VMEM((2, side, wrows, 2 * dim), bf16),
        dma((8,)),
        dma((1,)), dma((n_head,)), dma((1,)), dma((1,)), dma((1,)), dma((n_head,)), dma((4,)), dma((4,)),
        dma((1,)), dma((n_chip,)), dma((1,)), dma((1,)), dma((2,)), dma((2,)),
        dma((1,)), dma((1,)), dma((1,)), dma((1,)),
        dma((1,)), dma((1,)), dma((1,)), dma((1,)), dma((1,)), dma((8,)),
    ]
    shapes = (
        jax.ShapeDtypeStruct((share, width), f32),
        jax.ShapeDtypeStruct((tok, dim), f32),
        jax.ShapeDtypeStruct((tok, dim), f32),
        jax.ShapeDtypeStruct((tok, 2 * dim), f32),
        jax.ShapeDtypeStruct((2, tok), f32),
        jax.ShapeDtypeStruct((2, tok), f32),
        jax.ShapeDtypeStruct((wrows, 2 * dim), f32),
    )
    results = pl.pallas_call(
        functools.partial(kernel, n_ctx, n_head),
        out_shape=shapes,
        in_specs=[hbm] * 8,
        out_specs=(vmem,) * 7,
        scratch_shapes=scratch,
        compiler_params=pltpu.CompilerParams(collective_id=0, has_side_effects=True,
                                             vmem_limit_bytes=60 * 1024 * 1024),
        name="layer",
    )(doc_offsets, queries, key_vectors, value_rows, write_rate, log_decay, out_weight, grad_out)
    return pl.pallas_call(
        emit,
        out_shape=shapes,
        in_specs=[vmem] * 7,
        out_specs=(hbm,) * 7,
        scratch_shapes=[dma((7,))],
        name="emit",
    )(*results)


def emit(*refs):
    copies = [pltpu.make_async_copy(refs[i], refs[7 + i], refs[14].at[i]) for i in range(7)]
    for copy in copies:
        copy.start()
    for copy in copies:
        copy.wait()


def solution(mesh):
    n_ctx, n_head = mesh.shape["ctx"], mesh.shape["head"]
    return jax.shard_map(
        functools.partial(per_device, n_ctx, n_head),
        mesh=mesh,
        in_specs=(
            P("ctx", "head"), P("ctx", "head"), P("ctx", "head"), P("head", "ctx"), P("head", "ctx"),
            P(), P("head", None), P(("ctx", "head"), None),
        ),
        out_specs=(
            P(("ctx", "head"), None), P("ctx", "head"), P("ctx", "head"), P("ctx", "head"),
            P("head", "ctx"), P("head", "ctx"), P("ctx", "head"),
        ),
        check_vma=False,
    )
```
